32 devices in a mesh: section: 2 (over y), dp: 16 (over z, x, core).
Axes of the slice: x: 2, y: 2, z: 4, core: 2. Of those that a mesh axis runs over, the one named last changes fastest.
Arguments:
- boundary: bfloat16 [2, 16384, 768], P('section', 'dp'), may hold values from -10 to 10
- lengths: int32 [32], P('dp'), may hold values from 128 to 512, as said below
- neighbours: int32 [16384, 40], P('dp'), may hold values from 0 to 511, as said below
- counts: int32 [16384], P('dp'), may hold values from 1 to 40, as said below
- coords: float32 [16384], P('dp'), may hold values from 0 to 16
- square_weights: bfloat16 [2, 4, 768, 768], P('section'), may hold values from -2 to 2
- up_weight: bfloat16 [2, 768, 3072], P('section'), may hold values from -0.21875 to 0.21875
- down_weight: bfloat16 [2, 3072, 768], P('section'), may hold values from -0.109375 to 0.109375
- up_bias: float32 [2, 3072], P('section'), may hold values from -1.5 to 1.5
- norm_gain: float32 [2, 2, 768], P('section'), may hold values from 0.5 to 1.5
- norm_bias: float32 [2, 2, 768], P('section'), may hold values from -0.5 to 0.5
- rich_terms: float32 [2, 12], replicated, may hold values from -1 to 1
Outputs:
- boundary_out: bfloat16 [2, 16384, 768], P('section', 'dp')
- grad_squares: float32 [2, 4, 768, 768], P('section')
- grad_up: float32 [2, 768, 3072], P('section')
- grad_down: float32 [2, 3072, 768], P('section')
- grad_up_bias: float32 [2, 3072], P('section')
- grad_gain: float32 [2, 2, 768], P('section')
- grad_bias: float32 [2, 2, 768], P('section')
- grad_rich: float32 [2, 12], replicated
- rms: float32 [2, 4], replicated
The draws below stay inside these ranges and needn't reach their ends.
Inputs may be any that keep to these rules, and one draw needn't show every extreme that they name: `lengths`: at least a quarter of a slot; some document fills its slot. `neighbours`: positions of the token's own document at most 64 from it; a live token's neighbours are live, a padding token's are padding; slots at or past the count hold 0. `counts`: some token uses all 40 slots.
All inputs are finite; a program needn't handle non-finite values.
Results may differ from the reference program's by a relative error of at most 0.013.
Values may be sent and summed in bfloat16 or wider, within the bound.
No kernel may reach another device: no remote copies, remote signals or barrier semaphores. Data moves between devices by JAX's collectives and lax.ppermute only.
A program may use at most 448 MiB of HBM per device.

```python
import math
import jax
import jax.numpy as jnp
from jax import lax

D = 768
HEADS = 12
HEAD_DIM = 64
FF = 3072
RADIUS = 128
MAXDEG = 40
REACH = 64
BLOCK = 512
TOK_MB = 512
DOCS = 32
TOKENS = 16384


def doc_lengths(key):
    base = jax.random.randint(jax.random.fold_in(key, 101), (DOCS,), TOK_MB // 4, TOK_MB + 1)
    chosen = jax.random.randint(jax.random.fold_in(key, 102), (), 0, DOCS)
    return jnp.where(jnp.arange(DOCS) == chosen, TOK_MB, base).astype(jnp.int32)


def degree_counts(key):
    base = jax.random.randint(jax.random.fold_in(key, 103), (TOKENS,), 1, MAXDEG + 1)
    chosen = jax.random.randint(jax.random.fold_in(key, 104), (), 0, TOKENS)
    return jnp.where(jnp.arange(TOKENS) == chosen, MAXDEG, base).astype(jnp.int32)


def draw_lengths(key, part):
    return doc_lengths(key)


def draw_counts(key, part):
    return degree_counts(key)


def draw_neighbours(key, part):
    own_length = jnp.repeat(doc_lengths(key), TOK_MB, total_repeat_length=TOKENS)
    position = jnp.arange(TOKENS) % TOK_MB
    offsets = jax.random.randint(jax.random.fold_in(key, 105), (TOKENS, MAXDEG), -REACH, REACH + 1)
    target = position[:, None] + offsets
    living = position < own_length
    lowest = jnp.where(living, 0, own_length)
    highest = jnp.where(living, own_length - 1, TOK_MB - 1)
    target = jnp.clip(target, lowest[:, None], highest[:, None])
    slot_ids = jnp.arange(MAXDEG)
    used = slot_ids[None, :] < degree_counts(key)[:, None]
    return jnp.where(used, target, 0).astype(jnp.int32)


def draw_boundary(key, part):
    shape = (TOKENS, D)
    document = (jnp.arange(TOKENS) // TOK_MB).astype(jnp.float32)
    rising = 0.6 * (1.0 + 2.0 * document / max(DOCS - 1, 1))
    first_base = jax.random.truncated_normal(jax.random.fold_in(key, 111), -4.0, 4.0, shape, jnp.float32)
    second_base = jax.random.truncated_normal(jax.random.fold_in(key, 112), -4.0, 4.0, shape, jnp.float32)
    first_rows = jax.random.uniform(jax.random.fold_in(key, 113), (TOKENS, 1), jnp.float32, 0.7, 1.3)
    second_rows = jax.random.uniform(jax.random.fold_in(key, 114), (TOKENS, 1), jnp.float32, 0.7, 1.3)
    inputs = first_base * first_rows * rising[:, None]
    cotangent = second_base * second_rows
    return jnp.stack([inputs, cotangent]).astype(jnp.bfloat16)


def draw_square_weights(key, part):
    base = jax.random.truncated_normal(jax.random.fold_in(key, 121), -2.5, 2.5, (2, 4, D, D), jnp.float32) / math.sqrt(D)
    factors = jnp.array([[1.0, 4.0, 4.0, 1.0], [1.0, 1.0, 1.0, 6.0]], jnp.float32)
    return (base * factors[:, :, None, None]).astype(jnp.bfloat16)


def steps_of(stream_key, dims, pieces, smallest, top_value):
    level, own = 1.0, jax.random.fold_in(stream_key, 6)
    for axis_at, parts in pieces:
        heights = jnp.exp(jax.random.uniform(jax.random.fold_in(own, axis_at), (parts,), jnp.float32, smallest / len(pieces), top_value / len(pieces)))
        level = level * jnp.repeat(heights, dims[axis_at] // parts).reshape([-1 if axis == axis_at else 1 for axis in range(len(dims))])
    return level


def noise(rng, dims, scale, most, split=(), held_as=jnp.bfloat16):
    gain = steps_of(rng, dims, split, -0.22, 0.18) if split else 1.0
    drawn = jax.random.normal(rng, dims, jnp.float32) * scale * gain
    return jnp.minimum(jnp.maximum(drawn, -most), most).astype(held_as)


def setup_inputs(seed: int = 0) -> dict:
    seeds = jax.random.split(jax.random.key(seed), 13)
    return {
        "boundary": draw_boundary(jax.random.fold_in(seeds[12], 71), 0),
        "lengths": draw_lengths(jax.random.fold_in(seeds[12], 71), 0),
        "neighbours": draw_neighbours(jax.random.fold_in(seeds[12], 71), 0),
        "counts": draw_counts(jax.random.fold_in(seeds[12], 71), 0),
        "coords": jnp.clip(16.0 * jax.random.uniform(seeds[4], (TOKENS,), jnp.float32) ** steps_of(seeds[4], (TOKENS,), ((0, 16),), -0.2, 0.2), 0.0, 16.0),
        "square_weights": draw_square_weights(jax.random.fold_in(seeds[12], 71), 0),
        "up_weight": noise(seeds[6], (2, D, FF), D ** -0.5, 0.21875, ((0, 2),)),
        "down_weight": noise(seeds[7], (2, FF, D), FF ** -0.5, 0.109375, ((0, 2),)),
        "up_bias": noise(seeds[8], (2, FF), 0.3, 1.5, ((0, 2),), jnp.float32),
        "norm_gain": jnp.clip(1.0 + 0.1 * jax.random.normal(seeds[9], (2, 2, D), jnp.float32), 0.5, 1.5),
        "norm_bias": noise(seeds[10], (2, 2, D), 0.1, 0.5, ((0, 2),), jnp.float32),
        "rich_terms": jnp.clip(jax.random.uniform(seeds[11], (2, HEADS), jnp.float32, -1.0, 1.0), -1.0, 1.0),
    }


EPSILON = 1e-05
NEG_FILL = -1e+30
HIGHEST = lax.Precision.HIGHEST

@jax.custom_vjp
def low(v):
    return lax.optimization_barrier(v.astype(jnp.bfloat16)).astype(jnp.float32)

@jax.custom_vjp
def low_back(v):
    return v

def low_keep(v):
    return (low(v), None)

def low_pass(kept, grad):
    return (grad,)

def back_keep(v):
    return (v, None)

def back_low(kept, grad):
    return (low(grad),)
low.defvjp(low_keep, low_pass)
low_back.defvjp(back_keep, back_low)

def norm_forward(vector, gain_row, shift_row):
    center = vector - lax.optimization_barrier(jnp.mean(vector, axis=-1, keepdims=True))
    inverse = lax.rsqrt(lax.optimization_barrier(jnp.mean(center * center, axis=-1, keepdims=True)) + EPSILON)
    return center * inverse * gain_row + shift_row

def dense_product(left, right):
    return jnp.dot(left, right, precision=HIGHEST, preferred_element_type=jnp.float32)

def band_terms(row_start, block_rows, radius, total_rows, length, coords_pad, rich_terms):
    query_pos = row_start + jnp.arange(block_rows, dtype=jnp.int32)
    key_pos = row_start - radius + jnp.arange(block_rows + 2 * radius, dtype=jnp.int32)
    nearby = jnp.abs(query_pos[:, None] - key_pos[None, :]) <= radius
    inside = (key_pos >= 0) & (key_pos < total_rows)
    living = (key_pos < length)[None, :] | (key_pos[None, :] == query_pos[:, None])
    allowed = nearby & inside[None, :] & living
    query_coord = lax.dynamic_slice_in_dim(coords_pad, row_start + radius, block_rows, 0)
    key_coord = lax.dynamic_slice_in_dim(coords_pad, row_start, block_rows + 2 * radius, 0)
    offset = query_coord[:, None] - key_coord[None, :]
    spread = jnp.log1p(jnp.abs(offset))
    order_term = jnp.tanh(-offset)
    rich_bias = rich_terms[0][:, None, None] * spread[None] + rich_terms[1][:, None, None] * order_term[None]
    return (allowed, spread, order_term, rich_bias)

def feed_forward(resid, gain_row, shift_row, up_weight, up_bias, down_weight):
    normed = low(norm_forward(resid, gain_row, shift_row))
    pre_act = low_back(dense_product(normed, up_weight) + up_bias)
    return low_back(dense_product(low(jax.nn.gelu(pre_act)), down_weight))

def graph_block(inputs, neighbours, counts, squares, gain_row, shift_row):
    normed = low(norm_forward(inputs, gain_row, shift_row))
    slot_ids = jnp.arange(neighbours.shape[1], dtype=jnp.int32)
    slot_used = (slot_ids[None, :] < counts[:, None]).astype(jnp.float32)
    gathered = jnp.take(normed, neighbours, axis=0)
    neighbour_sum = low_back(lax.optimization_barrier(jnp.sum(gathered * slot_used[:, :, None], axis=1)))
    mean_near = low(neighbour_sum / counts.astype(jnp.float32)[:, None])
    pre_sum = low_back(dense_product(normed, squares[0]) + dense_product(mean_near, squares[1]))
    gate_pre = low_back(dense_product(mean_near, squares[2]))
    mixed = low(pre_sum * jax.nn.sigmoid(gate_pre))
    return low_back(dense_product(mixed, squares[3]))

def attention_block(inputs, length, coords, squares, gain_row, shift_row, rich_terms):
    total_rows = inputs.shape[0]
    normed = low(norm_forward(inputs, gain_row, shift_row))

    def project(which):
        return low(low_back(dense_product(normed, squares[which]))).reshape(total_rows, HEADS, HEAD_DIM)
    queries = project(0)
    key_rows = project(1)
    value_rows = project(2)
    margin = ((RADIUS, RADIUS), (0, 0), (0, 0))
    key_pad = jnp.pad(key_rows, margin)
    value_pad = jnp.pad(value_rows, margin)
    coords_pad = jnp.pad(coords, (RADIUS, RADIUS))
    score_scale = HEAD_DIM ** (-0.5)

    def one_block(row_start):
        allowed, spread, order_term, rich_bias = band_terms(row_start, BLOCK, RADIUS, total_rows, length, coords_pad, rich_terms)
        query_block = lax.dynamic_slice_in_dim(queries, row_start, BLOCK, 0)
        key_block = lax.dynamic_slice_in_dim(key_pad, row_start, BLOCK + 2 * RADIUS, 0)
        value_block = lax.dynamic_slice_in_dim(value_pad, row_start, BLOCK + 2 * RADIUS, 0)
        raw_scores = low_back(jnp.einsum('qhd,khd->hqk', query_block, key_block, precision=HIGHEST))
        scores = jnp.where(allowed[None], raw_scores * score_scale + rich_bias, NEG_FILL)
        highest = lax.optimization_barrier(jnp.max(scores, axis=-1, keepdims=True))
        weights = jnp.exp(scores - highest)
        probs = weights / lax.optimization_barrier(jnp.sum(weights, axis=-1, keepdims=True))
        context = jnp.einsum('hqk,khd->qhd', low(probs), value_block, precision=HIGHEST)
        return context.reshape(BLOCK, HEADS * HEAD_DIM)
    starts = (jnp.arange(total_rows // BLOCK) * BLOCK).astype(jnp.int32)
    context = lax.map(jax.checkpoint(one_block), starts).reshape(total_rows, HEADS * HEAD_DIM)
    context = low(low_back(context))
    return low_back(dense_product(context, squares[3]))

def document_forward(inputs, parameters, length, neighbours, counts, coords):
    squares, up_weight, down_weight, up_bias, norm_gain, norm_bias, rich_terms = parameters
    live_rows = (jnp.arange(inputs.shape[0], dtype=jnp.int32) < length).astype(jnp.float32)[:, None]

    def energy(vector):
        return jnp.sum(live_rows * vector * vector)
    branch_one = graph_block(inputs, neighbours, counts, squares[0], norm_gain[0, 0], norm_bias[0, 0])
    resid_one = inputs + branch_one
    branch_two = feed_forward(resid_one, norm_gain[0, 1], norm_bias[0, 1], up_weight[0], up_bias[0], down_weight[0])
    resid_two = resid_one + branch_two
    middle = low(low_back(resid_two))
    branch_three = attention_block(middle, length, coords, squares[1], norm_gain[1, 0], norm_bias[1, 0], rich_terms)
    resid_three = middle + branch_three
    branch_four = feed_forward(resid_three, norm_gain[1, 1], norm_bias[1, 1], up_weight[1], up_bias[1], down_weight[1])
    resid_four = resid_three + branch_four
    sums = jnp.stack([energy(item) for item in (branch_one, resid_one, branch_two, resid_two, branch_three, resid_three, branch_four, resid_four)])
    return (resid_four, sums)

def reference(boundary, lengths, neighbours, counts, coords, square_weights, up_weight, down_weight, up_bias, norm_gain, norm_bias, rich_terms):
    parameters = (square_weights.astype(jnp.float32), up_weight.astype(jnp.float32), down_weight.astype(jnp.float32), up_bias, norm_gain, norm_bias, rich_terms)
    documents = lengths.shape[0]
    inputs = boundary[0].reshape(documents, TOK_MB, D)
    cotangent = boundary[1].reshape(documents, TOK_MB, D)
    items = (inputs, cotangent, lengths, neighbours.reshape(documents, TOK_MB, MAXDEG), counts.reshape(documents, TOK_MB), coords.reshape(documents, TOK_MB))

    def document_step(carry, document):
        gradients, sums = carry
        doc_inputs, doc_cotangent, length, doc_near, doc_counts, doc_coords = document

        def forward(vector, weights):
            return document_forward(vector, weights, length, doc_near, doc_counts, doc_coords)
        output, pullback, doc_sums = jax.vjp(forward, doc_inputs.astype(jnp.float32), parameters, has_aux=True)
        grad_inputs, grad_parameters = pullback(doc_cotangent.astype(jnp.float32))
        gradients = jax.tree.map(jnp.add, gradients, grad_parameters)
        return ((gradients, sums + doc_sums), (grad_inputs.astype(jnp.bfloat16), output.astype(jnp.bfloat16)))
    start_gradients = jax.tree.map(jnp.zeros_like, parameters)
    (gradients, sums), (grad_inputs, outputs) = lax.scan(document_step, (start_gradients, jnp.zeros((8,), jnp.float32)), items)
    live_count = jnp.sum(lengths).astype(jnp.float32)
    rms = jnp.sqrt(sums.reshape(2, 4) / (live_count * D))
    boundary_out = jnp.stack([grad_inputs.reshape(-1, D), outputs.reshape(-1, D)])
    return (boundary_out, gradients[0], gradients[1], gradients[2], gradients[3], gradients[4], gradients[5], gradients[6], rms)
```

```python
import jax
import jax.numpy as jnp
from jax import lax
from jax.sharding import Mesh, PartitionSpec as P

RADIUS = 128
EPSILON = 1e-05
NEG_FILL = -1e30
GELU_C = 0.7978845608028654


def passed_along(block, axis, distance):
    devices = range(lax.axis_size(axis))
    route = [(i - distance, i) for i in devices if i - distance in devices]
    return lax.ppermute(block, axis, route)


def low(vector):
    return vector.astype(jnp.bfloat16)


def product(left, right):
    return jnp.dot(left, right, preferred_element_type=jnp.float32)


def product_left(left, right):
    return lax.dot_general(
        left, right, (((0,), (0,)), ((), ())), preferred_element_type=jnp.float32
    )


def product_right(left, right):
    return lax.dot_general(
        left, right, (((1,), (1,)), ((), ())), preferred_element_type=jnp.float32
    )


def norm_forward(vector, gain_row, shift_row):
    center = vector - jnp.mean(vector, axis=-1, keepdims=True)
    inverse = lax.rsqrt(jnp.mean(center * center, axis=-1, keepdims=True) + EPSILON)
    return center * inverse * gain_row + shift_row


def norm_backward(vector, gain_row, grad_normed):
    center = vector - jnp.mean(vector, axis=-1, keepdims=True)
    inverse = lax.rsqrt(jnp.mean(center * center, axis=-1, keepdims=True) + EPSILON)
    normed = center * inverse
    scaled = grad_normed * gain_row
    mean_scaled = jnp.mean(scaled, axis=-1, keepdims=True)
    mean_mixed = jnp.mean(scaled * normed, axis=-1, keepdims=True)
    grad_input = inverse * (scaled - mean_scaled - normed * mean_mixed)
    return grad_input, jnp.sum(grad_normed * normed, axis=0), jnp.sum(grad_normed, axis=0)


def mlp_forward(resid, gain_row, shift_row, up_matrix, bias_row, down_matrix):
    normed_low = low(norm_forward(resid, gain_row, shift_row))
    pre_act = product(normed_low, up_matrix) + bias_row
    curve = jnp.tanh(GELU_C * (pre_act + 0.044715 * pre_act * pre_act * pre_act))
    active_low = low(0.5 * pre_act * (1.0 + curve))
    slope = 0.5 * (1.0 + curve) + 0.5 * pre_act * (1.0 - curve * curve) * GELU_C * (
        1.0 + 3.0 * 0.044715 * pre_act * pre_act
    )
    branch = product(active_low, down_matrix)
    return branch, (resid, normed_low, active_low, low(slope))


def mlp_backward(kept, grad_low, grad_resid, gain_row, up_matrix, down_matrix):
    resid, normed_low, active_low, slope = kept
    grad_active = product_right(grad_low, down_matrix)
    grad_pre = low(slope.astype(jnp.float32) * grad_active)
    grad_bias = jnp.sum(grad_pre.astype(jnp.float32), axis=0)
    grad_normed = product_right(grad_pre, up_matrix)
    grad_input, grad_gain, grad_shift = norm_backward(resid, gain_row, grad_normed)
    return grad_resid + grad_input, grad_pre, grad_bias, grad_gain, grad_shift


def adjacency_rows(neighbours, counts, total_rows):
    slot_ids = jnp.arange(neighbours.shape[1])
    index_rows = jnp.where(slot_ids[None, :] < counts[:, None], neighbours, -1)
    columns = jnp.arange(total_rows)
    matches = index_rows[:, :, None] == columns[None, None, :]
    return jnp.sum(matches, axis=1, dtype=jnp.int32).astype(jnp.bfloat16)


def graph_forward(inputs, neighbours, counts, squares, gain_row, shift_row):
    normed_low = low(norm_forward(inputs, gain_row, shift_row))
    adjacency = adjacency_rows(neighbours, counts, inputs.shape[0])
    divisor = counts.astype(jnp.float32)[:, None]
    near = low(product(adjacency, normed_low) / divisor)
    pre = product(normed_low, squares[0]) + product(near, squares[1])
    sigma = jax.nn.sigmoid(product(near, squares[2]))
    mixed = low(pre * sigma)
    branch = product(mixed, squares[3])
    return branch, (inputs, normed_low, adjacency, divisor, near, pre, sigma, mixed)


def graph_backward(kept, grad_resid, squares, gain_row):
    inputs, normed_low, adjacency, divisor, near, pre, sigma, mixed = kept
    grad_low = low(grad_resid)
    grad_mixed = product_right(grad_low, squares[3])
    grad_pre = low(sigma * grad_mixed)
    grad_gate = low(pre * sigma * (1.0 - sigma) * grad_mixed)
    grad_mean = product_right(grad_pre, squares[1]) + product_right(grad_gate, squares[2])
    grad_total = low(grad_mean / divisor)
    grad_normed = product_right(grad_pre, squares[0]) + product_left(adjacency, grad_total)
    grad_input, grad_gain, grad_shift = norm_backward(inputs, gain_row, grad_normed)
    lefts = (normed_low, near, near, mixed)
    rights = (grad_pre, grad_pre, grad_gate, grad_low)
    return grad_resid + grad_input, lefts, rights, grad_gain, grad_shift


def attention_terms(length, coords, rich_terms):
    rows = coords.shape[0]
    position = jnp.arange(rows)
    nearby = jnp.abs(position[:, None] - position[None, :]) <= RADIUS
    living = (position < length)[None, :] | (position[None, :] == position[:, None])
    offset = coords[:, None] - coords[None, :]
    return nearby & living, jnp.log1p(jnp.abs(offset)), jnp.tanh(-offset)


def attention_forward(inputs, terms, squares, gain_row, shift_row, rich_terms):
    rows, width = inputs.shape
    heads = rich_terms.shape[1]
    allowed, spread, order = terms
    scale = (width // heads) ** (-0.5)
    normed_low = low(norm_forward(inputs, gain_row, shift_row))
    queries, keys, values = (
        low(product(normed_low, squares[c])).reshape(rows, heads, -1) for c in range(3)
    )
    raw = jnp.einsum("qhd,khd->hqk", queries, keys, preferred_element_type=jnp.float32)
    bias = rich_terms[0][:, None, None] * spread + rich_terms[1][:, None, None] * order
    scores = jnp.where(allowed[None], raw * scale + bias, NEG_FILL)
    weights = jnp.exp(scores - jnp.max(scores, axis=-1, keepdims=True))
    probs = weights / jnp.sum(weights, axis=-1, keepdims=True)
    context = jnp.einsum("hqk,khd->qhd", low(probs), values, preferred_element_type=jnp.float32)
    context = low(context.reshape(rows, width))
    branch = product(context, squares[3])
    return branch, (inputs, normed_low, queries, keys, values, probs, context)


def attention_backward(kept, terms, grad_resid, squares, gain_row, rich_terms):
    inputs, normed_low, queries, keys, values, probs, context = kept
    rows, width = inputs.shape
    heads = rich_terms.shape[1]
    allowed, spread, order = terms
    scale = (width // heads) ** (-0.5)
    grad_low = low(grad_resid)
    grad_context = low(product_right(grad_low, squares[3])).reshape(rows, heads, -1)
    grad_probs = jnp.einsum("qhd,khd->hqk", grad_context, values, preferred_element_type=jnp.float32)
    inner = jnp.sum(probs * grad_probs, axis=-1, keepdims=True)
    grad_scores = probs * (grad_probs - inner)
    grad_rich = jnp.stack(
        [
            jnp.sum(grad_scores * spread[None], axis=(1, 2)),
            jnp.sum(grad_scores * order[None], axis=(1, 2)),
        ]
    )
    grad_raw = low(grad_scores * scale)
    grad_q = jnp.einsum("hqk,khd->qhd", grad_raw, keys, preferred_element_type=jnp.float32)
    grad_k = jnp.einsum("hqk,qhd->khd", grad_raw, queries, preferred_element_type=jnp.float32)
    grad_v = jnp.einsum("hqk,qhd->khd", low(probs), grad_context, preferred_element_type=jnp.float32)
    grad_q, grad_k, grad_v = (low(item).reshape(rows, width) for item in (grad_q, grad_k, grad_v))
    grad_normed = (
        product_right(grad_q, squares[0])
        + product_right(grad_k, squares[1])
        + product_right(grad_v, squares[2])
    )
    grad_input, grad_gain, grad_shift = norm_backward(inputs, gain_row, grad_normed)
    lefts = (normed_low, normed_low, normed_low, context)
    rights = (grad_q, grad_k, grad_v, grad_low)
    return grad_resid + grad_input, lefts, rights, grad_gain, grad_shift, grad_rich


def live_squares(length, quantities):
    live_rows = (jnp.arange(quantities[0].shape[0]) < length).astype(jnp.float32)[:, None]
    return jnp.stack([jnp.sum(live_rows * item * item) for item in quantities])


def exchanged_sum(block, axis):
    size = lax.axis_size(axis)
    step = 1
    while step < size:
        route = [(i, i ^ step) for i in range(size)]
        block = block + lax.ppermute(block, axis, route)
        step *= 2
    return block


def summed_over_documents(block):
    core = lax.axis_index("core")
    swap = [(0, 1), (1, 0)]
    half = block.shape[0] // 2
    own = lax.dynamic_slice_in_dim(block, core * half, half, 0)
    other = lax.dynamic_slice_in_dim(block, (1 - core) * half, half, 0)
    part = own + lax.ppermute(other, "core", swap)
    part = lax.psum(part, "chip")
    other = lax.ppermute(part, "core", swap)
    return jnp.concatenate(
        [jnp.where(core == 0, part, other), jnp.where(core == 0, other, part)], axis=0
    )


def local(
    boundary,
    lengths,
    neighbours,
    counts,
    coords,
    square_weights,
    up_weight,
    down_weight,
    up_bias,
    norm_gain,
    norm_bias,
    rich_terms,
):
    first = lax.axis_index("section") == 0
    documents = lengths.shape[0]
    rows = boundary.shape[1] // documents
    width = boundary.shape[2]
    hidden = up_weight.shape[2]
    squares = square_weights[0]
    up, down, bias = up_weight[0], down_weight[0], up_bias[0]
    gains, shifts = norm_gain[0], norm_bias[0]

    def rows_of(array, doc):
        return lax.slice_in_dim(array, doc * rows, (doc + 1) * rows)

    inputs = [rows_of(boundary[0], doc) for doc in range(documents)]

    def layer_one_forward(doc, source):
        x = source.astype(jnp.float32)
        branch_a, graph_kept = graph_forward(
            x, rows_of(neighbours, doc), rows_of(counts, doc), squares, gains[0], shifts[0]
        )
        resid_a = x + branch_a
        branch_f, mlp_kept = mlp_forward(resid_a, gains[1], shifts[1], up, bias, down)
        resid_b = resid_a + branch_f
        stats = live_squares(lengths[doc], (branch_a, resid_a, branch_f, resid_b))
        return low(resid_b), graph_kept, mlp_kept, stats

    def layer_two(doc, mid, cotangent):
        x = mid.astype(jnp.float32)
        terms = attention_terms(lengths[doc], rows_of(coords, doc), rich_terms)
        branch_c, attend_kept = attention_forward(x, terms, squares, gains[0], shifts[0], rich_terms)
        resid_c = x + branch_c
        branch_f, mlp_kept = mlp_forward(resid_c, gains[1], shifts[1], up, bias, down)
        resid_d = resid_c + branch_f
        stats = live_squares(lengths[doc], (branch_c, resid_c, branch_f, resid_d))
        grad_c, grad_pre, grad_bias, gain_f, shift_f = mlp_backward(
            mlp_kept, cotangent, cotangent.astype(jnp.float32), gains[1], up, down
        )
        grad_b, lefts, rights, gain_c, shift_c, grad_rich = attention_backward(
            attend_kept, terms, grad_c, squares, gains[0], rich_terms
        )
        small = jnp.concatenate([grad_bias, gain_c, gain_f, shift_c, shift_f])
        operands = (mlp_kept[2], mlp_kept[1], grad_pre, lefts, rights)
        return low(grad_b), low(resid_d), operands, small, stats, grad_rich

    def layer_one_backward(graph_kept, mlp_kept, grad_mid):
        grad_a, grad_pre, grad_bias, gain_f, shift_f = mlp_backward(
            mlp_kept, grad_mid, grad_mid.astype(jnp.float32), gains[1], up, down
        )
        grad_x, lefts, rights, gain_a, shift_a = graph_backward(graph_kept, grad_a, squares, gains[0])
        small = jnp.concatenate([grad_bias, gain_a, gain_f, shift_a, shift_f])
        operands = (mlp_kept[2], mlp_kept[1], grad_pre, lefts, rights)
        return low(grad_x), operands, small

    kept_one, arrived, stats_one = [], [], 0.0
    for doc in range(documents):
        source = inputs[doc]
        if doc:
            source, _ = lax.optimization_barrier((source, sent))
        sent, graph_kept, mlp_kept, stats = layer_one_forward(doc, source)
        kept_one.append((graph_kept, mlp_kept))
        stats_one = stats_one + stats
        arrived.append(passed_along(sent, "section", 1))

    back, out_two, small_two, stats_two, rich_two, operands_two = [], [], 0.0, 0.0, 0.0, []
    for doc in range(documents):
        grad_mid, result, operands, small, stats, rich = layer_two(doc, arrived[doc], inputs[doc])
        operands_two.append(operands)
        out_two.append(result)
        small_two, stats_two, rich_two = small_two + small, stats_two + stats, rich_two + rich
        back.append(passed_along(grad_mid, "section", -1))
        last_sent = grad_mid

    small_one, out_one, operands_one = 0.0, [], []
    for doc in range(documents):
        grad_mid = back[doc]
        if doc < documents - 1:
            grad_mid, _ = lax.optimization_barrier((grad_mid, last_sent))
        result, operands, small = layer_one_backward(*kept_one[doc], grad_mid)
        out_one.append(result)
        small_one = small_one + small
        operands_one.append(operands)

    def both(pick_one, pick_two):
        one = jnp.concatenate([pick_one(doc) for doc in range(documents)], axis=0)
        two = jnp.concatenate([pick_two(doc) for doc in range(documents)], axis=0)
        return jnp.where(first, one, two)

    def side(index):
        return both(lambda d: operands_one[d][index], lambda d: operands_two[d][index])

    grad_down = low(product_left(side(0), both(lambda d: back[d], lambda d: inputs[d])))
    grad_up = low(product_left(side(1), side(2)))
    grad_squares = jnp.concatenate(
        [
            low(
                product_left(
                    both(lambda d: operands_one[d][3][c], lambda d: operands_two[d][3][c]),
                    both(lambda d: operands_one[d][4][c], lambda d: operands_two[d][4][c]),
                )
            )
            for c in range(4)
        ],
        axis=0,
    )
    down_total = summed_over_documents(grad_down).astype(jnp.float32)
    up_total = summed_over_documents(grad_up).astype(jnp.float32)
    square_total = summed_over_documents(grad_squares).astype(jnp.float32)

    heads = rich_terms.shape[1]
    small = jnp.where(first, small_one, small_two)
    count = jnp.sum(lengths).astype(jnp.float32)[None]
    shared = jnp.concatenate(
        [
            jnp.where(first, stats_one, 0.0),
            jnp.where(first, 0.0, stats_two),
            jnp.where(first, 0.0, rich_two).reshape(-1),
            jnp.where(first, 0.0, count),
        ]
    )
    packed = jnp.concatenate([small, shared])
    packed = jnp.pad(packed, (0, -packed.shape[0] % 1024))
    packed = exchanged_sum(exchanged_sum(packed, "core"), "chip")
    crossed = lax.ppermute(packed, "section", [(0, 1), (1, 0)])
    start = small.shape[0]
    shared = packed[start : start + shared.shape[0]] + crossed[start : start + shared.shape[0]]
    rms = jnp.sqrt(shared[:8].reshape(2, 4) / (shared[8 + 2 * heads] * width))
    rich_total = shared[8 : 8 + 2 * heads].reshape(2, heads)
    boundary_out = jnp.concatenate(
        [jnp.where(first, out_one[doc], out_two[doc]) for doc in range(documents)], axis=0
    )[None]
    return (
        boundary_out,
        square_total.reshape(1, 4, width, width),
        up_total[None],
        down_total[None],
        packed[:hidden][None],
        packed[hidden : hidden + 2 * width].reshape(1, 2, width),
        packed[hidden + 2 * width : hidden + 4 * width].reshape(1, 2, width),
        rich_total,
        rms,
    )


def solution(mesh):
    sections, dp = mesh.devices.shape
    split = Mesh(mesh.devices.reshape(sections, dp // 2, 2), ("section", "chip", "core"))
    data = ("chip", "core")
    in_specs = (
        P("section", data, None),
        P(data),
        P(data, None),
        P(data),
        P(data),
        P("section", None, None, None),
        P("section", None, None),
        P("section", None, None),
        P("section", None),
        P("section", None, None),
        P("section", None, None),
        P(),
    )
    out_specs = (
        P("section", data, None),
        P("section", None, None, None),
        P("section", None, None),
        P("section", None, None),
        P("section", None),
        P("section", None, None),
        P("section", None, None),
        P(),
        P(),
    )
    return jax.shard_map(local, mesh=split, in_specs=in_specs, out_specs=out_specs, check_vma=False)
```

```python
import functools
import jax
import jax.numpy as jnp
from jax import lax
from jax.sharding import Mesh, PartitionSpec as P
from jax.experimental import pallas as pl
from jax.experimental.pallas import tpu as pltpu

RADIUS = 128
REACH = 64
QUERY_BLOCK = 128
EPSILON = 1e-05
NEG_FILL = -1e30
GELU_C = 0.7978845608028654
F32, BF16 = jnp.float32, jnp.bfloat16
MIB = 1024 * 1024


def low(vector):
    return vector.astype(BF16)


def dot_nn(left, right):
    return jnp.dot(left, right, preferred_element_type=F32)


def dot_nt(left, right):
    return lax.dot_general(left, right, (((1,), (1,)), ((), ())), preferred_element_type=F32)


def dot_tn(left, right):
    return lax.dot_general(left, right, (((0,), (0,)), ((), ())), preferred_element_type=F32)


def normalized(vector):
    center = vector - jnp.mean(vector, axis=-1, keepdims=True)
    inverse = lax.rsqrt(jnp.mean(center * center, axis=-1, keepdims=True) + EPSILON)
    return center * inverse, inverse


def norm_backward(vector, gain_row, grad_normed):
    normed, inverse = normalized(vector)
    scaled = grad_normed * gain_row
    mean_scaled = jnp.mean(scaled, axis=-1, keepdims=True)
    mean_mixed = jnp.mean(scaled * normed, axis=-1, keepdims=True)
    grad_input = inverse * (scaled - mean_scaled - normed * mean_mixed)
    grad_gain = jnp.sum(grad_normed * normed, axis=0, keepdims=True)
    return grad_input, grad_gain, jnp.sum(grad_normed, axis=0, keepdims=True)


def live_sums(length, start, items):
    rows = items[0].shape[0]
    live = start + lax.broadcasted_iota(jnp.int32, (rows, 1), 0) < length
    return [jnp.sum(jnp.where(live, v * v, 0.0), axis=0, keepdims=True) for v in items]


def whole(shape):
    return pl.BlockSpec(shape, lambda *_: (0,) * len(shape))


def part_of(shape, doc, axis):
    place = tuple(doc if d == axis else 0 for d in range(len(shape)))
    return pl.BlockSpec(shape, lambda *_: place)


def column(row):
    return jnp.broadcast_to(row, (row.shape[1], row.shape[1])).T[:, 0:1]


def kernel_call(body, grid, in_specs, outs, scratch, limit, flops, moved, name, transcendentals=0):
    return pl.pallas_call(
        body,
        out_shape=[jax.ShapeDtypeStruct(shape, kind) for shape, kind, _ in outs],
        grid_spec=pltpu.PrefetchScalarGridSpec(
            num_scalar_prefetch=1,
            grid=grid,
            in_specs=in_specs,
            out_specs=[spec for _, _, spec in outs],
            scratch_shapes=scratch,
        ),
        compiler_params=pltpu.CompilerParams(
            dimension_semantics=("arbitrary",) * len(grid), vmem_limit_bytes=limit * MIB
        ),
        cost_estimate=pl.CostEstimate(
            flops=int(flops), bytes_accessed=int(moved), transcendentals=int(transcendentals)
        ),
        name=name,
    )


def feed_forward_body(
    length_ref, resid_ref, gain_ref, shift_ref, up_ref, bias_ref, down_ref,
    normed_ref, active_ref, slope_ref, out_ref, stat_ref, sum_ref,
):
    step = pl.program_id(0)
    rows = resid_ref.shape[0]

    @pl.when(step == 0)
    def _():
        normed_ref[...] = low(normalized(resid_ref[...])[0] * gain_ref[1:2, :] + shift_ref[1:2, :])
        sum_ref[...] = jnp.zeros_like(sum_ref)

    parts = 2
    for part in range(parts):
        own = pl.ds(part * (rows // parts), rows // parts)
        pre = dot_nn(normed_ref[own, :], up_ref[...]) + bias_ref[...]
        square = pre * pre
        curve = jnp.tanh(pre * (GELU_C + GELU_C * 0.044715 * square))
        half = 0.5 + 0.5 * curve
        active = low(pre * half)
        active_ref[own, :] = active
        rise = pre * (GELU_C + 3.0 * GELU_C * 0.044715 * square)
        slope_ref[own, :] = low(half + rise * (half - half * half) * 2.0)
        sum_ref[own, :] += dot_nn(active, down_ref[...])

    @pl.when(step == pl.num_programs(0) - 1)
    def _():
        branch = sum_ref[...]
        result = resid_ref[...] + branch
        out_ref[...] = low(result)
        first, second = live_sums(length_ref[0], 0, (branch, result))
        stat_ref[0:1, :] = first
        stat_ref[1:2, :] = second


def feed_forward(length, resid, gain, shift, up, bias, down, tile=1024):
    rows, width = resid.shape
    hidden = up.shape[1]
    over = lambda j, *_: (0, j)
    return kernel_call(
        feed_forward_body,
        (hidden // tile,),
        [
            whole((rows, width)), whole((2, width)), whole((2, width)),
            pl.BlockSpec((width, tile), over), pl.BlockSpec((1, tile), over),
            pl.BlockSpec((tile, width), lambda j, *_: (j, 0)),
        ],
        [
            ((rows, width), BF16, whole((rows, width))),
            ((rows, hidden), BF16, pl.BlockSpec((rows, tile), over)),
            ((rows, hidden), BF16, pl.BlockSpec((rows, tile), over)),
            ((rows, width), BF16, whole((rows, width))),
            ((2, width), F32, whole((2, width))),
        ],
        [pltpu.VMEM((rows, width), F32)],
        32,
        4 * rows * width * hidden,
        4 * (rows * hidden + width * hidden) + 8 * rows * width,
        "feed_forward",
        rows * hidden,
    )(length, resid, gain, shift, up, bias, down)


def feed_backward_body(
    length_ref, grad_ref, resid_ref, gain_ref, slope_ref, up_ref, down_ref,
    pre_ref, bias_ref, out_ref, gain_out, shift_out, sum_ref,
):
    step = pl.program_id(0)
    rows = resid_ref.shape[0]

    @pl.when(step == 0)
    def _():
        sum_ref[...] = jnp.zeros_like(sum_ref)

    parts = 2
    total = None
    for part in range(parts):
        own = pl.ds(part * (rows // parts), rows // parts)
        grad_active = dot_nt(grad_ref[own, :], down_ref[...])
        grad_pre = low(slope_ref[own, :].astype(F32) * grad_active)
        pre_ref[own, :] = grad_pre
        here = jnp.sum(grad_pre.astype(F32), axis=0, keepdims=True)
        total = here if total is None else total + here
        sum_ref[own, :] += dot_nt(grad_pre, up_ref[...])

    bias_ref[...] = total

    @pl.when(step == pl.num_programs(0) - 1)
    def _():
        grad_input, grad_gain, grad_shift = norm_backward(resid_ref[...], gain_ref[1:2, :], sum_ref[...])
        out_ref[...] = grad_ref[...].astype(F32) + grad_input
        gain_out[...] = grad_gain
        shift_out[...] = grad_shift


def feed_backward(length, grad, doc, resid, gain, slope, up, down, tile=1024):
    rows, width = resid.shape
    hidden = up.shape[1]
    over = lambda j, *_: (0, j)
    return kernel_call(
        feed_backward_body,
        (hidden // tile,),
        [
            part_of((rows, width), doc, 0), whole((rows, width)), whole((2, width)),
            pl.BlockSpec((rows, tile), over), pl.BlockSpec((width, tile), over),
            pl.BlockSpec((tile, width), lambda j, *_: (j, 0)),
        ],
        [
            ((rows, hidden), BF16, pl.BlockSpec((rows, tile), over)),
            ((1, hidden), F32, pl.BlockSpec((1, tile), over)),
            ((rows, width), F32, whole((rows, width))),
            ((1, width), F32, whole((1, width))),
            ((1, width), F32, whole((1, width))),
        ],
        [pltpu.VMEM((rows, width), F32)],
        32,
        4 * rows * width * hidden,
        4 * (rows * hidden + width * hidden) + 10 * rows * width,
        "feed_backward",
    )(length, grad, resid, gain, slope, up, down)


def graph_windows(rows):
    span = QUERY_BLOCK + 2 * REACH
    return [
        (start, min(max(start - REACH, 0), rows - span), span)
        for start in range(0, rows, QUERY_BLOCK)
    ]


def graph_forward_body(
    length_ref, x_ref, near_ref_t, counts_ref, gain_ref, shift_ref, w_ref,
    left_ref, link_ref, sigma_ref, pull_ref, resid_ref, stat_ref,
):
    normed_ref, mean_ref, mixed_ref = (left_ref.at[i] for i in range(3))
    rows = x_ref.shape[0]
    normed_ref[...] = low(normalized(x_ref[...].astype(F32))[0] * gain_ref[0:1, :] + shift_ref[0:1, :])
    slots = near_ref_t.shape[0]
    slot = lax.broadcasted_iota(jnp.int32, (slots, QUERY_BLOCK), 0)
    for row, start, span in graph_windows(rows):
        own = pl.ds(row, QUERY_BLOCK)
        counts = counts_ref[:, own]
        index = jnp.where(slot < counts, near_ref_t[:, own], -1)
        place = start + lax.broadcasted_iota(jnp.int32, (span, QUERY_BLOCK), 0)
        links = jnp.zeros((span, QUERY_BLOCK), F32)
        for s in range(slots):
            links += jnp.where(index[s : s + 1, :] == place, 1.0, 0.0)
        link_ref[:, own] = low(links)
        total = dot_nn(low(links.T), normed_ref[pl.ds(start, span), :])
        mean_ref[own, :] = low(total / column(counts.astype(F32)))
    sums = None
    parts = 2
    for part in range(parts):
        own = pl.ds(part * (rows // parts), rows // parts)
        pre = dot_nn(normed_ref[own, :], w_ref[0]) + dot_nn(mean_ref[own, :], w_ref[1])
        sigma = jax.nn.sigmoid(dot_nn(mean_ref[own, :], w_ref[2]))
        mixed = pre * sigma
        sigma_ref[own, :] = low(sigma)
        pull_ref[own, :] = low(mixed - mixed * sigma)
        mixed_ref[own, :] = low(mixed)
        branch = dot_nn(low(mixed), w_ref[3])
        resid = x_ref[own, :].astype(F32) + branch
        resid_ref[own, :] = resid
        here = live_sums(length_ref[0], part * (rows // parts), (branch, resid))
        sums = here if sums is None else [a + b for a, b in zip(sums, here)]
    stat_ref[0:1, :] = sums[0]
    stat_ref[1:2, :] = sums[1]


def graph_forward(length, x, doc, rows, near_t, counts, gain, shift, weights):
    width = x.shape[1]
    slots = near_t.shape[0]
    span = QUERY_BLOCK + 2 * REACH
    full = whole((rows, width))
    return kernel_call(
        graph_forward_body,
        (1,),
        [
            part_of((rows, width), doc, 0), part_of((slots, rows), doc, 1), part_of((1, rows), doc, 1),
            whole((2, width)), whole((2, width)), whole(weights.shape),
        ],
        [
            ((3, rows, width), BF16, whole((3, rows, width))),
            ((span, rows), BF16, whole((span, rows))),
            ((rows, width), BF16, full),
            ((rows, width), BF16, full),
            ((rows, width), F32, full),
            ((2, width), F32, whole((2, width))),
        ],
        [],
        40,
        8 * rows * width * width + 2 * rows * span * width,
        16 * rows * width + 8 * width * width,
        "graph_forward",
    )(length, x, near_t, counts, gain, shift, weights)


def graph_backward_body(
    length_ref, grad_ref, x_ref, gain_ref, sigma_ref, pull_ref, link_ref, counts_ref, w_ref,
    right_ref, out_ref, gain_out, shift_out, mean_ref, sum_ref,
):
    rows = x_ref.shape[0]
    counts_column = column(counts_ref[...].astype(F32))
    parts = 2
    for part in range(parts):
        own = pl.ds(part * (rows // parts), rows // parts)
        grad_low = low(grad_ref[own, :])
        right_ref[2, own, :] = grad_low
        grad_mixed = dot_nt(grad_low, w_ref[3])
        grad_pre = low(sigma_ref[own, :].astype(F32) * grad_mixed)
        grad_gate = low(pull_ref[own, :].astype(F32) * grad_mixed)
        right_ref[0, own, :] = grad_pre
        right_ref[1, own, :] = grad_gate
        sum_ref[own, :] = dot_nt(grad_pre, w_ref[0])
        grad_mean = dot_nt(grad_pre, w_ref[1]) + dot_nt(grad_gate, w_ref[2])
        mean_ref[own, :] = low(grad_mean / counts_column[part * (rows // parts) : (part + 1) * (rows // parts), :])
    for row, start, span in graph_windows(rows):
        own = pl.ds(row, QUERY_BLOCK)
        sum_ref[pl.ds(start, span), :] += dot_nn(link_ref[:, own], mean_ref[own, :])
    grad_input, grad_gain, grad_shift = norm_backward(
        x_ref[...].astype(F32), gain_ref[0:1, :], sum_ref[...]
    )
    out_ref[...] = low(grad_ref[...] + grad_input)
    gain_out[...] = grad_gain
    shift_out[...] = grad_shift


def graph_backward(length, grad, x, doc, gain, sigma, pull, links, counts, weights):
    rows, width = grad.shape
    full = whole((rows, width))
    return kernel_call(
        graph_backward_body,
        (1,),
        [
            full, part_of((rows, width), doc, 0), whole((2, width)), full, full, whole(links.shape),
            part_of((1, rows), doc, 1), whole(weights.shape),
        ],
        [
            ((3, rows, width), BF16, whole((3, rows, width))),
            ((rows, width), BF16, full),
            ((1, width), F32, whole((1, width))),
            ((1, width), F32, whole((1, width))),
        ],
        [pltpu.VMEM((rows, width), BF16), pltpu.VMEM((rows, width), F32)],
        40,
        8 * rows * width * width + 2 * rows * links.shape[0] * width,
        18 * rows * width + 8 * width * width,
        "graph_backward",
    )(length, grad, x, gain, sigma, pull, links, counts, weights)


def attend_windows(rows):
    windows, offset = [], 0
    for row in range(0, rows, QUERY_BLOCK):
        start = max(row - RADIUS, 0)
        span = min(row + QUERY_BLOCK + RADIUS, rows) - start
        windows.append((row, start, span, offset))
        offset += span
    return windows, offset


def two_heads(block, lane):
    zero = jnp.zeros_like(block)
    return jnp.concatenate([jnp.where(lane, block, zero), jnp.where(lane, zero, block)], axis=0)


def attend_forward_body(
    length_ref, mid_ref, coords_ref, rich_ref, gain_ref, shift_ref, w_ref,
    left_ref, query_ref, key_ref, value_ref, probs_ref, terms_ref, resid_ref, stat_ref,
    turned_ref, turned_context, mask_ref,
):
    normed_ref, context_ref = left_ref.at[0], left_ref.at[1]
    rows, width = mid_ref.shape
    heads = rich_ref.shape[1]
    head_width = width // heads
    scale = head_width ** (-0.5)
    length = length_ref[0]
    windows, _ = attend_windows(rows)
    parts = 2
    for part in range(parts):
        own = pl.ds(part * (rows // parts), rows // parts)
        x = mid_ref[own, :].astype(F32)
        normed = low(normalized(x)[0] * gain_ref[0:1, :] + shift_ref[0:1, :])
        normed_ref[own, :] = normed
        query_ref[own, :] = low(dot_nn(normed, w_ref[0]))
        key_ref[own, :] = low(dot_nn(normed, w_ref[1]))
        value = dot_nn(normed, w_ref[2])
        value_ref[own, :] = low(value)
        turned_ref[:, own] = low(value.T)
    for row, start, span, offset in windows:
        i = row + lax.broadcasted_iota(jnp.int32, (span, QUERY_BLOCK), 1)
        j = start + lax.broadcasted_iota(jnp.int32, (span, QUERY_BLOCK), 0)
        allowed = (jnp.abs(i - j) <= RADIUS) & ((j < length) | (i == j))
        mask_ref[pl.ds(offset, span), :] = jnp.where(allowed, 0.0, NEG_FILL)
        across = coords_ref[:, pl.ds(row, QUERY_BLOCK)]
        along = [
            jnp.broadcast_to(coords_ref[:, pl.ds(at, QUERY_BLOCK)], (QUERY_BLOCK, QUERY_BLOCK)).T
            for at in range(start, start + span, QUERY_BLOCK)
        ]
        gap = across - jnp.concatenate(along, axis=0)
        terms_ref[0, pl.ds(offset, span), :] = jnp.log(1.0 + jnp.abs(gap))
        terms_ref[1, pl.ds(offset, span), :] = jnp.tanh(-gap)

    lane = lax.broadcasted_iota(jnp.int32, (QUERY_BLOCK, 2 * head_width), 1) < head_width

    def pair(index, carry):
        columns = pl.ds(pl.multiple_of(index * 2 * head_width, 2 * head_width), 2 * head_width)
        for row, start, span, offset in windows:
            queries = two_heads(query_ref[pl.ds(row, QUERY_BLOCK), columns], lane)
            raw = dot_nt(key_ref[pl.ds(start, span), columns], queries)
            spread = terms_ref[0, pl.ds(offset, span), :]
            order = terms_ref[1, pl.ds(offset, span), :]
            mask = mask_ref[pl.ds(offset, span), :]
            for side in range(2):
                head = 2 * index + side
                own = raw[:, side * QUERY_BLOCK : (side + 1) * QUERY_BLOCK]
                scores = own * scale + (spread * rich_ref[0, head] + order * rich_ref[1, head]) + mask
                weights = jnp.exp(scores - jnp.max(scores, axis=0, keepdims=True))
                probs = low(weights * (1.0 / jnp.sum(weights, axis=0, keepdims=True)))
                probs_ref[index, pl.ds(offset, span), pl.ds(side * QUERY_BLOCK, QUERY_BLOCK)] = probs
                place = pl.ds(pl.multiple_of(head * head_width, head_width), head_width)
                turned_context[place, pl.ds(row, QUERY_BLOCK)] = dot_nn(
                    turned_ref[place, pl.ds(start, span)], probs
                )
        return carry

    lax.fori_loop(0, heads // 2, pair, 0)
    sums = None
    for part in range(parts):
        own = pl.ds(part * (rows // parts), rows // parts)
        context = low(turned_context[:, own].T)
        context_ref[own, :] = context
        branch = dot_nn(context, w_ref[3])
        resid = mid_ref[own, :].astype(F32) + branch
        resid_ref[own, :] = resid
        here = live_sums(length, part * (rows // parts), (branch, resid))
        sums = here if sums is None else [a + b for a, b in zip(sums, here)]
    stat_ref[0:1, :] = sums[0]
    stat_ref[1:2, :] = sums[1]


def attend_forward(length, mid, doc, coords, rich, gain, shift, weights):
    rows, width = mid.shape
    heads = rich.shape[1]
    full = whole((rows, width))
    _, band = attend_windows(rows)
    return kernel_call(
        attend_forward_body,
        (1,),
        [
            full, part_of((1, rows), doc, 1), pl.BlockSpec(memory_space=pltpu.SMEM),
            whole((2, width)), whole((2, width)), whole(weights.shape),
        ],
        [
            ((2, rows, width), BF16, whole((2, rows, width))),
            ((rows, width), BF16, full),
            ((rows, width), BF16, full),
            ((rows, width), BF16, full),
            ((heads // 2, band, 2 * QUERY_BLOCK), BF16, whole((heads // 2, band, 2 * QUERY_BLOCK))),
            ((2, band, QUERY_BLOCK), F32, whole((2, band, QUERY_BLOCK))),
            ((rows, width), F32, full),
            ((2, width), F32, whole((2, width))),
        ],
        [
            pltpu.VMEM((width, rows), BF16),
            pltpu.VMEM((width, rows), F32),
            pltpu.VMEM((band, QUERY_BLOCK), F32),
        ],
        56,
        8 * rows * width * width + 4 * band * QUERY_BLOCK * width,
        14 * rows * width + 8 * width * width + 2 * heads * band * QUERY_BLOCK,
        "attend_forward",
        heads * band * QUERY_BLOCK,
    )(length, mid, coords, rich, gain, shift, weights)


def attend_backward_body(
    length_ref, grad_ref, mid_ref, gain_ref, query_ref, key_ref, value_ref, probs_ref, terms_ref, w_ref,
    right_ref, out_ref, rich_out, gain_out, shift_out,
    turned_key, turned_query, context_ref, key_sum, value_sum,
):
    rows, width = mid_ref.shape
    pairs = probs_ref.shape[0]
    head_width = width // (2 * pairs)
    scale = head_width ** (-0.5)
    windows, _ = attend_windows(rows)
    parts = 2
    for part in range(parts):
        own = pl.ds(part * (rows // parts), rows // parts)
        grad_low = low(grad_ref[own, :])
        right_ref[3, own, :] = grad_low
        context_ref[own, :] = low(dot_nt(grad_low, w_ref[3]))
        turned_key[:, own] = low(key_ref[own, :].astype(F32).T)
    key_sum[...] = jnp.zeros_like(key_sum)
    value_sum[...] = jnp.zeros_like(value_sum)
    lane = lax.broadcasted_iota(jnp.int32, (QUERY_BLOCK, 2 * head_width), 1) < head_width

    def pair(index, carry):
        columns = pl.ds(pl.multiple_of(index * 2 * head_width, 2 * head_width), 2 * head_width)
        rich = [[0.0, 0.0], [0.0, 0.0]]
        for row, start, span, offset in windows:
            keys = pl.ds(start, span)
            context = two_heads(context_ref[pl.ds(row, QUERY_BLOCK), columns], lane)
            queries = two_heads(query_ref[pl.ds(row, QUERY_BLOCK), columns], lane)
            grad_probs = dot_nt(value_ref[keys, columns], context)
            probs = probs_ref[index, pl.ds(offset, span), :]
            value_sum[keys, columns] += dot_nn(probs, context)
            spread = terms_ref[0, pl.ds(offset, span), :]
            order = terms_ref[1, pl.ds(offset, span), :]
            grads = []
            for side in range(2):
                lanes = slice(side * QUERY_BLOCK, (side + 1) * QUERY_BLOCK)
                own = probs[:, lanes].astype(F32)
                mixed = own * grad_probs[:, lanes]
                grad_scores = mixed - own * jnp.sum(mixed, axis=0, keepdims=True)
                rich[0][side] += jnp.sum(grad_scores * spread, axis=0, keepdims=True)
                rich[1][side] += jnp.sum(grad_scores * order, axis=0, keepdims=True)
                grad_raw = low(grad_scores * scale)
                grads.append(grad_raw)
                place = pl.ds(
                    pl.multiple_of((2 * index + side) * head_width, head_width), head_width
                )
                turned_query[place, pl.ds(row, QUERY_BLOCK)] = dot_nn(turned_key[place, keys], grad_raw)
            key_sum[keys, columns] += dot_nn(jnp.concatenate(grads, axis=1), queries)
        for which in range(2):
            for side in range(2):
                rich_out[which, pl.ds(2 * index + side, 1), :] = rich[which][side]
        return carry

    lax.fori_loop(0, pairs, pair, 0)
    gains, shifts = None, None
    for part in range(parts):
        own = pl.ds(part * (rows // parts), rows // parts)
        grad_query = low(turned_query[:, own].T)
        grad_key = low(key_sum[own, :])
        grad_value = low(value_sum[own, :])
        right_ref[0, own, :] = grad_query
        right_ref[1, own, :] = grad_key
        right_ref[2, own, :] = grad_value
        grad_normed = (
            dot_nt(grad_query, w_ref[0]) + dot_nt(grad_key, w_ref[1]) + dot_nt(grad_value, w_ref[2])
        )
        grad_input, grad_gain, grad_shift = norm_backward(
            mid_ref[own, :].astype(F32), gain_ref[0:1, :], grad_normed
        )
        out_ref[own, :] = low(grad_ref[own, :] + grad_input)
        gains = grad_gain if gains is None else gains + grad_gain
        shifts = grad_shift if shifts is None else shifts + grad_shift
    gain_out[...] = gains
    shift_out[...] = shifts


def attend_backward(length, grad, mid, gain, query, key, value, probs, terms, weights):
    rows, width = mid.shape
    pairs, band, _ = probs.shape
    full = whole((rows, width))
    return kernel_call(
        attend_backward_body,
        (1,),
        [
            full, full, whole((2, width)), full, full, full, whole(probs.shape), whole(terms.shape),
            whole(weights.shape),
        ],
        [
            ((4, rows, width), BF16, whole((4, rows, width))),
            ((rows, width), BF16, full),
            ((2, 2 * pairs, QUERY_BLOCK), F32, whole((2, 2 * pairs, QUERY_BLOCK))),
            ((1, width), F32, whole((1, width))),
            ((1, width), F32, whole((1, width))),
        ],
        [
            pltpu.VMEM((width, rows), BF16),
            pltpu.VMEM((width, rows), F32),
            pltpu.VMEM((rows, width), BF16),
            pltpu.VMEM((rows, width), F32),
            pltpu.VMEM((rows, width), F32),
        ],
        56,
        8 * rows * width * width + 8 * band * QUERY_BLOCK * width,
        18 * rows * width + 8 * width * width + 4 * pairs * band * QUERY_BLOCK,
        "attend_backward",
    )(length, grad, mid, gain, query, key, value, probs, terms, weights)


def weight_body(count, flag_ref, *refs):
    one, two, out_ref = refs[: 2 * count], refs[2 * count : 4 * count], refs[4 * count]

    def write(side):
        total = None
        for doc in range(count):
            left, right = side[2 * doc][...], side[2 * doc + 1][...]
            left, right = (v.reshape(v.shape[-2:]) for v in (left, right))
            here = dot_tn(left, right)
            total = here if total is None else total + here
        out_ref[...] = low(total)

    @pl.when(flag_ref[0] == 1)
    def _():
        write(one)

    @pl.when(flag_ref[0] == 0)
    def _():
        write(two)


def weight_product(flag, one, two, grid, block, name):
    count = len(one)
    specs, operands = [], []
    for pick, side in ((1, one), (0, two)):
        for left, left_block, left_map, right, right_block, right_map in side:
            for array, shape, place in ((left, left_block, left_map), (right, right_block, right_map)):
                operands.append(array)
                specs.append(
                    pl.BlockSpec(
                        shape,
                        functools.partial(
                            lambda place, pick, j, chosen: place(jnp.where(chosen[0] == pick, j, 0)),
                            place,
                            pick,
                        ),
                    )
                )
    tall, wide = block
    return kernel_call(
        functools.partial(weight_body, count),
        (grid,),
        specs,
        [((grid * tall, wide), BF16, pl.BlockSpec(block, lambda j, *_: (j, 0)))],
        [],
        32,
        2 * grid * tall * wide * count * one[0][0].shape[-2],
        2 * (grid * tall * wide + sum(v.size for v in operands) // 2),
        name,
    )(flag, *operands)[0]


def passed_along(block, axis, distance):
    devices = range(lax.axis_size(axis))
    route = [(i - distance, i) for i in devices if i - distance in devices]
    return lax.ppermute(block, axis, route)


def exchanged_sum(block, axis):
    size = lax.axis_size(axis)
    step = 1
    while step < size:
        route = [(i, i ^ step) for i in range(size)]
        block = block + lax.ppermute(block, axis, route)
        step *= 2
    return block


def summed_over_documents(block):
    core = lax.axis_index("core")
    swap = [(0, 1), (1, 0)]
    half = block.shape[0] // 2
    own = lax.dynamic_slice_in_dim(block, core * half, half, 0)
    other = lax.dynamic_slice_in_dim(block, (1 - core) * half, half, 0)
    part = own + lax.ppermute(other, "core", swap)
    part = lax.psum(part, "chip")
    other = lax.ppermute(part, "core", swap)
    return jnp.concatenate(
        [jnp.where(core == 0, part, other), jnp.where(core == 0, other, part)], axis=0
    )


def local(
    boundary,
    lengths,
    neighbours,
    counts,
    coords,
    square_weights,
    up_weight,
    down_weight,
    up_bias,
    norm_gain,
    norm_bias,
    rich_terms,
):
    first = lax.axis_index("section") == 0
    flag = first.astype(jnp.int32)[None]
    documents = lengths.shape[0]
    rows = boundary.shape[1] // documents
    width = boundary.shape[2]
    hidden = up_weight.shape[2]
    heads = rich_terms.shape[1]
    source = boundary[0]
    squares = square_weights[0]
    up, down, bias = up_weight[0], down_weight[0], up_bias
    gains, shifts = norm_gain[0], norm_bias[0]
    near_t = neighbours.T
    counts_row, coords_row = counts[None], coords[None]
    length = [lax.slice_in_dim(lengths, doc, doc + 1) for doc in range(documents)]

    graph_kept, ff_one, resid_one, arrived, stats_one = [], [], [], [], []
    sent = None
    for doc in range(documents):
        here = source
        if doc:
            here, _ = lax.optimization_barrier((source, sent))
        left, links, sigma, pull, resid, stat = graph_forward(
            length[doc], here, doc, rows, near_t, counts_row, gains, shifts, squares
        )
        normed, active, slope, sent, stat_f = feed_forward(
            length[doc], resid, gains, shifts, up, bias, down
        )
        graph_kept.append((left, links, sigma, pull))
        ff_one.append((normed, active, slope))
        resid_one.append(resid)
        stats_one.append((stat, stat_f))
        arrived.append(passed_along(sent, "section", 1))

    back, out_two, rich_two, stats_two, ff_two, rights_two, small_two = [], [], [], [], [], [], []
    for doc in range(documents):
        left, query, key, value, probs, terms, resid, stat = attend_forward(
            length[doc], arrived[doc], doc, coords_row, rich_terms, gains, shifts, squares
        )
        normed, active, slope, result, stat_f = feed_forward(
            length[doc], resid, gains, shifts, up, bias, down
        )
        grad_pre, grad_bias, grad_resid, gain_f, shift_f = feed_backward(
            length[doc], source, doc, resid, gains, slope, up, down
        )
        right, grad_mid, rich, gain_a, shift_a = attend_backward(
            length[doc], grad_resid, arrived[doc], gains, query, key, value, probs, terms, squares
        )
        out_two.append(result)
        ff_two.append((normed, active, grad_pre))
        rights_two.append((left, right))
        stats_two.append((stat, stat_f))
        rich_two.append(rich)
        small_two.append((grad_bias, gain_a, gain_f, shift_a, shift_f))
        back.append(passed_along(grad_mid, "section", -1))
        last_sent = grad_mid

    out_one, pre_one, rights_one, small_one = [], [], [], []
    for doc in range(documents):
        grad_mid = back[doc]
        if doc < documents - 1:
            grad_mid, _ = lax.optimization_barrier((grad_mid, last_sent))
        left, links, sigma, pull = graph_kept[doc]
        normed, active, slope = ff_one[doc]
        grad_pre, grad_bias, grad_resid, gain_f, shift_f = feed_backward(
            length[doc], grad_mid, 0, resid_one[doc], gains, slope, up, down
        )
        right, grad_x, gain_a, shift_a = graph_backward(
            length[doc], grad_resid, source, doc, gains, sigma, pull, links, counts_row, squares
        )
        out_one.append(grad_x)
        pre_one.append(grad_pre)
        rights_one.append((left, right))
        small_one.append((grad_bias, gain_a, gain_f, shift_a, shift_f))

    docs = range(documents)
    tile = 512
    grad_down = weight_product(
        flag,
        [
            (ff_one[d][1], (rows, tile), lambda j: (0, j), back[d], (rows, width), lambda j: (0, 0))
            for d in docs
        ],
        [
            (
                ff_two[d][1], (rows, tile), lambda j: (0, j),
                source, (rows, width), functools.partial(lambda d, j: (d, 0), d),
            )
            for d in docs
        ],
        hidden // tile,
        (tile, width),
        "down_gradient",
    )
    still, across = lambda j: (0, 0), lambda j: (0, j)
    grad_up = weight_product(
        flag,
        [(ff_one[d][0], (rows, width), still, pre_one[d], (rows, width), across) for d in docs],
        [(ff_two[d][0], (rows, width), still, ff_two[d][2], (rows, width), across) for d in docs],
        hidden // width,
        (width, width),
        "up_gradient",
    )
    stack = (1, rows, width)
    grad_squares = weight_product(
        flag,
        [
            (
                rights_one[d][0], stack, lambda j: ((j + 1) // 2, 0, 0),
                rights_one[d][1], stack, lambda j: (jnp.maximum(j - 1, 0), 0, 0),
            )
            for d in docs
        ],
        [
            (
                rights_two[d][0], stack, lambda j: (j // 3, 0, 0),
                rights_two[d][1], stack, lambda j: (j, 0, 0),
            )
            for d in docs
        ],
        4,
        (width, width),
        "square_gradients",
    )
    down_total = summed_over_documents(grad_down).astype(F32)
    up_total = summed_over_documents(grad_up).astype(F32)
    up_total = up_total.reshape(hidden // width, width, width).transpose(1, 0, 2)
    square_total = summed_over_documents(grad_squares).astype(F32)

    def small_of(parts):
        return jnp.concatenate([sum(p[i] for p in parts).reshape(-1) for i in range(5)])

    def stats_of(parts):
        return sum(jnp.concatenate(p, axis=0) for p in parts).sum(axis=1)

    small = jnp.where(first, small_of(small_one), small_of(small_two))
    count = jnp.sum(lengths).astype(F32)[None]
    shared = jnp.concatenate(
        [
            jnp.where(first, stats_of(stats_one), 0.0),
            jnp.where(first, 0.0, stats_of(stats_two)),
            jnp.where(first, 0.0, sum(rich_two).sum(axis=-1)).reshape(-1),
            jnp.where(first, 0.0, count),
        ]
    )
    packed = jnp.concatenate([small, shared])
    packed = jnp.pad(packed, (0, -packed.shape[0] % 1024))
    packed = exchanged_sum(exchanged_sum(packed, "core"), "chip")
    crossed = lax.ppermute(packed, "section", [(0, 1), (1, 0)])
    start = small.shape[0]
    shared = packed[start : start + shared.shape[0]] + crossed[start : start + shared.shape[0]]
    rms = jnp.sqrt(shared[:8].reshape(2, 4) / (shared[8 + 2 * heads] * width))
    rich_total = shared[8 : 8 + 2 * heads].reshape(2, heads)
    boundary_out = jnp.concatenate(
        [jnp.where(first, out_one[doc], out_two[doc]) for doc in range(documents)], axis=0
    )[None]
    return (
        boundary_out,
        square_total.reshape(1, 4, width, width),
        up_total.reshape(1, width, hidden),
        down_total[None],
        packed[:hidden][None],
        packed[hidden : hidden + 2 * width].reshape(1, 2, width),
        packed[hidden + 2 * width : hidden + 4 * width].reshape(1, 2, width),
        rich_total,
        rms,
    )


def solution(mesh):
    sections, dp = mesh.devices.shape
    split = Mesh(mesh.devices.reshape(sections, dp // 2, 2), ("section", "chip", "core"))
    data = ("chip", "core")
    in_specs = (
        P("section", data, None),
        P(data),
        P(data, None),
        P(data),
        P(data),
        P("section", None, None, None),
        P("section", None, None),
        P("section", None, None),
        P("section", None),
        P("section", None, None),
        P("section", None, None),
        P(),
    )
    out_specs = (
        P("section", data, None),
        P("section", None, None, None),
        P("section", None, None),
        P("section", None, None),
        P("section", None),
        P("section", None, None),
        P("section", None, None),
        P(),
        P(),
    )
    return jax.shard_map(local, mesh=split, in_specs=in_specs, out_specs=out_specs, check_vma=False)
```

```python
import functools
import jax
import jax.numpy as jnp
from jax import lax
from jax.sharding import Mesh, PartitionSpec as P
from jax.experimental import pallas as pl
from jax.experimental.pallas import tpu as pltpu

RADIUS = 128
REACH = 64
QUERY_BLOCK = 128
EPSILON = 1e-05
NEG_FILL = -1e30
HIDDEN_TILE = 1024
GELU_C = 0.7978845608028654
F32, BF16 = jnp.float32, jnp.bfloat16
MIB = 1024 * 1024


def low(vector):
    return vector.astype(BF16)


def dot_nn(left, right):
    return jnp.dot(left, right, preferred_element_type=F32)


def dot_nt(left, right):
    return lax.dot_general(left, right, (((1,), (1,)), ((), ())), preferred_element_type=F32)


def dot_tn(left, right):
    return lax.dot_general(left, right, (((0,), (0,)), ((), ())), preferred_element_type=F32)


def normalized(vector):
    center = vector - jnp.mean(vector, axis=-1, keepdims=True)
    inverse = lax.rsqrt(jnp.mean(center * center, axis=-1, keepdims=True) + EPSILON)
    return center * inverse, inverse


def norm_backward(vector, gain_row, grad_normed):
    normed, inverse = normalized(vector)
    scaled = grad_normed * gain_row
    mean_scaled = jnp.mean(scaled, axis=-1, keepdims=True)
    mean_mixed = jnp.mean(scaled * normed, axis=-1, keepdims=True)
    grad_input = inverse * (scaled - mean_scaled - normed * mean_mixed)
    grad_gain = jnp.sum(grad_normed * normed, axis=0, keepdims=True)
    return grad_input, grad_gain, jnp.sum(grad_normed, axis=0, keepdims=True)


def live_sums(length, start, items):
    rows = items[0].shape[0]
    live = start + lax.broadcasted_iota(jnp.int32, (rows, 1), 0) < length
    return [jnp.sum(jnp.where(live, v * v, 0.0), axis=0, keepdims=True) for v in items]


def whole(shape):
    return pl.BlockSpec(shape, lambda *_: (0,) * len(shape))


def part_of(shape, doc, axis):
    place = tuple(doc if d == axis else 0 for d in range(len(shape)))
    return pl.BlockSpec(shape, lambda *_: place)


def column(row):
    return jnp.broadcast_to(row, (row.shape[1], row.shape[1])).T[:, 0:1]


def kernel_call(body, grid, in_specs, outs, scratch, flops, moved, name, aliases=None):
    return pl.pallas_call(
        body,
        out_shape=[jax.ShapeDtypeStruct(shape, kind) for shape, kind, _ in outs],
        grid_spec=pltpu.PrefetchScalarGridSpec(
            num_scalar_prefetch=1,
            grid=grid,
            in_specs=in_specs,
            out_specs=[spec for _, _, spec in outs],
            scratch_shapes=scratch,
        ),
        compiler_params=pltpu.CompilerParams(
            dimension_semantics=("arbitrary",) * len(grid), vmem_limit_bytes=60 * MIB
        ),
        cost_estimate=pl.CostEstimate(
            flops=int(flops) * 1, bytes_accessed=int(moved) * 1, transcendentals=0
        ),
        input_output_aliases=aliases or {},
        name=name,
    )


ANYWHERE = pl.BlockSpec(memory_space=pl.ANY)
PARTS = 2


def row_parts(rows):
    return [(at, pl.ds(at, rows // PARTS)) for at in range(0, rows, rows // PARTS)]


class Copies:
    def __init__(self, semaphores):
        self.semaphores, self.used, self.pending = semaphores, 0, []

    def start(self, source, target):
        copy = pltpu.make_async_copy(source, target, self.semaphores.at[self.used])
        self.used += 1
        copy.start()
        return copy

    def leave(self, source, target):
        self.pending.append(self.start(source, target))

    def finish(self):
        for copy in self.pending:
            copy.wait()


def add_rows(ref, rows, values):
    for at, value in zip(rows, values):
        ref[at : at + 1, :] += value


def feed_forward(resid_ref, gain, shift, up_ref, bias_ref, down_ref, normed_ref, active_ref, slope_ref, sum_ref):
    rows, hidden = active_ref.shape
    for _, own in row_parts(rows):
        normed_ref[own, :] = low(normalized(resid_ref[own, :])[0] * gain + shift)
    sum_ref[...] = jnp.zeros_like(sum_ref)

    def tile(index, carry):
        columns = pl.ds(pl.multiple_of(index * HIDDEN_TILE, HIDDEN_TILE), HIDDEN_TILE)
        for _, own in row_parts(rows):
            pre = dot_nn(normed_ref[own, :], up_ref[:, columns]) + bias_ref[:, columns]
            square = pre * pre
            curve = jnp.tanh(pre * (GELU_C + GELU_C * 0.044715 * square))
            half = 0.5 + 0.5 * curve
            active = low(pre * half)
            active_ref[own, columns] = active
            rise = pre * (GELU_C + 3.0 * GELU_C * 0.044715 * square)
            slope_ref[own, columns] = low(half + rise * (half - half * half) * 2.0)
            sum_ref[own, :] += dot_nn(active, down_ref[columns, :])
        return carry

    lax.fori_loop(0, hidden // HIDDEN_TILE, tile, 0)


def feed_backward_tile(columns, grad_ref, slope_ref, up_ref, down_ref, pre_ref, bias_ref, sum_ref):
    total = None
    for _, own in row_parts(grad_ref.shape[0]):
        grad_active = dot_nt(grad_ref[own, :], down_ref[columns, :])
        grad_pre = low(slope_ref[own, columns].astype(F32) * grad_active)
        pre_ref[own, columns] = grad_pre
        here = jnp.sum(grad_pre.astype(F32), axis=0, keepdims=True)
        total = here if total is None else total + here
        sum_ref[own, :] += dot_nt(grad_pre, up_ref[:, columns])
    bias_ref[:, columns] = total


def norm_back(out_ref, grad_ref, vector_ref, gain, sum_ref, gain_ref, shift_ref, at):
    gain_ref[at : at + 1, :] = jnp.zeros_like(gain)
    shift_ref[at : at + 1, :] = jnp.zeros_like(gain)
    for _, own in row_parts(out_ref.shape[0]):
        grad_input, grad_gain, grad_shift = norm_backward(vector_ref[own, :].astype(F32), gain, sum_ref[own, :])
        out_ref[own, :] = (grad_ref[own, :].astype(F32) + grad_input).astype(out_ref.dtype)
        gain_ref[at : at + 1, :] += grad_gain
        shift_ref[at : at + 1, :] += grad_shift


def graph_windows(rows):
    span = QUERY_BLOCK + 2 * REACH
    return [
        (start, min(max(start - REACH, 0), rows - span), span)
        for start in range(0, rows, QUERY_BLOCK)
    ]


def layer_one_forward_body(
    length_ref, x_ref, near_ref_t, counts_ref, gain_ref, shift_ref, bias_ref, w_any, up_any, down_any,
    mid_ref, stat_ref, link_ref, left_any, sigma_any, pull_any, resid_any, normed_any, active_any, slope_any,
    w_ref, up_ref, down_ref, left_ref, sigma_ref, pull_ref, resid_ref, normed_ref, active_ref, slope_ref, sum_ref,
    semaphores,
):
    rows, width = x_ref.shape
    length = length_ref[0]
    copies = Copies(semaphores)
    w_copies = [copies.start(w_any.at[i], w_ref.at[i]) for i in range(4)]
    up_copy, down_copy = copies.start(up_any, up_ref), copies.start(down_any, down_ref)
    graph_normed, mean_ref, mixed_ref = (left_ref.at[i] for i in range(3))
    stat_ref[...] = jnp.zeros_like(stat_ref)
    for _, own in row_parts(rows):
        graph_normed[own, :] = low(
            normalized(x_ref[own, :].astype(F32))[0] * gain_ref[0:1, :] + shift_ref[0:1, :]
        )
    slots = near_ref_t.shape[0]
    slot = lax.broadcasted_iota(jnp.int32, (slots, QUERY_BLOCK), 0)
    for row, start, span in graph_windows(rows):
        own = pl.ds(row, QUERY_BLOCK)
        counts = counts_ref[:, own]
        index = jnp.where(slot < counts, near_ref_t[:, own], -1)
        place = start + lax.broadcasted_iota(jnp.int32, (span, QUERY_BLOCK), 0)
        links = jnp.zeros((span, QUERY_BLOCK), F32)
        for s in range(slots):
            links += jnp.where(index[s : s + 1, :] == place, 1.0, 0.0)
        link_ref[:, own] = low(links)
        total = dot_nn(low(links.T), graph_normed[pl.ds(start, span), :])
        mean_ref[own, :] = low(total / column(counts.astype(F32)))
    for copy in w_copies:
        copy.wait()
    for at, own in row_parts(rows):
        pre = dot_nn(graph_normed[own, :], w_ref[0]) + dot_nn(mean_ref[own, :], w_ref[1])
        sigma = jax.nn.sigmoid(dot_nn(mean_ref[own, :], w_ref[2]))
        mixed = pre * sigma
        sigma_ref[own, :] = low(sigma)
        pull_ref[own, :] = low(mixed - mixed * sigma)
        mixed_ref[own, :] = low(mixed)
        branch = dot_nn(low(mixed), w_ref[3])
        resid = x_ref[own, :].astype(F32) + branch
        resid_ref[own, :] = resid
        add_rows(stat_ref, (0, 1), live_sums(length, at, (branch, resid)))
    copies.leave(left_ref, left_any)
    copies.leave(sigma_ref, sigma_any)
    copies.leave(pull_ref, pull_any)
    copies.leave(resid_ref, resid_any)
    up_copy.wait()
    down_copy.wait()
    feed_forward(
        resid_ref, gain_ref[1:2, :], shift_ref[1:2, :], up_ref, bias_ref, down_ref,
        normed_ref, active_ref, slope_ref, sum_ref,
    )
    copies.leave(normed_ref, normed_any)
    copies.leave(active_ref, active_any)
    copies.leave(slope_ref, slope_any)
    for at, own in row_parts(rows):
        branch = sum_ref[own, :]
        result = resid_ref[own, :] + branch
        mid_ref[own, :] = low(result)
        add_rows(stat_ref, (2, 3), live_sums(length, at, (branch, result)))
    copies.finish()


def layer_one_forward(length, x, doc, rows, near_t, counts, gain, shift, bias, weights, up, down):
    width, hidden = up.shape
    slots = near_t.shape[0]
    span = QUERY_BLOCK + 2 * REACH
    flat, wide = ((rows, width), BF16), ((rows, hidden), BF16)
    kept = [((3, rows, width), BF16), flat, flat, ((rows, width), F32), flat, wide, wide]
    return kernel_call(
        layer_one_forward_body,
        (1,),
        [
            part_of((rows, width), doc, 0), part_of((slots, rows), doc, 1), part_of((1, rows), doc, 1),
            whole((2, width)), whole((2, width)), whole((1, hidden)), ANYWHERE, ANYWHERE, ANYWHERE,
        ],
        [
            ((rows, width), BF16, whole((rows, width))),
            ((4, width), F32, whole((4, width))),
            ((span, rows), BF16, whole((span, rows))),
        ]
        + [(*what, ANYWHERE) for what in kept],
        [pltpu.VMEM(v.shape, BF16) for v in (weights, up, down)]
        + [pltpu.VMEM(*what) for what in kept]
        + [pltpu.VMEM((rows, width), F32), pltpu.SemaphoreType.DMA((13,))],
        8 * rows * width * width + 4 * rows * width * hidden,
        16 * rows * width + 8 * width * width + 4 * (rows + width) * hidden,
        "layer_one_forward",
    )(length, x, near_t, counts, gain, shift, bias, weights, up, down)


def layer_one_backward_body(
    length_ref, grad_ref, x_ref, gain_ref, counts_ref, link_ref,
    resid_any, slope_any, sigma_any, pull_any, w_any, up_any, down_any,
    out_ref, bias_out, gain_out, shift_out, pre_any, right_any,
    resid_ref, slope_ref, sigma_ref, pull_ref, w_ref, up_ref, down_ref,
    pre_ref, right_ref, grad_resid, mean_ref, sum_ref,
    semaphores,
):
    rows, width = x_ref.shape
    hidden = slope_ref.shape[1]
    copies = Copies(semaphores)
    tiles = [pl.ds(at, HIDDEN_TILE) for at in range(0, hidden, HIDDEN_TILE)]
    arriving = [
        [
            copies.start(down_any.at[columns, :], down_ref.at[columns, :]),
            copies.start(slope_any.at[:, columns], slope_ref.at[:, columns]),
            copies.start(up_any.at[:, columns], up_ref.at[:, columns]),
        ]
        for columns in tiles
    ]
    resid_copy = copies.start(resid_any, resid_ref)
    w_copies = [copies.start(w_any.at[i], w_ref.at[i]) for i in range(4)]
    gate_copies = [copies.start(sigma_any, sigma_ref), copies.start(pull_any, pull_ref)]
    counts_column = column(counts_ref[...].astype(F32))
    sum_ref[...] = jnp.zeros_like(sum_ref)
    for columns, parts in zip(tiles, arriving):
        for copy in parts:
            copy.wait()
        feed_backward_tile(columns, grad_ref, slope_ref, up_ref, down_ref, pre_ref, bias_out, sum_ref)
    copies.leave(pre_ref, pre_any)
    resid_copy.wait()
    norm_back(grad_resid, grad_ref, resid_ref, gain_ref[1:2, :], sum_ref, gain_out, shift_out, 1)
    for copy in w_copies + gate_copies:
        copy.wait()
    for at, own in row_parts(rows):
        grad_low = low(grad_resid[own, :])
        right_ref[2, own, :] = grad_low
        grad_mixed = dot_nt(grad_low, w_ref[3])
        grad_pre = low(sigma_ref[own, :].astype(F32) * grad_mixed)
        grad_gate = low(pull_ref[own, :].astype(F32) * grad_mixed)
        right_ref[0, own, :] = grad_pre
        right_ref[1, own, :] = grad_gate
        sum_ref[own, :] = dot_nt(grad_pre, w_ref[0])
        grad_mean = dot_nt(grad_pre, w_ref[1]) + dot_nt(grad_gate, w_ref[2])
        mean_ref[own, :] = low(grad_mean / counts_column[at : at + rows // PARTS, :])
    copies.leave(right_ref, right_any)
    for row, start, span in graph_windows(rows):
        own = pl.ds(row, QUERY_BLOCK)
        sum_ref[pl.ds(start, span), :] += dot_nn(link_ref[:, own], mean_ref[own, :])
    norm_back(out_ref, grad_resid, x_ref, gain_ref[0:1, :], sum_ref, gain_out, shift_out, 0)
    copies.finish()


def layer_one_backward(length, grad, x, doc, gain, counts, links, resid, slope, sigma, pull, weights, up, down):
    rows, width = grad.shape
    hidden = slope.shape[1]
    full = whole((rows, width))
    sent = [((rows, hidden), BF16), ((3, rows, width), BF16)]
    return kernel_call(
        layer_one_backward_body,
        (1,),
        [
            full, part_of((rows, width), doc, 0), whole((2, width)), part_of((1, rows), doc, 1), whole(links.shape),
        ]
        + [ANYWHERE] * 7,
        [
            ((rows, width), BF16, full),
            ((1, hidden), F32, whole((1, hidden))),
            ((2, width), F32, whole((2, width))),
            ((2, width), F32, whole((2, width))),
        ]
        + [(*what, ANYWHERE) for what in sent],
        [pltpu.VMEM(v.shape, v.dtype) for v in (resid, slope, sigma, pull, weights, up, down)]
        + [pltpu.VMEM(*what) for what in sent]
        + [
            pltpu.VMEM((rows, width), F32),
            pltpu.VMEM((rows, width), BF16),
            pltpu.VMEM((rows, width), F32),
            pltpu.SemaphoreType.DMA((3 * (hidden // HIDDEN_TILE) + 9,)),
        ],
        8 * rows * width * width + 4 * rows * width * hidden,
        18 * rows * width + 8 * width * width + 4 * (rows + width) * hidden,
        "layer_one_backward",
    )(length, grad, x, gain, counts, links, resid, slope, sigma, pull, weights, up, down)


def attend_windows(rows):
    windows, offset = [], 0
    for row in range(0, rows, QUERY_BLOCK):
        start = max(row - RADIUS, 0)
        span = min(row + QUERY_BLOCK + RADIUS, rows) - start
        windows.append((row, start, span, offset))
        offset += span
    return windows, offset


def two_heads(block, lane):
    zero = jnp.zeros_like(block)
    return jnp.concatenate([jnp.where(lane, block, zero), jnp.where(lane, zero, block)], axis=0)


def layer_two_body(
    length_ref, mid_ref, cotangent_ref, coords_ref, rich_ref, gain_ref, shift_ref, bias_ref, w_any, up_any, down_any,
    out_ref, result_ref, stat_ref, bias_out, gain_out, shift_out, rich_out,
    left_any, right_any, normed_any, active_any, pre_any,
    left_ref, right_ref, normed_ref, active_ref, pre_ref,
    w_ref, up_ref, down_ref, query_ref, key_ref, value_ref, probs_ref, terms_ref, mask_ref, slope_ref, resid_ref,
    grad_ref, sum_ref, key_sum, value_sum, turned_ref, turned_sum, semaphores,
):
    rows, width = mid_ref.shape
    hidden = active_ref.shape[1]
    heads = rich_ref.shape[1]
    head_width = width // heads
    scale = head_width ** (-0.5)
    length = length_ref[0]
    windows, _ = attend_windows(rows)
    copies = Copies(semaphores)
    w_copies = [copies.start(w_any.at[i], w_ref.at[i]) for i in range(4)]
    up_copy, down_copy = copies.start(up_any, up_ref), copies.start(down_any, down_ref)
    attend_normed, context_ref = left_ref.at[0], left_ref.at[1]
    stat_ref[...] = jnp.zeros_like(stat_ref)

    for row, start, span, offset in windows:
        i = row + lax.broadcasted_iota(jnp.int32, (span, QUERY_BLOCK), 1)
        j = start + lax.broadcasted_iota(jnp.int32, (span, QUERY_BLOCK), 0)
        allowed = (jnp.abs(i - j) <= RADIUS) & ((j < length) | (i == j))
        mask_ref[pl.ds(offset, span), :] = jnp.where(allowed, 0.0, NEG_FILL)
        across = coords_ref[:, pl.ds(row, QUERY_BLOCK)]
        along = [
            jnp.broadcast_to(coords_ref[:, pl.ds(at, QUERY_BLOCK)], (QUERY_BLOCK, QUERY_BLOCK)).T
            for at in range(start, start + span, QUERY_BLOCK)
        ]
        gap = across - jnp.concatenate(along, axis=0)
        terms_ref[0, pl.ds(offset, span), :] = jnp.log(1.0 + jnp.abs(gap))
        terms_ref[1, pl.ds(offset, span), :] = jnp.tanh(-gap)
    for copy in w_copies:
        copy.wait()
    for _, own in row_parts(rows):
        normed = low(normalized(mid_ref[own, :].astype(F32))[0] * gain_ref[0:1, :] + shift_ref[0:1, :])
        attend_normed[own, :] = normed
        query_ref[own, :] = low(dot_nn(normed, w_ref[0]))
        key_ref[own, :] = low(dot_nn(normed, w_ref[1]))
        value = dot_nn(normed, w_ref[2])
        value_ref[own, :] = low(value)
        turned_ref[:, own] = low(value.T)
    lane = lax.broadcasted_iota(jnp.int32, (QUERY_BLOCK, 2 * head_width), 1) < head_width

    def pair_of(index):
        return pl.ds(pl.multiple_of(index * 2 * head_width, 2 * head_width), 2 * head_width)

    def head_of(index, side):
        return pl.ds(pl.multiple_of((2 * index + side) * head_width, head_width), head_width)

    def attend(index, carry):
        columns = pair_of(index)
        for row, start, span, offset in windows:
            queries = two_heads(query_ref[pl.ds(row, QUERY_BLOCK), columns], lane)
            raw = dot_nt(key_ref[pl.ds(start, span), columns], queries)
            spread = terms_ref[0, pl.ds(offset, span), :]
            order = terms_ref[1, pl.ds(offset, span), :]
            mask = mask_ref[pl.ds(offset, span), :]
            for side in range(2):
                head = 2 * index + side
                own = raw[:, side * QUERY_BLOCK : (side + 1) * QUERY_BLOCK]
                scores = own * scale + (spread * rich_ref[0, head] + order * rich_ref[1, head]) + mask
                weights = jnp.exp(scores - jnp.max(scores, axis=0, keepdims=True))
                probs = low(weights * (1.0 / jnp.sum(weights, axis=0, keepdims=True)))
                probs_ref[index, pl.ds(offset, span), pl.ds(side * QUERY_BLOCK, QUERY_BLOCK)] = probs
                place = head_of(index, side)
                turned_sum[place, pl.ds(row, QUERY_BLOCK)] = dot_nn(
                    turned_ref[place, pl.ds(start, span)], probs
                )
        return carry

    lax.fori_loop(0, heads // 2, attend, 0)
    for at, own in row_parts(rows):
        context = low(turned_sum[:, own].T)
        context_ref[own, :] = context
        branch = dot_nn(context, w_ref[3])
        resid = mid_ref[own, :].astype(F32) + branch
        resid_ref[own, :] = resid
        add_rows(stat_ref, (0, 1), live_sums(length, at, (branch, resid)))
    copies.leave(left_ref, left_any)

    up_copy.wait()
    down_copy.wait()
    feed_forward(
        resid_ref, gain_ref[1:2, :], shift_ref[1:2, :], up_ref, bias_ref, down_ref,
        normed_ref, active_ref, slope_ref, sum_ref,
    )
    copies.leave(normed_ref, normed_any)
    copies.leave(active_ref, active_any)
    for at, own in row_parts(rows):
        branch = sum_ref[own, :]
        result = resid_ref[own, :] + branch
        result_ref[own, :] = low(result)
        add_rows(stat_ref, (2, 3), live_sums(length, at, (branch, result)))
    sum_ref[...] = jnp.zeros_like(sum_ref)

    def tile(index, carry):
        columns = pl.ds(pl.multiple_of(index * HIDDEN_TILE, HIDDEN_TILE), HIDDEN_TILE)
        feed_backward_tile(columns, cotangent_ref, slope_ref, up_ref, down_ref, pre_ref, bias_out, sum_ref)
        return carry

    lax.fori_loop(0, hidden // HIDDEN_TILE, tile, 0)
    copies.leave(pre_ref, pre_any)
    norm_back(grad_ref, cotangent_ref, resid_ref, gain_ref[1:2, :], sum_ref, gain_out, shift_out, 1)

    grad_context = right_ref.at[0]
    for _, own in row_parts(rows):
        grad_low = low(grad_ref[own, :])
        right_ref[3, own, :] = grad_low
        grad_context[own, :] = low(dot_nt(grad_low, w_ref[3]))
        turned_ref[:, own] = low(key_ref[own, :].astype(F32).T)
    key_sum[...] = jnp.zeros_like(key_sum)
    value_sum[...] = jnp.zeros_like(value_sum)

    def attend_back(index, carry):
        columns = pair_of(index)
        rich = [[0.0, 0.0], [0.0, 0.0]]
        for row, start, span, offset in windows:
            keys = pl.ds(start, span)
            context = two_heads(grad_context[pl.ds(row, QUERY_BLOCK), columns], lane)
            queries = two_heads(query_ref[pl.ds(row, QUERY_BLOCK), columns], lane)
            grad_probs = dot_nt(value_ref[keys, columns], context)
            probs = probs_ref[index, pl.ds(offset, span), :]
            value_sum[keys, columns] += dot_nn(probs, context)
            spread = terms_ref[0, pl.ds(offset, span), :]
            order = terms_ref[1, pl.ds(offset, span), :]
            grads = []
            for side in range(2):
                lanes = slice(side * QUERY_BLOCK, (side + 1) * QUERY_BLOCK)
                own = probs[:, lanes].astype(F32)
                mixed = own * grad_probs[:, lanes]
                grad_scores = mixed - own * jnp.sum(mixed, axis=0, keepdims=True)
                rich[0][side] += jnp.sum(grad_scores * spread, axis=0, keepdims=True)
                rich[1][side] += jnp.sum(grad_scores * order, axis=0, keepdims=True)
                grad_raw = low(grad_scores * scale)
                grads.append(grad_raw)
                place = head_of(index, side)
                turned_sum[place, pl.ds(row, QUERY_BLOCK)] = dot_nn(turned_ref[place, keys], grad_raw)
            key_sum[keys, columns] += dot_nn(jnp.concatenate(grads, axis=1), queries)
        for which in range(2):
            for side in range(2):
                rich_out[which, pl.ds(2 * index + side, 1), :] = rich[which][side]
        return carry

    lax.fori_loop(0, heads // 2, attend_back, 0)
    for _, own in row_parts(rows):
        grad_query = low(turned_sum[:, own].T)
        grad_key = low(key_sum[own, :])
        grad_value = low(value_sum[own, :])
        right_ref[0, own, :] = grad_query
        right_ref[1, own, :] = grad_key
        right_ref[2, own, :] = grad_value
        sum_ref[own, :] = (
            dot_nt(grad_query, w_ref[0]) + dot_nt(grad_key, w_ref[1]) + dot_nt(grad_value, w_ref[2])
        )
    copies.leave(right_ref, right_any)
    norm_back(out_ref, grad_ref, mid_ref, gain_ref[0:1, :], sum_ref, gain_out, shift_out, 0)
    copies.finish()


def layer_two(length, mid, cotangent, doc, coords, rich, gain, shift, bias, weights, up, down):
    rows, width = mid.shape
    hidden = up.shape[1]
    heads = rich.shape[1]
    full = whole((rows, width))
    _, band = attend_windows(rows)
    flat, wide = ((rows, width), BF16), ((rows, hidden), BF16)
    sent = [((2, rows, width), BF16), ((4, rows, width), BF16), flat, wide, wide]
    exact = ((rows, width), F32)
    held = [
        flat, flat, flat, ((heads // 2, band, 2 * QUERY_BLOCK), BF16), ((2, band, QUERY_BLOCK), F32),
        ((band, QUERY_BLOCK), F32), wide, exact, exact, exact, exact, exact, ((width, rows), BF16), ((width, rows), F32),
    ]
    return kernel_call(
        layer_two_body,
        (1,),
        [
            full, part_of((rows, width), doc, 0), part_of((1, rows), doc, 1), pl.BlockSpec(memory_space=pltpu.SMEM),
            whole((2, width)), whole((2, width)), whole((1, hidden)), ANYWHERE, ANYWHERE, ANYWHERE,
        ],
        [
            (*flat, full),
            (*flat, full),
            ((4, width), F32, whole((4, width))),
            ((1, hidden), F32, whole((1, hidden))),
            ((2, width), F32, whole((2, width))),
            ((2, width), F32, whole((2, width))),
            ((2, heads, QUERY_BLOCK), F32, whole((2, heads, QUERY_BLOCK))),
        ]
        + [(*what, ANYWHERE) for what in sent],
        [pltpu.VMEM(*what) for what in sent]
        + [pltpu.VMEM(v.shape, BF16) for v in (weights, up, down)]
        + [pltpu.VMEM(*what) for what in held]
        + [pltpu.SemaphoreType.DMA((11,))],
        16 * rows * width * width + 8 * rows * width * hidden + 12 * band * QUERY_BLOCK * width,
        20 * rows * width + 8 * width * width + 4 * (rows + width) * hidden,
        "layer_two",
    )(length, mid, cotangent, coords, rich, gain, shift, bias, weights, up, down)


def weight_body(count, picks_ref, *refs):
    one, two, outs = refs[: 2 * count], refs[2 * count : 4 * count], refs[4 * count :]
    step = pl.program_id(0)

    def write(side):
        total = None
        for doc in range(count):
            left, right = (v[...].reshape(v.shape[-2:]) for v in side[2 * doc : 2 * doc + 2])
            here = dot_tn(left, right)
            total = here if total is None else total + here
        for at in range(2):

            @pl.when(step == at)
            def _():
                outs[at][...] = low(total)

    for which, side in ((1, one), (0, two)):

        @pl.when(picks_ref[0] == which)
        def _():
            write(side)


def weight_quarters(picks, one, two, name):
    count = len(one)
    specs, operands = [], []
    for which, side in ((1, one), (0, two)):
        for left, left_block, left_map, right, right_block, right_map in side:
            for array, shape, place in ((left, left_block, left_map), (right, right_block, right_map)):

                def index(j, chosen, place=place, which=which):
                    return place(jnp.where(chosen[0] == which, chosen[1 + j], 0))

                operands.append(array)
                specs.append(pl.BlockSpec(shape, index))
    width, rows = one[0][4][-1], one[0][1][-2]
    quarter = whole((width, width))
    return kernel_call(
        functools.partial(weight_body, count),
        (2,),
        specs,
        [((width, width), BF16, quarter)] * 2,
        [],
        4 * width * width * count * rows,
        8 * width * width + 8 * count * rows * width,
        name,
    )(picks, *operands)


def place_body(count, places_ref, *refs):
    out_ref = refs[-1]
    for at, piece in enumerate(refs[:count]):

        @pl.when(pl.program_id(0) == at)
        def _():
            out_ref[...] = piece[...].astype(F32)


def placed(places, pieces, shape, columns, into, name):
    width = pieces[0].shape[0]
    if columns:
        spec = pl.BlockSpec((width, width), lambda i, where: (0, where[i]))
    else:
        spec = pl.BlockSpec((width, width), lambda i, where: (where[i], 0))
    more = [] if into is None else [into]
    return kernel_call(
        functools.partial(place_body, len(pieces)),
        (len(pieces),),
        [whole((width, width))] * len(pieces) + [ANYWHERE] * len(more),
        [(shape, F32, spec)],
        [],
        0,
        6 * len(pieces) * width * width,
        name,
        {1 + len(pieces): 0} if more else {},
    )(places, *pieces, *more)[0]


def pack_body(docs, flag_ref, lengths_ref, *refs):
    sides = {1: refs[: 4 * docs], 0: refs[4 * docs : 8 * docs]}
    rich_refs, out_ref = refs[8 * docs : 9 * docs], refs[9 * docs]
    width = out_ref.shape[1]

    def spread(values, base):
        sums = jnp.sum(values, axis=1, keepdims=True)
        shape = (values.shape[0], width)
        lane = lax.broadcasted_iota(jnp.int32, shape, 1)
        row = lax.broadcasted_iota(jnp.int32, shape, 0)
        return jnp.sum(jnp.where(lane == base + row, sums, 0.0), axis=0, keepdims=True)

    for which, side in sides.items():

        @pl.when(flag_ref[0] == which)
        def _():
            bias, gain, shift, stat = (sum(side[4 * d + i][...] for d in range(docs)) for i in range(4))
            for at in range(0, bias.shape[1], width):
                out_ref[at // width : at // width + 1, :] = bias[:, at : at + width]
            base = bias.shape[1] // width
            out_ref[base : base + 2, :] = gain
            out_ref[base + 2 : base + 4, :] = shift
            scalars = spread(stat, 0 if which else stat.shape[0])
            if not which:
                heads = rich_refs[0].shape[1]
                for term in range(2):
                    total = sum(ref[term] for ref in rich_refs)
                    scalars += spread(total, 2 * stat.shape[0] + term * heads)
                count = lengths_ref[0]
                for d in range(1, docs):
                    count += lengths_ref[d]
                lane = lax.broadcasted_iota(jnp.int32, (1, width), 1)
                scalars += jnp.where(lane == 2 * (stat.shape[0] + heads), count.astype(F32), 0.0)
            out_ref[base + 4 : base + 5, :] = scalars


def packed_row(flag, lengths, one, two, rich):
    docs = len(one)
    width = one[0][1].shape[1]
    operands = [v for side in (one, two) for parts in side for v in parts] + list(rich)
    rows = one[0][0].shape[1] // width + 5
    return kernel_call(
        functools.partial(pack_body, docs),
        (1,),
        [pl.BlockSpec(memory_space=pltpu.SMEM)] + [whole(v.shape) for v in operands],
        [((rows, width), F32, whole((rows, width)))],
        [],
        0,
        4 * sum(v.size for v in operands),
        "packed_row",
    )(flag, lengths, *operands)[0]


def passed_along(block, axis, distance):
    devices = range(lax.axis_size(axis))
    route = [(i - distance, i) for i in devices if i - distance in devices]
    return lax.ppermute(block, axis, route)


def after(value, token):
    return lax.optimization_barrier((value, token))[0]


def core_swap(block):
    return lax.ppermute(block, "core", [(0, 1), (1, 0)])


class Ordered:
    def __init__(self):
        self.token = None

    def read(self, *values):
        if self.token is None:
            return values if len(values) > 1 else values[0]
        values = lax.optimization_barrier((*values, self.token))[:-1]
        return values if len(values) > 1 else values[0]

    def gave(self, value):
        self.token = value
        return value


def rounded_sum(*blocks):
    return low(sum(block.astype(F32) for block in blocks))


def quarters_sum(order, sent, kept):
    swap = [(0, 1), (1, 0)]
    inward, outward, across = [(0, 1), (3, 2)], [(1, 0), (2, 3)], [(1, 2), (2, 1)]
    z = lax.axis_index("z")
    arrived = lax.ppermute(sent, "x", swap)
    yield
    total = order.gave(rounded_sum(*kept, order.read(arrived)))
    arrived = lax.ppermute(total, "z", inward)
    yield
    total = order.gave(rounded_sum(total, order.read(arrived)))
    arrived = lax.ppermute(total, "z", across)
    yield
    total = order.gave(rounded_sum(total, order.read(arrived)))
    arrived = lax.ppermute(total, "z", outward)
    yield
    total = order.gave(jnp.where((z == 1) | (z == 2), total, order.read(arrived)))
    arrived, near = lax.ppermute(total, "x", swap), core_swap(total)
    yield
    arrived = order.gave(order.read(arrived))
    yield total, near, arrived, core_swap(arrived)


def small_sum(order, block):
    for axis in ("core", "x", "z"):
        step = 1
        while step < lax.axis_size(axis):
            route = [(i, i ^ step) for i in range(lax.axis_size(axis))]
            arrived = lax.ppermute(block, axis, route)
            yield
            block = order.gave(block + order.read(arrived))
            step *= 2
    arrived = lax.ppermute(block, "section", [(0, 1), (1, 0)])
    yield
    arrived = order.read(arrived)
    yield block, arrived


def local(
    boundary,
    lengths,
    neighbours,
    counts,
    coords,
    square_weights,
    up_weight,
    down_weight,
    up_bias,
    norm_gain,
    norm_bias,
    rich_terms,
):
    first = lax.axis_index("section") == 0
    core, across_x = lax.axis_index("core"), lax.axis_index("x")
    if lax.axis_size("z") != 4 or lax.axis_size("x") != 2:
        across_x = across_x * 0
    use_one = first.astype(jnp.int32)
    give = jnp.stack([use_one, 2 * (1 - core) + 1 - across_x, 2 * (1 - core) + across_x])
    keep = jnp.stack([use_one, 2 * core + 1 - across_x, 2 * core + across_x])
    places = jnp.stack([keep[2], give[2], keep[1], give[1]])
    documents = lengths.shape[0]
    docs = range(documents)
    rows = boundary.shape[1] // documents
    width = boundary.shape[2]
    hidden = up_weight.shape[2]
    heads = rich_terms.shape[1]
    source = boundary[0]
    squares = square_weights[0]
    up, down, bias = up_weight[0], down_weight[0], up_bias
    gains, shifts = norm_gain[0], norm_bias[0]
    near_t = neighbours.T
    counts_row, coords_row = counts[None], coords[None]
    length = [lax.slice_in_dim(lengths, doc, doc + 1) for doc in range(documents)]

    kept_one, arrived, stats_one = [], [], []
    sent = None
    for doc in docs:
        here = source if sent is None else after(source, sent)
        sent, stat, links, left, sigma, pull, resid, normed, active, slope = layer_one_forward(
            length[doc], here, doc, rows, near_t, counts_row, gains, shifts, bias, squares, up, down
        )
        kept_one.append((links, resid, slope, sigma, pull, left, normed, active))
        stats_one.append(stat)
        arrived.append(passed_along(sent, "section", 1))

    back, out_two, rich_two, kept_two, small_two = [], [], [], [], []
    for doc in docs:
        grad_mid, result, stat, bias_grad, gain_grad, shift_grad, rich, left, right, normed, active, pre = layer_two(
            length[doc], arrived[doc], source, doc, coords_row, rich_terms, gains, shifts, bias, squares, up, down
        )
        out_two.append(result)
        kept_two.append((left, right, normed, active, pre))
        small_two.append((bias_grad, gain_grad, shift_grad, stat))
        rich_two.append(rich)
        back.append(passed_along(grad_mid, "section", -1))
        last_sent = grad_mid

    out_one, pre_one, right_one, small_one = [], [], [], []

    def first_back(doc, grad_mid):
        links, resid, slope, sigma, pull = kept_one[doc][:5]
        grad_x, bias_grad, gain_grad, shift_grad, pre, right = layer_one_backward(
            length[doc], grad_mid, source, doc, gains, counts_row, links, resid, slope, sigma, pull, squares, up, down
        )
        out_one.append(grad_x)
        pre_one.append(pre)
        right_one.append(right)
        small_one.append((bias_grad, gain_grad, shift_grad, stats_one[doc]))
        return grad_x

    token = last_sent
    for doc in range(documents - 1):
        token = first_back(doc, after(back[doc], token))
    if documents > 1:
        back[-1] = after(back[-1], token)

    quarter, stack = (rows, width), (1, rows, width)
    still, across = lambda q: (0, 0), lambda q: (0, q)
    own_rows = [functools.partial(lambda d, q: (d, 0), d) for d in docs]
    down_pairs = (
        [(kept_one[d][7], quarter, across, back[d], quarter, still) for d in docs],
        [(kept_two[d][3], quarter, across, source, quarter, own_rows[d]) for d in docs],
    )

    def up_pairs():
        return (
            [(kept_one[d][6], quarter, still, pre_one[d], quarter, across) for d in docs],
            [(kept_two[d][2], quarter, still, kept_two[d][4], quarter, across) for d in docs],
        )

    def square_pairs():
        left_one, right_of_one = lambda q: ((q + 1) // 2, 0, 0), lambda q: (jnp.maximum(q - 1, 0), 0, 0)
        left_two, right_of_two = lambda q: (q // 3, 0, 0), lambda q: (q, 0, 0)
        return (
            [(kept_one[d][5], stack, left_one, right_one[d], stack, right_of_one) for d in docs],
            [(kept_two[d][0], stack, left_two, kept_two[d][1], stack, right_of_two) for d in docs],
        )

    order = Ordered()
    custom = lax.axis_size("z") == 4 and lax.axis_size("x") == 2

    def products(pairs, name):
        given = weight_quarters(order.read(give), *pairs, name + "_give")
        order.gave(given[1])
        given = [core_swap(v) for v in given]
        kept = weight_quarters(order.read(keep), *pairs, name + "_keep")
        order.gave(kept[1])
        yield
        sent = order.gave(rounded_sum(kept[0], order.read(given[0])))
        if custom:
            yield from quarters_sum(order, sent, (kept[1], given[1]))
        else:
            near = lax.psum(rounded_sum(kept[1], given[1]), ("z", "x"))
            far = lax.psum(sent, ("z", "x"))
            yield from [None] * 5 + [(near, core_swap(near), far, core_swap(far))]

    totals = {}

    def place(name, pieces):
        shape = (width, hidden) if name == "up" else (hidden, width)
        near, near_swapped, far, far_swapped = pieces
        out = placed(
            places[:2], order.read(near, near_swapped), shape, name == "up", None, name + "_near"
        )
        order.gave(out)
        out = placed(places[2:], order.read(far, far_swapped), shape, name == "up", out, name + "_far")
        totals[name] = order.gave(out)

    down_sum = products(down_pairs, "down")
    next(down_sum)
    next(down_sum)
    order.gave(first_back(documents - 1, order.read(back[-1])))
    up_sum = products(up_pairs(), "up")
    next(up_sum)
    next(down_sum)
    next(up_sum)
    square_sum = products(square_pairs(), "square")
    next(square_sum)
    next(down_sum)
    next(square_sum)
    rows_out = [jnp.where(first, *order.read(out_one[doc], out_two[doc])) for doc in docs]
    boundary_out = order.gave(jnp.concatenate(rows_out, axis=0))[None]
    small = packed_row(use_one[None], order.read(lengths), small_one, small_two, rich_two)
    row_sum = small_sum(order, order.gave(small))
    next(row_sum)
    for steps in (up_sum, row_sum, down_sum, square_sum, up_sum, row_sum, down_sum, square_sum, up_sum, row_sum):
        next(steps)
    down_pieces = next(down_sum)
    next(square_sum)
    next(up_sum)
    for _ in range(lax.axis_size("z").bit_length() - 3):
        next(row_sum)
    next(row_sum)
    place("down", down_pieces)
    next(square_sum)
    up_pieces = next(up_sum)
    packed, crossed = next(row_sum)
    place("up", up_pieces)
    place("square", next(square_sum))
    down_total, up_total, square_total = totals["down"], totals["up"], totals["square"]

    at = hidden // width
    size = 9 + 2 * heads
    shared = packed[at + 4, :size] + crossed[at + 4, :size]
    rms = jnp.sqrt(shared[:8].reshape(2, 4) / (shared[8 + 2 * heads] * width))
    rich_total = shared[8 : 8 + 2 * heads].reshape(2, heads)
    return (
        boundary_out,
        square_total.reshape(1, 4, width, width),
        up_total.reshape(1, width, hidden),
        down_total[None],
        packed[:at].reshape(1, hidden),
        packed[at : at + 2][None],
        packed[at + 2 : at + 4][None],
        rich_total,
        rms,
    )


def solution(mesh):
    sections, dp = mesh.devices.shape
    split = Mesh(mesh.devices.reshape(sections, dp // 4, 2, 2), ("section", "z", "x", "core"))
    data = ("z", "x", "core")
    in_specs = (
        P("section", data, None),
        P(data),
        P(data, None),
        P(data),
        P(data),
        P("section", None, None, None),
        P("section", None, None),
        P("section", None, None),
        P("section", None),
        P("section", None, None),
        P("section", None, None),
        P(),
    )
    out_specs = (
        P("section", data, None),
        P("section", None, None, None),
        P("section", None, None),
        P("section", None, None),
        P("section", None),
        P("section", None, None),
        P("section", None, None),
        P(),
        P(),
    )
    return jax.shard_map(local, mesh=split, in_specs=in_specs, out_specs=out_specs, check_vma=False)
```

```python
import functools
import jax
import jax.numpy as jnp
from jax import lax
from jax.sharding import Mesh, PartitionSpec as P
from jax.experimental import pallas as pl
from jax.experimental.pallas import tpu as pltpu

RADIUS = 128
REACH = 64
QUERY_BLOCK = 128
EPSILON = 1e-05
NEG_FILL = -1e30
HIDDEN_TILE = 1024
SCALE = 1
GELU_C = 0.7978845608028654
F32, BF16 = jnp.float32, jnp.bfloat16
MIB = 1024 * 1024


def low(vector):
    return vector.astype(BF16)


def dot_nn(left, right):
    return jnp.dot(left, right, preferred_element_type=F32)


def dot_nt(left, right):
    return lax.dot_general(left, right, (((1,), (1,)), ((), ())), preferred_element_type=F32)


def dot_tn(left, right):
    return lax.dot_general(left, right, (((0,), (0,)), ((), ())), preferred_element_type=F32)


def normalized(vector):
    center = vector - jnp.mean(vector, axis=-1, keepdims=True)
    inverse = lax.rsqrt(jnp.mean(center * center, axis=-1, keepdims=True) + EPSILON)
    return center * inverse, inverse


def norm_backward(vector, gain_row, grad_normed):
    normed, inverse = normalized(vector)
    scaled = grad_normed * gain_row
    mean_scaled = jnp.mean(scaled, axis=-1, keepdims=True)
    mean_mixed = jnp.mean(scaled * normed, axis=-1, keepdims=True)
    grad_input = inverse * (scaled - mean_scaled - normed * mean_mixed)
    grad_gain = jnp.sum(grad_normed * normed, axis=0, keepdims=True)
    return grad_input, grad_gain, jnp.sum(grad_normed, axis=0, keepdims=True)


def live_sums(length, start, items):
    rows = items[0].shape[0]
    live = start + lax.broadcasted_iota(jnp.int32, (rows, 1), 0) < length
    return [jnp.sum(jnp.where(live, v * v, 0.0), axis=0, keepdims=True) for v in items]


def whole(shape):
    return pl.BlockSpec(shape, lambda *_: (0,) * len(shape))


def part_of(shape, doc, axis):
    place = tuple(doc if d == axis else 0 for d in range(len(shape)))
    return pl.BlockSpec(shape, lambda *_: place)


def column(row):
    return jnp.broadcast_to(row, (row.shape[1], row.shape[1])).T[:, 0:1]


def kernel_call(body, grid, in_specs, outs, scratch, flops, moved, name, aliases=None, token=None):
    taken, given = 1 + len(in_specs), len(outs)

    def with_token(*refs):
        rest = refs[taken + 1 :]
        body(*refs[:taken], *rest[:given], *rest[given + 1 :])

    if token is not None:
        in_specs = [*in_specs, pl.BlockSpec(memory_space=pl.ANY)]
        outs = [*outs, (token.shape, token.dtype, pl.BlockSpec(memory_space=pl.ANY))]
    call = pl.pallas_call(
        body if token is None else with_token,
        out_shape=[jax.ShapeDtypeStruct(shape, kind) for shape, kind, _ in outs],
        grid_spec=pltpu.PrefetchScalarGridSpec(
            num_scalar_prefetch=1,
            grid=grid,
            in_specs=in_specs,
            out_specs=[spec for _, _, spec in outs],
            scratch_shapes=scratch,
        ),
        compiler_params=pltpu.CompilerParams(
            dimension_semantics=("arbitrary",) * len(grid), vmem_limit_bytes=60 * MIB
        ),
        cost_estimate=pl.CostEstimate(flops=SCALE * int(flops), bytes_accessed=SCALE * int(moved), transcendentals=0),
        input_output_aliases=aliases or {},
        name=name,
    )
    return call if token is None else lambda *operands: call(*operands, token)


ANYWHERE = pl.BlockSpec(memory_space=pl.ANY)
PARTS = 2


def row_parts(rows):
    return [(at, pl.ds(at, rows // PARTS)) for at in range(0, rows, rows // PARTS)]


class Copies:
    def __init__(self, semaphores):
        self.semaphores, self.used, self.pending = semaphores, 0, []

    def start(self, source, target):
        copy = pltpu.make_async_copy(source, target, self.semaphores.at[self.used])
        self.used += 1
        copy.start()
        return copy

    def leave(self, source, target):
        self.pending.append(self.start(source, target))

    def finish(self):
        for copy in self.pending:
            copy.wait()


def add_rows(ref, rows, values):
    for at, value in zip(rows, values):
        ref[at : at + 1, :] += value


def feed_forward(resid_ref, gain, shift, up_ref, bias_ref, down_ref, normed_ref, active_ref, slope_ref, sum_ref):
    rows, hidden = active_ref.shape
    for _, own in row_parts(rows):
        normed_ref[own, :] = low(normalized(resid_ref[own, :])[0] * gain + shift)
    sum_ref[...] = jnp.zeros_like(sum_ref)

    def tile(index, carry):
        columns = pl.ds(pl.multiple_of(index * HIDDEN_TILE, HIDDEN_TILE), HIDDEN_TILE)
        parts = [own for _, own in row_parts(rows)]
        pres = [dot_nn(normed_ref[own, :], up_ref[:, columns]) + bias_ref[:, columns] for own in parts]
        for own, pre in zip(parts, pres):
            square = pre * pre
            curve = jnp.tanh(pre * (GELU_C + GELU_C * 0.044715 * square))
            half = 0.5 + 0.5 * curve
            active = low(pre * half)
            active_ref[own, columns] = active
            rise = pre * (GELU_C + 3.0 * GELU_C * 0.044715 * square)
            slope_ref[own, columns] = low(half + rise * (half - half * half) * 2.0)
            sum_ref[own, :] += dot_nn(active, down_ref[columns, :])
        return carry

    lax.fori_loop(0, hidden // HIDDEN_TILE, tile, 0)


def feed_backward_tile(columns, grad_ref, slope_ref, up_ref, down_ref, pre_ref, bias_ref, sum_ref):
    total = None
    for _, own in row_parts(grad_ref.shape[0]):
        grad_active = dot_nt(grad_ref[own, :], down_ref[columns, :])
        grad_pre = low(slope_ref[own, columns].astype(F32) * grad_active)
        pre_ref[own, columns] = grad_pre
        here = jnp.sum(grad_pre.astype(F32), axis=0, keepdims=True)
        total = here if total is None else total + here
        sum_ref[own, :] += dot_nt(grad_pre, up_ref[:, columns])
    bias_ref[:, columns] = total


def norm_back(out_ref, grad_ref, vector_ref, gain, sum_ref, gain_ref, shift_ref, at):
    gain_ref[at : at + 1, :] = jnp.zeros_like(gain)
    shift_ref[at : at + 1, :] = jnp.zeros_like(gain)
    for _, own in row_parts(out_ref.shape[0]):
        grad_input, grad_gain, grad_shift = norm_backward(vector_ref[own, :].astype(F32), gain, sum_ref[own, :])
        out_ref[own, :] = (grad_ref[own, :].astype(F32) + grad_input).astype(out_ref.dtype)
        gain_ref[at : at + 1, :] += grad_gain
        shift_ref[at : at + 1, :] += grad_shift


def graph_windows(rows):
    span = QUERY_BLOCK + 2 * REACH
    return [
        (start, min(max(start - REACH, 0), rows - span), span)
        for start in range(0, rows, QUERY_BLOCK)
    ]


def layer_one_forward_body(
    length_ref, x_ref, near_ref_t, counts_ref, gain_ref, shift_ref, bias_ref, w_any, up_any, down_any,
    mid_ref, stat_ref, link_ref, left_any, sigma_any, pull_any, resid_any, normed_any, active_any, slope_any,
    w_ref, up_ref, down_ref, left_ref, sigma_ref, pull_ref, resid_ref, normed_ref, active_ref, slope_ref, sum_ref,
    semaphores,
):
    @pl.when(length_ref[1] == 1)
    def _():
        rows, width = x_ref.shape
        length = length_ref[0]
        copies = Copies(semaphores)
        w_copies = [copies.start(w_any.at[i], w_ref.at[i]) for i in range(4)]
        up_copy, down_copy = copies.start(up_any, up_ref), copies.start(down_any, down_ref)
        graph_normed, mean_ref, mixed_ref = (left_ref.at[i] for i in range(3))
        stat_ref[...] = jnp.zeros_like(stat_ref)
        for _, own in row_parts(rows):
            graph_normed[own, :] = low(
                normalized(x_ref[own, :].astype(F32))[0] * gain_ref[0:1, :] + shift_ref[0:1, :]
            )
        slots = near_ref_t.shape[0]
        slot = lax.broadcasted_iota(jnp.int32, (slots, QUERY_BLOCK), 0)
        for row, start, span in graph_windows(rows):
            own = pl.ds(row, QUERY_BLOCK)
            counts = counts_ref[:, own]
            index = jnp.where(slot < counts, near_ref_t[:, own], -1)
            place = start + lax.broadcasted_iota(jnp.int32, (span, QUERY_BLOCK), 0)
            links = jnp.zeros((span, QUERY_BLOCK), F32)
            for s in range(slots):
                links += jnp.where(index[s : s + 1, :] == place, 1.0, 0.0)
            link_ref[:, own] = low(links)
            total = dot_nn(low(links.T), graph_normed[pl.ds(start, span), :])
            mean_ref[own, :] = low(total / column(counts.astype(F32)))
        for copy in w_copies:
            copy.wait()
        for at, own in row_parts(rows):
            pre = dot_nn(graph_normed[own, :], w_ref[0]) + dot_nn(mean_ref[own, :], w_ref[1])
            sigma = jax.nn.sigmoid(dot_nn(mean_ref[own, :], w_ref[2]))
            mixed = pre * sigma
            sigma_ref[own, :] = low(sigma)
            pull_ref[own, :] = low(mixed - mixed * sigma)
            mixed_ref[own, :] = low(mixed)
            branch = dot_nn(low(mixed), w_ref[3])
            resid = x_ref[own, :].astype(F32) + branch
            resid_ref[own, :] = resid
            add_rows(stat_ref, (0, 1), live_sums(length, at, (branch, resid)))
        copies.leave(left_ref, left_any)
        copies.leave(sigma_ref, sigma_any)
        copies.leave(pull_ref, pull_any)
        copies.leave(resid_ref, resid_any)
        up_copy.wait()
        down_copy.wait()
        feed_forward(
            resid_ref, gain_ref[1:2, :], shift_ref[1:2, :], up_ref, bias_ref, down_ref,
            normed_ref, active_ref, slope_ref, sum_ref,
        )
        copies.leave(normed_ref, normed_any)
        copies.leave(active_ref, active_any)
        copies.leave(slope_ref, slope_any)
        for at, own in row_parts(rows):
            branch = sum_ref[own, :]
            result = resid_ref[own, :] + branch
            mid_ref[own, :] = low(result)
            add_rows(stat_ref, (2, 3), live_sums(length, at, (branch, result)))
        copies.finish()


def layer_one_forward(length, x, doc, rows, near_t, counts, gain, shift, bias, weights, up, down):
    width, hidden = up.shape
    slots = near_t.shape[0]
    span = QUERY_BLOCK + 2 * REACH
    flat, wide = ((rows, width), BF16), ((rows, hidden), BF16)
    kept = [((3, rows, width), BF16), flat, flat, ((rows, width), F32), flat, wide, wide]
    return kernel_call(
        layer_one_forward_body,
        (1,),
        [
            part_of((rows, width), doc, 0), part_of((slots, rows), doc, 1), part_of((1, rows), doc, 1),
            whole((2, width)), whole((2, width)), whole((1, hidden)), ANYWHERE, ANYWHERE, ANYWHERE,
        ],
        [
            ((rows, width), BF16, whole((rows, width))),
            ((4, width), F32, whole((4, width))),
            ((span, rows), BF16, whole((span, rows))),
        ]
        + [(*what, ANYWHERE) for what in kept],
        [pltpu.VMEM(v.shape, BF16) for v in (weights, up, down)]
        + [pltpu.VMEM(*what) for what in kept]
        + [pltpu.VMEM((rows, width), F32), pltpu.SemaphoreType.DMA((13,))],
        8 * rows * width * width + 4 * rows * width * hidden,
        16 * rows * width + 8 * width * width + 4 * (rows + width) * hidden,
        "layer_one_forward",
    )(length, x, near_t, counts, gain, shift, bias, weights, up, down)


def layer_one_backward_body(
    length_ref, grad_ref, x_ref, gain_ref, counts_ref, link_ref,
    resid_any, slope_any, sigma_any, pull_any, w_any, up_any, down_any, pre_given, right_given,
    out_ref, bias_out, gain_out, shift_out, pre_any, right_any,
    resid_ref, slope_ref, sigma_ref, pull_ref, w_ref, up_ref, down_ref,
    pre_ref, right_ref, grad_resid, mean_ref, sum_ref,
    semaphores,
):
    @pl.when(length_ref[1] == 1)
    def _():
        rows, width = x_ref.shape
        hidden = slope_ref.shape[1]
        copies = Copies(semaphores)
        tiles = [pl.ds(at, HIDDEN_TILE) for at in range(0, hidden, HIDDEN_TILE)]
        arriving = [
            [
                copies.start(down_any.at[columns, :], down_ref.at[columns, :]),
                copies.start(slope_any.at[:, columns], slope_ref.at[:, columns]),
                copies.start(up_any.at[:, columns], up_ref.at[:, columns]),
            ]
            for columns in tiles
        ]
        resid_copy = copies.start(resid_any, resid_ref)
        w_copies = [copies.start(w_any.at[i], w_ref.at[i]) for i in range(4)]
        gate_copies = [copies.start(sigma_any, sigma_ref), copies.start(pull_any, pull_ref)]
        counts_column = column(counts_ref[...].astype(F32))
        sum_ref[...] = jnp.zeros_like(sum_ref)
        for columns, parts in zip(tiles, arriving):
            for copy in parts:
                copy.wait()
            feed_backward_tile(columns, grad_ref, slope_ref, up_ref, down_ref, pre_ref, bias_out, sum_ref)
        copies.leave(pre_ref, pre_any)
        resid_copy.wait()
        norm_back(grad_resid, grad_ref, resid_ref, gain_ref[1:2, :], sum_ref, gain_out, shift_out, 1)
        for copy in w_copies + gate_copies:
            copy.wait()
        for at, own in row_parts(rows):
            grad_low = low(grad_resid[own, :])
            right_ref[2, own, :] = grad_low
            grad_mixed = dot_nt(grad_low, w_ref[3])
            grad_pre = low(sigma_ref[own, :].astype(F32) * grad_mixed)
            grad_gate = low(pull_ref[own, :].astype(F32) * grad_mixed)
            right_ref[0, own, :] = grad_pre
            right_ref[1, own, :] = grad_gate
            sum_ref[own, :] = dot_nt(grad_pre, w_ref[0])
            grad_mean = dot_nt(grad_pre, w_ref[1]) + dot_nt(grad_gate, w_ref[2])
            mean_ref[own, :] = low(grad_mean / counts_column[at : at + rows // PARTS, :])
        copies.leave(right_ref, right_any.at[0:3])
        for row, start, span in graph_windows(rows):
            own = pl.ds(row, QUERY_BLOCK)
            sum_ref[pl.ds(start, span), :] += dot_nn(link_ref[:, own], mean_ref[own, :])
        norm_back(out_ref, grad_resid, x_ref, gain_ref[0:1, :], sum_ref, gain_out, shift_out, 0)
        copies.finish()


def layer_one_backward(length, grad, x, doc, gain, counts, links, resid, slope, sigma, pull, weights, up, down, pre, right, token=None):
    rows, width = grad.shape
    hidden = slope.shape[1]
    full = whole((rows, width))
    sent = [((rows, hidden), BF16), ((3, rows, width), BF16)]
    return kernel_call(
        layer_one_backward_body,
        (1,),
        [
            full, part_of((rows, width), doc, 0), whole((2, width)), part_of((1, rows), doc, 1), whole(links.shape),
        ]
        + [ANYWHERE] * 9,
        [
            ((rows, width), BF16, full),
            ((1, hidden), F32, whole((1, hidden))),
            ((2, width), F32, whole((2, width))),
            ((2, width), F32, whole((2, width))),
        ]
        + [(pre.shape, BF16, ANYWHERE), (right.shape, BF16, ANYWHERE)],
        [pltpu.VMEM(v.shape, v.dtype) for v in (resid, slope, sigma, pull, weights, up, down)]
        + [pltpu.VMEM(*what) for what in sent]
        + [
            pltpu.VMEM((rows, width), F32),
            pltpu.VMEM((rows, width), BF16),
            pltpu.VMEM((rows, width), F32),
            pltpu.SemaphoreType.DMA((3 * (hidden // HIDDEN_TILE) + 9,)),
        ],
        8 * rows * width * width + 4 * rows * width * hidden,
        18 * rows * width + 8 * width * width + 4 * (rows + width) * hidden,
        "layer_one_backward",
        {13: 4, 14: 5},
        token,
    )(length, grad, x, gain, counts, links, resid, slope, sigma, pull, weights, up, down, pre, right)


def attend_windows(rows):
    windows, offset = [], 0
    for row in range(0, rows, QUERY_BLOCK):
        start = max(row - RADIUS, 0)
        span = min(row + QUERY_BLOCK + RADIUS, rows) - start
        windows.append((row, start, span, offset))
        offset += span
    return windows, offset


def two_heads(block, lane):
    zero = jnp.zeros_like(block)
    return jnp.concatenate([jnp.where(lane, block, zero), jnp.where(lane, zero, block)], axis=0)


def layer_two_body(
    length_ref, mid_ref, cotangent_ref, coords_ref, rich_ref, gain_ref, shift_ref, bias_ref, w_any, up_any, down_any,
    left_given, normed_given, active_given,
    out_ref, result_ref, stat_ref, bias_out, gain_out, shift_out, rich_out,
    left_any, right_any, normed_any, active_any, pre_any,
    left_ref, right_ref, normed_ref, active_ref, pre_ref,
    w_ref, up_ref, down_ref, query_ref, key_ref, value_ref, probs_ref, terms_ref, mask_ref, slope_ref, resid_ref,
    grad_ref, sum_ref, key_sum, value_sum, turned_ref, turned_sum, semaphores,
):
    @pl.when(length_ref[1] == 0)
    def _():
        rows, width = mid_ref.shape
        hidden = active_ref.shape[1]
        heads = rich_ref.shape[1]
        head_width = width // heads
        scale = head_width ** (-0.5)
        length = length_ref[0]
        windows, _ = attend_windows(rows)
        copies = Copies(semaphores)
        w_copies = [copies.start(w_any.at[i], w_ref.at[i]) for i in range(4)]
        attend_normed, context_ref = left_ref.at[0], left_ref.at[1]
        stat_ref[...] = jnp.zeros_like(stat_ref)

        for row, start, span, offset in windows:
            i = row + lax.broadcasted_iota(jnp.int32, (span, QUERY_BLOCK), 1)
            j = start + lax.broadcasted_iota(jnp.int32, (span, QUERY_BLOCK), 0)
            allowed = (jnp.abs(i - j) <= RADIUS) & ((j < length) | (i == j))
            mask_ref[pl.ds(offset, span), :] = jnp.where(allowed, 0.0, NEG_FILL)
            across = coords_ref[:, pl.ds(row, QUERY_BLOCK)]
            along = [
                jnp.broadcast_to(coords_ref[:, pl.ds(at, QUERY_BLOCK)], (QUERY_BLOCK, QUERY_BLOCK)).T
                for at in range(start, start + span, QUERY_BLOCK)
            ]
            gap = across - jnp.concatenate(along, axis=0)
            terms_ref[0, pl.ds(offset, span), :] = jnp.log(1.0 + jnp.abs(gap))
            terms_ref[1, pl.ds(offset, span), :] = jnp.tanh(-gap)
        for copy in w_copies:
            copy.wait()
        up_copy, down_copy = copies.start(up_any, up_ref), copies.start(down_any, down_ref)
        for _, own in row_parts(rows):
            normed = low(normalized(mid_ref[own, :].astype(F32))[0] * gain_ref[0:1, :] + shift_ref[0:1, :])
            attend_normed[own, :] = normed
            query_ref[own, :] = low(dot_nn(normed, w_ref[0]))
            key_ref[own, :] = low(dot_nn(normed, w_ref[1]))
            value = dot_nn(normed, w_ref[2])
            value_ref[own, :] = low(value)
            turned_ref[:, own] = low(value.T)
        lane = lax.broadcasted_iota(jnp.int32, (QUERY_BLOCK, 2 * head_width), 1) < head_width

        def pair_of(index):
            return pl.ds(pl.multiple_of(index * 2 * head_width, 2 * head_width), 2 * head_width)

        def head_of(index, side):
            return pl.ds(pl.multiple_of((2 * index + side) * head_width, head_width), head_width)

        def attend(index, carry):
            columns = pair_of(index)
            for row, start, span, offset in windows:
                queries = two_heads(query_ref[pl.ds(row, QUERY_BLOCK), columns], lane)
                raw = dot_nt(key_ref[pl.ds(start, span), columns], queries)
                spread = terms_ref[0, pl.ds(offset, span), :]
                order = terms_ref[1, pl.ds(offset, span), :]
                mask = mask_ref[pl.ds(offset, span), :]
                for side in range(2):
                    head = 2 * index + side
                    own = raw[:, side * QUERY_BLOCK : (side + 1) * QUERY_BLOCK]
                    scores = own * scale + (spread * rich_ref[0, head] + order * rich_ref[1, head]) + mask
                    weights = jnp.exp(scores - jnp.max(scores, axis=0, keepdims=True))
                    probs = low(weights * (1.0 / jnp.sum(weights, axis=0, keepdims=True)))
                    probs_ref[index, pl.ds(offset, span), pl.ds(side * QUERY_BLOCK, QUERY_BLOCK)] = probs
                    place = head_of(index, side)
                    turned_sum[place, pl.ds(row, QUERY_BLOCK)] = dot_nn(
                        turned_ref[place, pl.ds(start, span)], probs
                    )
            return carry

        lax.fori_loop(0, heads // 2, attend, 0, unroll=2)
        for at, own in row_parts(rows):
            context = low(turned_sum[:, own].T)
            context_ref[own, :] = context
            branch = dot_nn(context, w_ref[3])
            resid = mid_ref[own, :].astype(F32) + branch
            resid_ref[own, :] = resid
            add_rows(stat_ref, (0, 1), live_sums(length, at, (branch, resid)))
        copies.leave(left_ref, left_any.at[0:2])

        up_copy.wait()
        down_copy.wait()
        feed_forward(
            resid_ref, gain_ref[1:2, :], shift_ref[1:2, :], up_ref, bias_ref, down_ref,
            normed_ref, active_ref, slope_ref, sum_ref,
        )
        copies.leave(normed_ref, normed_any)
        copies.leave(active_ref, active_any)
        for at, own in row_parts(rows):
            branch = sum_ref[own, :]
            result = resid_ref[own, :] + branch
            result_ref[own, :] = low(result)
            add_rows(stat_ref, (2, 3), live_sums(length, at, (branch, result)))
        sum_ref[...] = jnp.zeros_like(sum_ref)

        def tile(index, carry):
            columns = pl.ds(pl.multiple_of(index * HIDDEN_TILE, HIDDEN_TILE), HIDDEN_TILE)
            feed_backward_tile(columns, cotangent_ref, slope_ref, up_ref, down_ref, pre_ref, bias_out, sum_ref)
            return carry

        lax.fori_loop(0, hidden // HIDDEN_TILE, tile, 0)
        copies.leave(pre_ref, pre_any)
        norm_back(grad_ref, cotangent_ref, resid_ref, gain_ref[1:2, :], sum_ref, gain_out, shift_out, 1)

        grad_context = right_ref.at[0]
        for _, own in row_parts(rows):
            grad_low = low(grad_ref[own, :])
            right_ref[3, own, :] = grad_low
            grad_context[own, :] = low(dot_nt(grad_low, w_ref[3]))
            turned_ref[:, own] = low(key_ref[own, :].astype(F32).T)
        key_sum[...] = jnp.zeros_like(key_sum)
        value_sum[...] = jnp.zeros_like(value_sum)

        def attend_back(index, carry):
            columns = pair_of(index)
            rich = [[0.0, 0.0], [0.0, 0.0]]
            for row, start, span, offset in windows:
                keys = pl.ds(start, span)
                context = two_heads(grad_context[pl.ds(row, QUERY_BLOCK), columns], lane)
                queries = two_heads(query_ref[pl.ds(row, QUERY_BLOCK), columns], lane)
                grad_probs = dot_nt(value_ref[keys, columns], context)
                probs = probs_ref[index, pl.ds(offset, span), :]
                value_sum[keys, columns] += dot_nn(probs, context)
                spread = terms_ref[0, pl.ds(offset, span), :]
                order = terms_ref[1, pl.ds(offset, span), :]
                grads = []
                for side in range(2):
                    lanes = slice(side * QUERY_BLOCK, (side + 1) * QUERY_BLOCK)
                    own = probs[:, lanes].astype(F32)
                    mixed = own * grad_probs[:, lanes]
                    grad_scores = mixed - own * jnp.sum(mixed, axis=0, keepdims=True)
                    rich[0][side] += jnp.sum(grad_scores * spread, axis=0, keepdims=True)
                    rich[1][side] += jnp.sum(grad_scores * order, axis=0, keepdims=True)
                    grad_raw = low(grad_scores * scale)
                    grads.append(grad_raw)
                    place = head_of(index, side)
                    turned_sum[place, pl.ds(row, QUERY_BLOCK)] = dot_nn(turned_ref[place, keys], grad_raw)
                key_sum[keys, columns] += dot_nn(jnp.concatenate(grads, axis=1), queries)
            for which in range(2):
                for side in range(2):
                    rich_out[which, pl.ds(2 * index + side, 1), :] = rich[which][side]
            return carry

        lax.fori_loop(0, heads // 2, attend_back, 0)
        for _, own in row_parts(rows):
            grad_query = low(turned_sum[:, own].T)
            grad_key = low(key_sum[own, :])
            grad_value = low(value_sum[own, :])
            right_ref[0, own, :] = grad_query
            right_ref[1, own, :] = grad_key
            right_ref[2, own, :] = grad_value
            sum_ref[own, :] = (
                dot_nt(grad_query, w_ref[0]) + dot_nt(grad_key, w_ref[1]) + dot_nt(grad_value, w_ref[2])
            )
        copies.leave(right_ref, right_any)
        norm_back(out_ref, grad_ref, mid_ref, gain_ref[0:1, :], sum_ref, gain_out, shift_out, 0)
        copies.finish()


def layer_two(length, mid, cotangent, doc, coords, rich, gain, shift, bias, weights, up, down, left, normed, active):
    rows, width = mid.shape
    hidden = up.shape[1]
    heads = rich.shape[1]
    full = whole((rows, width))
    _, band = attend_windows(rows)
    flat, wide = ((rows, width), BF16), ((rows, hidden), BF16)
    sent = [((2, rows, width), BF16), ((4, rows, width), BF16), flat, wide, wide]
    exact = ((rows, width), F32)
    held = [
        flat, flat, flat, ((heads // 2, band, 2 * QUERY_BLOCK), BF16), ((2, band, QUERY_BLOCK), F32),
        ((band, QUERY_BLOCK), F32), wide, exact, exact, exact, exact, exact, ((width, rows), BF16), ((width, rows), F32),
    ]
    return kernel_call(
        layer_two_body,
        (1,),
        [
            full, part_of((rows, width), doc, 0), part_of((1, rows), doc, 1), pl.BlockSpec(memory_space=pltpu.SMEM),
            whole((2, width)), whole((2, width)), whole((1, hidden)),
        ]
        + [ANYWHERE] * 6,
        [
            (*flat, full),
            (*flat, full),
            ((4, width), F32, whole((4, width))),
            ((1, hidden), F32, whole((1, hidden))),
            ((2, width), F32, whole((2, width))),
            ((2, width), F32, whole((2, width))),
            ((2, heads, QUERY_BLOCK), F32, whole((2, heads, QUERY_BLOCK))),
        ]
        + [(left.shape, BF16, ANYWHERE)]
        + [(*what, ANYWHERE) for what in sent[1:]],
        [pltpu.VMEM(*what) for what in sent]
        + [pltpu.VMEM(v.shape, BF16) for v in (weights, up, down)]
        + [pltpu.VMEM(*what) for what in held]
        + [pltpu.SemaphoreType.DMA((11,))],
        16 * rows * width * width + 8 * rows * width * hidden + 12 * band * QUERY_BLOCK * width,
        20 * rows * width + 8 * width * width + 4 * (rows + width) * hidden,
        "layer_two",
        {11: 7, 12: 9, 13: 10},
    )(length, mid, cotangent, coords, rich, gain, shift, bias, weights, up, down, left, normed, active)


def weight_body(count, adds, picks_ref, *refs):
    lefts, rights, outs = refs[:count], refs[count : -2 - adds], refs[-2:]
    step = pl.program_id(0)

    def write(right_refs):
        total = None
        for left_ref, right_ref in zip(lefts, right_refs):
            left, right = (v[...].reshape(v.shape[-2:]) for v in (left_ref, right_ref))
            here = dot_tn(left, right)
            total = here if total is None else total + here
        for at in range(2):

            @pl.when(step == at)
            def _():
                outs[at][...] = low(total + refs[-3][...].astype(F32) if adds and at == 0 else total)

    if len(rights) == count:
        write(rights)
        return
    for which in range(2):

        @pl.when(picks_ref[0] == which)
        def _():
            write(rights[which * count : (which + 1) * count])


def weight_quarters(picks, lefts, rights, rights_one, arrived, name, token=None):
    count = len(lefts)
    specs, operands = [], []
    for array, shape, place in lefts + rights + (rights_one or []):
        operands.append(array)
        specs.append(pl.BlockSpec(shape, lambda j, chosen, place=place: place(chosen[0], chosen[1 + j])))
    width, rows = rights[0][1][-1], lefts[0][1][-2]
    quarter = (width, width)
    if arrived is not None:
        operands.append(arrived)
        specs.append(whole(quarter))
    return kernel_call(
        functools.partial(weight_body, count, int(arrived is not None)),
        (2,),
        specs,
        [(quarter, BF16, whole(quarter))] * 2,
        [],
        4 * width * width * count * rows,
        8 * width * width + 8 * count * rows * width,
        name,
        None,
        token,
    )(picks, *operands)


def place_body(count, places_ref, *refs):
    out_ref, copy_ref = refs[-2:]
    for at, piece in enumerate(refs[:count]):

        @pl.when(pl.program_id(0) == at)
        def _():
            out_ref[...] = piece[...].astype(F32)

    @pl.when(pl.program_id(0) == 0)
    def _():
        copy_ref[...] = refs[0][...]


def placed(places, first, pieces, shape, columns, into, name, token):
    width = pieces[0].shape[0]

    def index(i, where):
        return (0, where[first + i]) if columns else (where[first + i], 0)

    more = [] if into is None else [into]
    quarter = whole((width, width))
    return kernel_call(
        functools.partial(place_body, len(pieces)),
        (len(pieces),),
        [quarter] * len(pieces) + [ANYWHERE] * len(more),
        [(shape, F32, pl.BlockSpec((width, width), index)), ((width, width), BF16, quarter)],
        [],
        0,
        6 * len(pieces) * width * width,
        name,
        {1 + len(pieces): 0} if more else {},
        token,
    )(places, *pieces, *more)


def pack_body(docs, flag_ref, lengths_ref, *refs):
    sides = {1: refs[: 4 * docs], 0: refs[4 * docs : 8 * docs]}
    rich_refs, out_ref = refs[8 * docs : 9 * docs], refs[9 * docs]
    width = out_ref.shape[1]

    def spread(values, base):
        sums = jnp.sum(values, axis=1, keepdims=True)
        shape = (values.shape[0], width)
        lane = lax.broadcasted_iota(jnp.int32, shape, 1)
        row = lax.broadcasted_iota(jnp.int32, shape, 0)
        return jnp.sum(jnp.where(lane == base + row, sums, 0.0), axis=0, keepdims=True)

    for which, side in sides.items():

        @pl.when(flag_ref[0] == which)
        def _():
            bias, gain, shift, stat = (sum(side[4 * d + i][...] for d in range(docs)) for i in range(4))
            for at in range(0, bias.shape[1], width):
                out_ref[at // width : at // width + 1, :] = bias[:, at : at + width]
            base = bias.shape[1] // width
            out_ref[base : base + 2, :] = gain
            out_ref[base + 2 : base + 4, :] = shift
            scalars = spread(stat, 0 if which else stat.shape[0])
            if not which:
                heads = rich_refs[0].shape[1]
                for term in range(2):
                    total = sum(ref[term] for ref in rich_refs)
                    scalars += spread(total, 2 * stat.shape[0] + term * heads)
                count = lengths_ref[0]
                for d in range(1, docs):
                    count += lengths_ref[d]
                lane = lax.broadcasted_iota(jnp.int32, (1, width), 1)
                scalars += jnp.where(lane == 2 * (stat.shape[0] + heads), count.astype(F32), 0.0)
            out_ref[base + 4 : base + 5, :] = scalars
            out_ref[base + 5 :, :] = jnp.zeros((out_ref.shape[0] - base - 5, width), F32)


def packed_row(flag, lengths, one, two, rich, token=None):
    docs = len(one)
    width = one[0][1].shape[1]
    operands = [v for side in (one, two) for parts in side for v in parts] + list(rich)
    rows = -(-(one[0][0].shape[1] // width + 5) // 8) * 8
    return kernel_call(
        functools.partial(pack_body, docs),
        (1,),
        [pl.BlockSpec(memory_space=pltpu.SMEM)] + [whole(v.shape) for v in operands],
        [((rows, width), F32, whole((rows, width)))],
        [],
        0,
        4 * sum(v.size for v in operands),
        "packed_row",
        None,
        token,
    )(flag, lengths, *operands)


def rows_body(docs, flag_ref, *refs):
    out_ref = refs[2 * docs]
    for doc in range(docs):
        for which in range(2):

            @pl.when((flag_ref[0] == which) & (pl.program_id(0) == doc))
            def _():
                out_ref[...] = refs[(1 - which) * docs + doc][...]


def section_rows(flag, one, two):
    docs = len(one)
    rows, width = one[0].shape
    return kernel_call(
        functools.partial(rows_body, docs),
        (docs,),
        [whole((rows, width))] * (2 * docs),
        [((docs * rows, width), one[0].dtype, pl.BlockSpec((rows, width), lambda i, *_: (i, 0)))],
        [],
        0,
        4 * docs * rows * width,
        "section_rows",
    )(flag, *one, *two)


def sum_body(flag_ref, left_ref, right_ref, out_ref):
    out_ref[...] = left_ref[...] + right_ref[...]


def summed(flag, left, right, token):
    return kernel_call(
        sum_body,
        (1,),
        [whole(left.shape)] * 2,
        [(left.shape, left.dtype, whole(left.shape))],
        [],
        0,
        12 * left.size,
        "small_sum",
        None,
        token,
    )(flag, left, right)


STEPS = (
    "d", "d", "D", "back", "pack", "u", "q", "D", "u", "U", "s", "D",
    "s", "S", "U", "D", "U", "D", "S", "rows", "S", "U", "S", "U",
    "S", "q", "ad", "q", "bu", "q", "ns", "fs", "ou", "os",
)


def passed_along(block, axis, distance):
    devices = range(lax.axis_size(axis))
    route = [(i - distance, i) for i in devices if i - distance in devices]
    return lax.ppermute(block, axis, route)


def after(value, token):
    return lax.optimization_barrier((value, token))[0]


def core_swap(block):
    return lax.ppermute(block, "core", [(0, 1), (1, 0)])


class Ordered:
    def __init__(self):
        self.token = None

    def read(self, *values):
        if self.token is None:
            return values if len(values) > 1 else values[0]
        values = lax.optimization_barrier((*values, self.token))[:-1]
        return values if len(values) > 1 else values[0]

    def gave(self, value):
        self.token = value
        return value


def rounded_sum(*blocks):
    return low(sum(block.astype(F32) for block in blocks))


def chips_sum(order, sent, kept):
    across_x = [(0, 1), (1, 0)]
    neighbours = [(0, 1), (1, 0), (2, 3), (3, 2)]
    partners = [(1, 2), (2, 1), (0, 3), (3, 0)]
    z = lax.axis_index("z")
    middle = (z == 1) | (z == 2)
    half = sent.shape[0] // 2
    arrived = lax.ppermute(sent, "x", across_x)
    yield
    parts = (*kept, order.read(arrived))

    def half_of(start):
        return rounded_sum(*(lax.dynamic_slice_in_dim(part, start, half, 0) for part in parts))

    other = half_of(jnp.where(middle, half, 0))
    arrived = lax.ppermute(other, "z", neighbours)
    mine = order.gave(half_of(jnp.where(middle, 0, half)))
    yield
    mine = order.gave(rounded_sum(mine, order.read(arrived)))
    arrived = lax.ppermute(mine, "z", partners)
    yield
    mine = order.gave(rounded_sum(mine, order.read(arrived)))
    arrived = lax.ppermute(mine, "z", neighbours)
    yield
    other = order.read(arrived)
    total = jnp.concatenate([jnp.where(middle, mine, other), jnp.where(middle, other, mine)], axis=0)
    order.gave(total)
    yield total, core_swap(total), lax.ppermute(total, "x", across_x)


def small_sum(flag, block, totals, axes):
    for axis in axes:
        step = 1
        while step < lax.axis_size(axis):
            route = [(i, i ^ step) for i in range(lax.axis_size(axis))]
            arrived = lax.ppermute(block, axis, route)
            yield
            block, totals["token"] = summed(flag, block, arrived, totals["token"])
            step *= 2
    yield block


def local(
    boundary,
    lengths,
    neighbours,
    counts,
    coords,
    square_weights,
    up_weight,
    down_weight,
    up_bias,
    norm_gain,
    norm_bias,
    rich_terms,
):
    first = lax.axis_index("section") == 0
    core, across_x = lax.axis_index("core"), lax.axis_index("x")
    if lax.axis_size("z") != 4 or lax.axis_size("x") != 2:
        across_x = across_x * 0
    use_one = first.astype(jnp.int32)
    keep = jnp.stack([use_one, 2 * core + 1 - across_x, 2 * core + across_x])
    give = jnp.stack([use_one, 2 * (1 - core) + 1 - across_x, 2 * (1 - core) + across_x])
    places = jnp.stack([keep[2], 2 - 4 * core + keep[2], keep[1], 2 - 4 * core + keep[1]])
    documents = lengths.shape[0]
    docs = range(documents)
    rows = boundary.shape[1] // documents
    width = boundary.shape[2]
    hidden = up_weight.shape[2]
    heads = rich_terms.shape[1]
    source = boundary[0]
    squares = square_weights[0]
    up, down, bias = up_weight[0], down_weight[0], up_bias
    gains, shifts = norm_gain[0], norm_bias[0]
    near_t = neighbours.T
    counts_row, coords_row = counts[None], coords[None]
    about = [jnp.stack([lengths[doc], use_one]) for doc in docs]

    kept_one, arrived, stats_one = [], [], []
    sent = None
    for doc in docs:
        here = source if sent is None else after(source, sent)
        sent, stat, links, left, sigma, pull, resid, normed, active, slope = layer_one_forward(
            about[doc], here, doc, rows, near_t, counts_row, gains, shifts, bias, squares, up, down
        )
        kept_one.append((links, resid, slope, sigma, pull, left, normed, active))
        stats_one.append(stat)
        arrived.append(passed_along(sent, "section", 1))

    back, out_two, rich_two, kept, small_two = [], [], [], [], []
    for doc in docs:
        grad_mid, result, stat, bias_grad, gain_grad, shift_grad, rich, left, right, normed, active, pre = layer_two(
            about[doc], arrived[doc], source, doc, coords_row, rich_terms, gains, shifts, bias, squares, up, down,
            *kept_one[doc][5:]
        )
        out_two.append(result)
        kept.append([left, right, normed, active, pre])
        small_two.append((bias_grad, gain_grad, shift_grad, stat))
        rich_two.append(rich)
        back.append(passed_along(grad_mid, "section", -1))
        last_sent = grad_mid

    out_one, small_one = [], []

    def first_back(doc, grad_mid, token=None):
        links, resid, slope, sigma, pull = kept_one[doc][:5]
        grad_x, bias_grad, gain_grad, shift_grad, pre, right, *token = layer_one_backward(
            about[doc], grad_mid, source, doc, gains, counts_row, links, resid, slope, sigma, pull, squares, up, down,
            kept[doc][4], kept[doc][1], token,
        )
        out_one.append(grad_x)
        kept[doc][4], kept[doc][1] = pre, right
        small_one.append((bias_grad, gain_grad, shift_grad, stats_one[doc]))
        return grad_x, *token

    token = last_sent
    for doc in range(documents - 1):
        (token,) = first_back(doc, after(back[doc], token))
    if documents > 1:
        back[-1] = after(back[-1], token)

    quarter, stack = (rows, width), (1, rows, width)
    still, across = lambda one, q: (0, 0), lambda one, q: (0, q)
    own_rows = [functools.partial(lambda d, one, q: (d, 0), d) for d in docs]

    def left_of(one, q):
        return jnp.where(one == 1, (q + 1) // 2, q // 3), 0, 0

    def right_of(one, q):
        return jnp.where(one == 1, jnp.maximum(q - 1, 0), q), 0, 0

    def pairs_of(name):
        if name == "down":
            return (
                [(kept[d][3], quarter, across) for d in docs],
                [(source, quarter, own_rows[d]) for d in docs],
                [(back[d], quarter, still) for d in docs],
            )
        if name == "up":
            return (
                [(kept[d][2], quarter, still) for d in docs],
                [(kept[d][4], quarter, across) for d in docs],
                None,
            )
        return (
            [(kept[d][0], stack, left_of) for d in docs],
            [(kept[d][1], stack, right_of) for d in docs],
            None,
        )

    order = Ordered()
    custom = lax.axis_size("z") == 4 and lax.axis_size("x") == 2
    names = {"d": "down", "u": "up", "s": "square"}
    totals, given, made, pieces = {"token": jnp.zeros((8, 128), F32)}, {}, {}, {}

    def products(letter):
        name, pairs = names[letter], pairs_of(names[letter])
        *quarters, totals["token"] = weight_quarters(give, *pairs, None, name + "_give", totals["token"])
        given[letter] = [core_swap(v) for v in quarters]
        yield
        *made[letter], totals["token"] = weight_quarters(keep, *pairs, given[letter][0], name + "_keep", totals["token"])
        yield

    def flow(letter):
        sent, kept_own = made[letter]
        kept_other = given[letter][1]
        if custom:
            for value in chips_sum(order, sent, (kept_own, kept_other)):
                pieces[letter] = value
                yield
            return
        near, far = lax.psum(rounded_sum(kept_own, kept_other), ("z", "x")), lax.psum(sent, ("z", "x"))
        pieces[letter] = near, core_swap(near), far
        for _ in range(5):
            yield

    def place(letter, which):
        near, near_other, far = pieces[letter]
        first, blocks = {
            "a": (0, lambda: (near, near_other, far, core_swap(far))),
            "b": (0, lambda: (near, near_other, far)),
            "n": (0, lambda: (near, near_other)),
            "f": (2, lambda: (far,)),
            "o": (3, lambda: (core_swap(far),)),
        }[which]
        shape = (width, hidden) if letter == "u" else (hidden, width)
        blocks = [order.read(block) for block in blocks()]
        totals[letter], copy, totals["token"] = placed(
            places, first, blocks, shape, letter == "u", totals.get(letter), names[letter] + "_placed", totals["token"]
        )
        order.gave(copy)
        if which == "f":
            pieces[letter] = (near, near_other, copy)

    running = {letter: products(letter) for letter in names}
    running.update({letter.upper(): flow(letter) for letter in names})
    for step in STEPS:
        if step == "back":
            _, totals["token"] = first_back(documents - 1, back[-1], totals["token"])
        elif step == "pack":
            small, totals["token"] = packed_row(
                use_one[None], lengths, small_one, small_two, rich_two, totals["token"]
            )
            running["q"] = small_sum(use_one[None], small, totals, ("x", "core", "z"))
            next(running["q"])
        elif step == "rows":
            (boundary_out,) = section_rows(order.read(use_one[None]), out_one, out_two)
            order.gave(boundary_out)
        elif step[0] in "abnfo":
            place(step[1], step[0])
        elif step == "q":
            packed = next(running["q"])
        else:
            next(running[step])
    for packed in running["q"]:
        pass
    crossed = lax.ppermute(packed, "section", [(0, 1), (1, 0)])
    down_total, up_total, square_total = (totals[letter] for letter in names)

    at = hidden // width
    size = 9 + 2 * heads
    shared = packed[at + 4, :size] + crossed[at + 4, :size]
    rms = jnp.sqrt(shared[:8].reshape(2, 4) / (shared[8 + 2 * heads] * width))
    rich_total = shared[8 : 8 + 2 * heads].reshape(2, heads)
    return (
        boundary_out[None],
        square_total.reshape(1, 4, width, width),
        up_total.reshape(1, width, hidden),
        down_total[None],
        packed[:at].reshape(1, hidden),
        packed[at : at + 2][None],
        packed[at + 2 : at + 4][None],
        rich_total,
        rms,
    )


def solution(mesh):
    sections, dp = mesh.devices.shape
    split = Mesh(mesh.devices.reshape(sections, dp // 4, 2, 2), ("section", "z", "x", "core"))
    data = ("z", "x", "core")
    in_specs = (
        P("section", data, None),
        P(data),
        P(data, None),
        P(data),
        P(data),
        P("section", None, None, None),
        P("section", None, None),
        P("section", None, None),
        P("section", None),
        P("section", None, None),
        P("section", None, None),
        P(),
    )
    out_specs = (
        P("section", data, None),
        P("section", None, None, None),
        P("section", None, None),
        P("section", None, None),
        P("section", None),
        P("section", None, None),
        P("section", None, None),
        P(),
        P(),
    )
    return jax.shard_map(local, mesh=split, in_specs=in_specs, out_specs=out_specs, check_vma=False)
```

```python
import functools
import jax
import jax.numpy as jnp
from jax import lax
from jax.sharding import Mesh, PartitionSpec as P
from jax.experimental import pallas as pl
from jax.experimental.pallas import tpu as pltpu

RADIUS = 128
REACH = 64
QUERY_BLOCK = 128
EPSILON = 1e-05
NEG_FILL = -1e30
HIDDEN_TILE = 1024
SCALE = 1
GELU_C = 0.7978845608028654
F32, BF16 = jnp.float32, jnp.bfloat16
MIB = 1024 * 1024


def low(vector):
    return vector.astype(BF16)


def dot_nn(left, right):
    return jnp.dot(left, right, preferred_element_type=F32)


def dot_nt(left, right):
    return lax.dot_general(left, right, (((1,), (1,)), ((), ())), preferred_element_type=F32)


def dot_tn(left, right):
    return lax.dot_general(left, right, (((0,), (0,)), ((), ())), preferred_element_type=F32)


def normalized(vector):
    center = vector - jnp.mean(vector, axis=-1, keepdims=True)
    inverse = lax.rsqrt(jnp.mean(center * center, axis=-1, keepdims=True) + EPSILON)
    return center * inverse, inverse


def norm_backward(vector, gain_row, grad_normed):
    normed, inverse = normalized(vector)
    scaled = grad_normed * gain_row
    mean_scaled = jnp.mean(scaled, axis=-1, keepdims=True)
    mean_mixed = jnp.mean(scaled * normed, axis=-1, keepdims=True)
    grad_input = inverse * (scaled - mean_scaled - normed * mean_mixed)
    grad_gain = jnp.sum(grad_normed * normed, axis=0, keepdims=True)
    return grad_input, grad_gain, jnp.sum(grad_normed, axis=0, keepdims=True)


def live_sums(length, start, items):
    rows = items[0].shape[0]
    live = start + lax.broadcasted_iota(jnp.int32, (rows, 1), 0) < length
    return [jnp.sum(jnp.where(live, v * v, 0.0), axis=0, keepdims=True) for v in items]


def whole(shape):
    return pl.BlockSpec(shape, lambda *_: (0,) * len(shape))


def part_of(shape, doc, axis):
    place = tuple(doc if d == axis else 0 for d in range(len(shape)))
    return pl.BlockSpec(shape, lambda *_: place)


def column(row):
    return jnp.broadcast_to(row, (row.shape[1], row.shape[1])).T[:, 0:1]


def kernel_call(body, grid, in_specs, outs, scratch, flops, moved, name, aliases=None, token=None):
    taken, given = 1 + len(in_specs), len(outs)

    def with_token(*refs):
        rest = refs[taken + 1 :]
        body(*refs[:taken], *rest[:given], *rest[given + 1 :])

    if token is not None:
        in_specs = [*in_specs, pl.BlockSpec(memory_space=pl.ANY)]
        outs = [*outs, (token.shape, token.dtype, pl.BlockSpec(memory_space=pl.ANY))]
    call = pl.pallas_call(
        body if token is None else with_token,
        out_shape=[jax.ShapeDtypeStruct(shape, kind) for shape, kind, _ in outs],
        grid_spec=pltpu.PrefetchScalarGridSpec(
            num_scalar_prefetch=1,
            grid=grid,
            in_specs=in_specs,
            out_specs=[spec for _, _, spec in outs],
            scratch_shapes=scratch,
        ),
        compiler_params=pltpu.CompilerParams(
            dimension_semantics=("arbitrary",) * len(grid), vmem_limit_bytes=60 * MIB
        ),
        cost_estimate=pl.CostEstimate(flops=SCALE * int(flops), bytes_accessed=SCALE * int(moved), transcendentals=0),
        input_output_aliases=aliases or {},
        name=name,
    )
    return call if token is None else lambda *operands: call(*operands, token)


ANYWHERE = pl.BlockSpec(memory_space=pl.ANY)
PARTS = 2


def row_parts(rows):
    return [(at, pl.ds(at, rows // PARTS)) for at in range(0, rows, rows // PARTS)]


class Copies:
    def __init__(self, semaphores):
        self.semaphores, self.used, self.pending = semaphores, 0, []

    def start(self, source, target):
        copy = pltpu.make_async_copy(source, target, self.semaphores.at[self.used])
        self.used += 1
        copy.start()
        return copy

    def leave(self, source, target):
        self.pending.append(self.start(source, target))

    def finish(self):
        for copy in self.pending:
            copy.wait()


def add_rows(ref, rows, values):
    for at, value in zip(rows, values):
        ref[at : at + 1, :] += value


def feed_forward(
    resid_ref, gain, shift, up_ref, bias_ref, down_ref, normed_ref, active_ref, slope_ref, sum_ref, done=None
):
    rows, hidden = active_ref.shape
    for _, own in row_parts(rows):
        normed_ref[own, :] = low(normalized(resid_ref[own, :])[0] * gain + shift)
    sum_ref[...] = jnp.zeros_like(sum_ref)

    def tile_at(columns):
        parts = [own for _, own in row_parts(rows)]
        pres = [dot_nn(normed_ref[own, :], up_ref[:, columns]) + bias_ref[:, columns] for own in parts]
        for own, pre in zip(parts, pres):
            square = pre * pre
            curve = jnp.tanh(pre * (GELU_C + GELU_C * 0.044715 * square))
            half = 0.5 + 0.5 * curve
            active = low(pre * half)
            active_ref[own, columns] = active
            rise = pre * (GELU_C + 3.0 * GELU_C * 0.044715 * square)
            slope_ref[own, columns] = low(half + rise * (half - half * half) * 2.0)
            sum_ref[own, :] += dot_nn(active, down_ref[columns, :])

    def tile(index, carry):
        tile_at(pl.ds(pl.multiple_of(index * HIDDEN_TILE, HIDDEN_TILE), HIDDEN_TILE))
        return carry

    if done is None:
        lax.fori_loop(0, hidden // HIDDEN_TILE, tile, 0)
        return
    for start in range(0, hidden, HIDDEN_TILE):
        columns = pl.ds(start, HIDDEN_TILE)
        tile_at(columns)
        done(columns)


def feed_backward_tile(columns, grad_ref, slope_ref, up_ref, down_ref, pre_ref, bias_ref, sum_ref):
    total = None
    for _, own in row_parts(grad_ref.shape[0]):
        grad_active = dot_nt(grad_ref[own, :], down_ref[columns, :])
        grad_pre = low(slope_ref[own, columns].astype(F32) * grad_active)
        pre_ref[own, columns] = grad_pre
        here = jnp.sum(grad_pre.astype(F32), axis=0, keepdims=True)
        total = here if total is None else total + here
        sum_ref[own, :] += dot_nt(grad_pre, up_ref[:, columns])
    bias_ref[:, columns] = total


def norm_back(out_ref, grad_ref, vector_ref, gain, sum_ref, gain_ref, shift_ref, at):
    gain_ref[at : at + 1, :] = jnp.zeros_like(gain)
    shift_ref[at : at + 1, :] = jnp.zeros_like(gain)
    for _, own in row_parts(out_ref.shape[0]):
        grad_input, grad_gain, grad_shift = norm_backward(vector_ref[own, :].astype(F32), gain, sum_ref[own, :])
        out_ref[own, :] = (grad_ref[own, :].astype(F32) + grad_input).astype(out_ref.dtype)
        gain_ref[at : at + 1, :] += grad_gain
        shift_ref[at : at + 1, :] += grad_shift


def graph_windows(rows):
    span = QUERY_BLOCK + 2 * REACH
    return [
        (start, min(max(start - REACH, 0), rows - span), span)
        for start in range(0, rows, QUERY_BLOCK)
    ]


def layer_one_forward_body(
    length_ref, x_ref, near_ref_t, counts_ref, gain_ref, shift_ref, bias_ref, w_any, up_any, down_any,
    mid_ref, stat_ref, link_ref, left_any, sigma_any, pull_any, resid_any, normed_any, active_any, slope_any,
    w_ref, up_ref, down_ref, left_ref, sigma_ref, pull_ref, resid_ref, normed_ref, active_ref, slope_ref, sum_ref,
    semaphores,
):
    @pl.when(length_ref[1] == 1)
    def _():
        rows, width = x_ref.shape
        length = length_ref[0]
        copies = Copies(semaphores)
        w_copies = [copies.start(w_any.at[i], w_ref.at[i]) for i in range(4)]
        up_copy, down_copy = copies.start(up_any, up_ref), copies.start(down_any, down_ref)
        graph_normed, mean_ref, mixed_ref = (left_ref.at[i] for i in range(3))
        stat_ref[...] = jnp.zeros_like(stat_ref)
        for _, own in row_parts(rows):
            graph_normed[own, :] = low(
                normalized(x_ref[own, :].astype(F32))[0] * gain_ref[0:1, :] + shift_ref[0:1, :]
            )
        slots = near_ref_t.shape[0]
        slot = lax.broadcasted_iota(jnp.int32, (slots, QUERY_BLOCK), 0)
        for row, start, span in graph_windows(rows):
            own = pl.ds(row, QUERY_BLOCK)
            counts = counts_ref[:, own]
            index = jnp.where(slot < counts, near_ref_t[:, own], -1)
            place = start + lax.broadcasted_iota(jnp.int32, (span, QUERY_BLOCK), 0)
            links = jnp.zeros((span, QUERY_BLOCK), F32)
            for s in range(slots):
                links += jnp.where(index[s : s + 1, :] == place, 1.0, 0.0)
            link_ref[:, own] = low(links)
            total = dot_nn(low(links.T), graph_normed[pl.ds(start, span), :])
            mean_ref[own, :] = low(total / column(counts.astype(F32)))
        for copy in w_copies:
            copy.wait()
        for at, own in row_parts(rows):
            pre = dot_nn(graph_normed[own, :], w_ref[0]) + dot_nn(mean_ref[own, :], w_ref[1])
            sigma = jax.nn.sigmoid(dot_nn(mean_ref[own, :], w_ref[2]))
            mixed = pre * sigma
            sigma_ref[own, :] = low(sigma)
            pull_ref[own, :] = low(mixed - mixed * sigma)
            mixed_ref[own, :] = low(mixed)
            branch = dot_nn(low(mixed), w_ref[3])
            resid = x_ref[own, :].astype(F32) + branch
            resid_ref[own, :] = resid
            add_rows(stat_ref, (0, 1), live_sums(length, at, (branch, resid)))
        copies.leave(left_ref, left_any)
        copies.leave(sigma_ref, sigma_any)
        copies.leave(pull_ref, pull_any)
        copies.leave(resid_ref, resid_any)
        up_copy.wait()
        down_copy.wait()

        def done(columns):
            copies.leave(active_ref.at[:, columns], active_any.at[:, columns])
            copies.leave(slope_ref.at[:, columns], slope_any.at[:, columns])

        feed_forward(
            resid_ref, gain_ref[1:2, :], shift_ref[1:2, :], up_ref, bias_ref, down_ref,
            normed_ref, active_ref, slope_ref, sum_ref, done,
        )
        copies.leave(normed_ref, normed_any)
        for at, own in row_parts(rows):
            branch = sum_ref[own, :]
            result = resid_ref[own, :] + branch
            mid_ref[own, :] = low(result)
            add_rows(stat_ref, (2, 3), live_sums(length, at, (branch, result)))
        copies.finish()


def layer_one_forward(length, x, doc, rows, near_t, counts, gain, shift, bias, weights, up, down):
    width, hidden = up.shape
    slots = near_t.shape[0]
    span = QUERY_BLOCK + 2 * REACH
    flat, wide = ((rows, width), BF16), ((rows, hidden), BF16)
    kept = [((3, rows, width), BF16), flat, flat, ((rows, width), F32), flat, wide, wide]
    return kernel_call(
        layer_one_forward_body,
        (1,),
        [
            part_of((rows, width), doc, 0), part_of((slots, rows), doc, 1), part_of((1, rows), doc, 1),
            whole((2, width)), whole((2, width)), whole((1, hidden)), ANYWHERE, ANYWHERE, ANYWHERE,
        ],
        [
            ((rows, width), BF16, whole((rows, width))),
            ((4, width), F32, whole((4, width))),
            ((span, rows), BF16, whole((span, rows))),
        ]
        + [(*what, ANYWHERE) for what in kept],
        [pltpu.VMEM(v.shape, BF16) for v in (weights, up, down)]
        + [pltpu.VMEM(*what) for what in kept]
        + [pltpu.VMEM((rows, width), F32), pltpu.SemaphoreType.DMA((11 + 2 * (hidden // HIDDEN_TILE),))],
        8 * rows * width * width + 4 * rows * width * hidden,
        16 * rows * width + 8 * width * width + 4 * (rows + width) * hidden,
        "layer_one_forward",
    )(length, x, near_t, counts, gain, shift, bias, weights, up, down)


def layer_one_backward_body(
    length_ref, grad_ref, x_ref, gain_ref, counts_ref, link_ref,
    resid_any, slope_any, sigma_any, pull_any, w_any, up_any, down_any, pre_given, right_given,
    out_ref, bias_out, gain_out, shift_out, pre_any, right_any,
    resid_ref, slope_ref, sigma_ref, pull_ref, w_ref, up_ref, down_ref,
    pre_ref, right_ref, grad_resid, mean_ref, sum_ref,
    semaphores,
):
    @pl.when(length_ref[1] == 1)
    def _():
        rows, width = x_ref.shape
        hidden = slope_ref.shape[1]
        copies = Copies(semaphores)
        tiles = [pl.ds(at, HIDDEN_TILE) for at in range(0, hidden, HIDDEN_TILE)]
        arriving = [
            [
                copies.start(down_any.at[columns, :], down_ref.at[columns, :]),
                copies.start(slope_any.at[:, columns], slope_ref.at[:, columns]),
                copies.start(up_any.at[:, columns], up_ref.at[:, columns]),
            ]
            for columns in tiles
        ]
        resid_copy = copies.start(resid_any, resid_ref)
        w_copies = [copies.start(w_any.at[i], w_ref.at[i]) for i in range(4)]
        gate_copies = [copies.start(sigma_any, sigma_ref), copies.start(pull_any, pull_ref)]
        counts_column = column(counts_ref[...].astype(F32))
        sum_ref[...] = jnp.zeros_like(sum_ref)
        for columns, parts in zip(tiles, arriving):
            for copy in parts:
                copy.wait()
            feed_backward_tile(columns, grad_ref, slope_ref, up_ref, down_ref, pre_ref, bias_out, sum_ref)
        copies.leave(pre_ref, pre_any)
        resid_copy.wait()
        norm_back(grad_resid, grad_ref, resid_ref, gain_ref[1:2, :], sum_ref, gain_out, shift_out, 1)
        for copy in w_copies + gate_copies:
            copy.wait()
        for at, own in row_parts(rows):
            grad_low = low(grad_resid[own, :])
            right_ref[2, own, :] = grad_low
            grad_mixed = dot_nt(grad_low, w_ref[3])
            grad_pre = low(sigma_ref[own, :].astype(F32) * grad_mixed)
            grad_gate = low(pull_ref[own, :].astype(F32) * grad_mixed)
            right_ref[0, own, :] = grad_pre
            right_ref[1, own, :] = grad_gate
            sum_ref[own, :] = dot_nt(grad_pre, w_ref[0])
            grad_mean = dot_nt(grad_pre, w_ref[1]) + dot_nt(grad_gate, w_ref[2])
            mean_ref[own, :] = low(grad_mean / counts_column[at : at + rows // PARTS, :])
        copies.leave(right_ref, right_any.at[0:3])
        for row, start, span in graph_windows(rows):
            own = pl.ds(row, QUERY_BLOCK)
            sum_ref[pl.ds(start, span), :] += dot_nn(link_ref[:, own], mean_ref[own, :])
        norm_back(out_ref, grad_resid, x_ref, gain_ref[0:1, :], sum_ref, gain_out, shift_out, 0)
        copies.finish()


def layer_one_backward(length, grad, x, doc, gain, counts, links, resid, slope, sigma, pull, weights, up, down, pre, right, token=None):
    rows, width = grad.shape
    hidden = slope.shape[1]
    full = whole((rows, width))
    sent = [((rows, hidden), BF16), ((3, rows, width), BF16)]
    return kernel_call(
        layer_one_backward_body,
        (1,),
        [
            full, part_of((rows, width), doc, 0), whole((2, width)), part_of((1, rows), doc, 1), whole(links.shape),
        ]
        + [ANYWHERE] * 9,
        [
            ((rows, width), BF16, full),
            ((1, hidden), F32, whole((1, hidden))),
            ((2, width), F32, whole((2, width))),
            ((2, width), F32, whole((2, width))),
        ]
        + [(pre.shape, BF16, ANYWHERE), (right.shape, BF16, ANYWHERE)],
        [pltpu.VMEM(v.shape, v.dtype) for v in (resid, slope, sigma, pull, weights, up, down)]
        + [pltpu.VMEM(*what) for what in sent]
        + [
            pltpu.VMEM((rows, width), F32),
            pltpu.VMEM((rows, width), BF16),
            pltpu.VMEM((rows, width), F32),
            pltpu.SemaphoreType.DMA((3 * (hidden // HIDDEN_TILE) + 9,)),
        ],
        8 * rows * width * width + 4 * rows * width * hidden,
        18 * rows * width + 8 * width * width + 4 * (rows + width) * hidden,
        "layer_one_backward",
        {13: 4, 14: 5},
        token,
    )(length, grad, x, gain, counts, links, resid, slope, sigma, pull, weights, up, down, pre, right)


def attend_windows(rows):
    windows, offset = [], 0
    for row in range(0, rows, QUERY_BLOCK):
        start = max(row - RADIUS, 0)
        span = min(row + QUERY_BLOCK + RADIUS, rows) - start
        windows.append((row, start, span, offset))
        offset += span
    return windows, offset


def two_heads(block, lane):
    zero = jnp.zeros_like(block)
    return jnp.concatenate([jnp.where(lane, block, zero), jnp.where(lane, zero, block)], axis=0)


def layer_two_body(
    length_ref, mid_ref, cotangent_ref, coords_ref, rich_ref, gain_ref, shift_ref, bias_ref, w_any, up_any, down_any,
    left_given, normed_given, active_given,
    out_ref, result_ref, stat_ref, bias_out, gain_out, shift_out, rich_out,
    left_any, right_any, normed_any, active_any, pre_any,
    left_ref, right_ref, normed_ref, active_ref, pre_ref,
    w_ref, up_ref, down_ref, query_ref, key_ref, value_ref, probs_ref, terms_ref, mask_ref, slope_ref, resid_ref,
    grad_ref, sum_ref, key_sum, value_sum, turned_ref, turned_sum, semaphores,
):
    @pl.when(length_ref[1] == 0)
    def _():
        rows, width = mid_ref.shape
        hidden = active_ref.shape[1]
        heads = rich_ref.shape[1]
        head_width = width // heads
        scale = head_width ** (-0.5)
        length = length_ref[0]
        windows, _ = attend_windows(rows)
        copies = Copies(semaphores)
        w_copies = [copies.start(w_any.at[i], w_ref.at[i]) for i in range(4)]
        attend_normed, context_ref = left_ref.at[0], left_ref.at[1]
        stat_ref[...] = jnp.zeros_like(stat_ref)

        for row, start, span, offset in windows:
            i = row + lax.broadcasted_iota(jnp.int32, (span, QUERY_BLOCK), 1)
            j = start + lax.broadcasted_iota(jnp.int32, (span, QUERY_BLOCK), 0)
            allowed = (jnp.abs(i - j) <= RADIUS) & ((j < length) | (i == j))
            mask_ref[pl.ds(offset, span), :] = jnp.where(allowed, 0.0, NEG_FILL)
            across = coords_ref[:, pl.ds(row, QUERY_BLOCK)]
            along = [
                jnp.broadcast_to(coords_ref[:, pl.ds(at, QUERY_BLOCK)], (QUERY_BLOCK, QUERY_BLOCK)).T
                for at in range(start, start + span, QUERY_BLOCK)
            ]
            gap = across - jnp.concatenate(along, axis=0)
            terms_ref[0, pl.ds(offset, span), :] = jnp.log(1.0 + jnp.abs(gap))
            terms_ref[1, pl.ds(offset, span), :] = jnp.tanh(-gap)
        for copy in w_copies:
            copy.wait()
        up_copy, down_copy = copies.start(up_any, up_ref), copies.start(down_any, down_ref)
        for _, own in row_parts(rows):
            normed = low(normalized(mid_ref[own, :].astype(F32))[0] * gain_ref[0:1, :] + shift_ref[0:1, :])
            attend_normed[own, :] = normed
            query_ref[own, :] = low(dot_nn(normed, w_ref[0]))
            key_ref[own, :] = low(dot_nn(normed, w_ref[1]))
            value = dot_nn(normed, w_ref[2])
            value_ref[own, :] = low(value)
            turned_ref[:, own] = low(value.T)
        lane = lax.broadcasted_iota(jnp.int32, (QUERY_BLOCK, 2 * head_width), 1) < head_width

        def pair_of(index):
            return pl.ds(pl.multiple_of(index * 2 * head_width, 2 * head_width), 2 * head_width)

        def head_of(index, side):
            return pl.ds(pl.multiple_of((2 * index + side) * head_width, head_width), head_width)

        def attend(index, carry):
            columns = pair_of(index)
            for row, start, span, offset in windows:
                queries = two_heads(query_ref[pl.ds(row, QUERY_BLOCK), columns], lane)
                raw = dot_nt(key_ref[pl.ds(start, span), columns], queries)
                spread = terms_ref[0, pl.ds(offset, span), :]
                order = terms_ref[1, pl.ds(offset, span), :]
                mask = mask_ref[pl.ds(offset, span), :]
                for side in range(2):
                    head = 2 * index + side
                    own = raw[:, side * QUERY_BLOCK : (side + 1) * QUERY_BLOCK]
                    scores = own * scale + (spread * rich_ref[0, head] + order * rich_ref[1, head]) + mask
                    weights = jnp.exp(scores - jnp.max(scores, axis=0, keepdims=True))
                    probs = low(weights * (1.0 / jnp.sum(weights, axis=0, keepdims=True)))
                    probs_ref[index, pl.ds(offset, span), pl.ds(side * QUERY_BLOCK, QUERY_BLOCK)] = probs
                    place = head_of(index, side)
                    turned_sum[place, pl.ds(row, QUERY_BLOCK)] = dot_nn(
                        turned_ref[place, pl.ds(start, span)], probs
                    )
            return carry

        lax.fori_loop(0, heads // 2, attend, 0, unroll=2)
        for at, own in row_parts(rows):
            context = low(turned_sum[:, own].T)
            context_ref[own, :] = context
            branch = dot_nn(context, w_ref[3])
            resid = mid_ref[own, :].astype(F32) + branch
            resid_ref[own, :] = resid
            add_rows(stat_ref, (0, 1), live_sums(length, at, (branch, resid)))
        copies.leave(left_ref, left_any.at[0:2])

        up_copy.wait()
        down_copy.wait()
        feed_forward(
            resid_ref, gain_ref[1:2, :], shift_ref[1:2, :], up_ref, bias_ref, down_ref,
            normed_ref, active_ref, slope_ref, sum_ref,
        )
        copies.leave(normed_ref, normed_any)
        copies.leave(active_ref, active_any)
        for at, own in row_parts(rows):
            branch = sum_ref[own, :]
            result = resid_ref[own, :] + branch
            result_ref[own, :] = low(result)
            add_rows(stat_ref, (2, 3), live_sums(length, at, (branch, result)))
        sum_ref[...] = jnp.zeros_like(sum_ref)

        def tile(index, carry):
            columns = pl.ds(pl.multiple_of(index * HIDDEN_TILE, HIDDEN_TILE), HIDDEN_TILE)
            feed_backward_tile(columns, cotangent_ref, slope_ref, up_ref, down_ref, pre_ref, bias_out, sum_ref)
            return carry

        lax.fori_loop(0, hidden // HIDDEN_TILE, tile, 0)
        copies.leave(pre_ref, pre_any)
        norm_back(grad_ref, cotangent_ref, resid_ref, gain_ref[1:2, :], sum_ref, gain_out, shift_out, 1)

        grad_context = right_ref.at[0]
        for _, own in row_parts(rows):
            grad_low = low(grad_ref[own, :])
            right_ref[3, own, :] = grad_low
            grad_context[own, :] = low(dot_nt(grad_low, w_ref[3]))
            turned_ref[:, own] = low(key_ref[own, :].astype(F32).T)
        key_sum[...] = jnp.zeros_like(key_sum)
        value_sum[...] = jnp.zeros_like(value_sum)

        def attend_back(index, carry):
            columns = pair_of(index)
            rich = [[0.0, 0.0], [0.0, 0.0]]
            for row, start, span, offset in windows:
                keys = pl.ds(start, span)
                context = two_heads(grad_context[pl.ds(row, QUERY_BLOCK), columns], lane)
                queries = two_heads(query_ref[pl.ds(row, QUERY_BLOCK), columns], lane)
                grad_probs = dot_nt(value_ref[keys, columns], context)
                probs = probs_ref[index, pl.ds(offset, span), :]
                value_sum[keys, columns] += dot_nn(probs, context)
                spread = terms_ref[0, pl.ds(offset, span), :]
                order = terms_ref[1, pl.ds(offset, span), :]
                grads = []
                for side in range(2):
                    lanes = slice(side * QUERY_BLOCK, (side + 1) * QUERY_BLOCK)
                    own = probs[:, lanes].astype(F32)
                    mixed = own * grad_probs[:, lanes]
                    grad_scores = mixed - own * jnp.sum(mixed, axis=0, keepdims=True)
                    rich[0][side] += jnp.sum(grad_scores * spread, axis=0, keepdims=True)
                    rich[1][side] += jnp.sum(grad_scores * order, axis=0, keepdims=True)
                    grad_raw = low(grad_scores * scale)
                    grads.append(grad_raw)
                    place = head_of(index, side)
                    turned_sum[place, pl.ds(row, QUERY_BLOCK)] = dot_nn(turned_ref[place, keys], grad_raw)
                key_sum[keys, columns] += dot_nn(jnp.concatenate(grads, axis=1), queries)
            for which in range(2):
                for side in range(2):
                    rich_out[which, pl.ds(2 * index + side, 1), :] = rich[which][side]
            return carry

        lax.fori_loop(0, heads // 2, attend_back, 0)
        for _, own in row_parts(rows):
            grad_query = low(turned_sum[:, own].T)
            grad_key = low(key_sum[own, :])
            grad_value = low(value_sum[own, :])
            right_ref[0, own, :] = grad_query
            right_ref[1, own, :] = grad_key
            right_ref[2, own, :] = grad_value
            sum_ref[own, :] = (
                dot_nt(grad_query, w_ref[0]) + dot_nt(grad_key, w_ref[1]) + dot_nt(grad_value, w_ref[2])
            )
        copies.leave(right_ref, right_any)
        norm_back(out_ref, grad_ref, mid_ref, gain_ref[0:1, :], sum_ref, gain_out, shift_out, 0)
        copies.finish()


def layer_two(length, mid, cotangent, doc, coords, rich, gain, shift, bias, weights, up, down, left, normed, active):
    rows, width = mid.shape
    hidden = up.shape[1]
    heads = rich.shape[1]
    full = whole((rows, width))
    _, band = attend_windows(rows)
    flat, wide = ((rows, width), BF16), ((rows, hidden), BF16)
    sent = [((2, rows, width), BF16), ((4, rows, width), BF16), flat, wide, wide]
    exact = ((rows, width), F32)
    held = [
        flat, flat, flat, ((heads // 2, band, 2 * QUERY_BLOCK), BF16), ((2, band, QUERY_BLOCK), F32),
        ((band, QUERY_BLOCK), F32), wide, exact, exact, exact, exact, exact, ((width, rows), BF16), ((width, rows), F32),
    ]
    return kernel_call(
        layer_two_body,
        (1,),
        [
            full, part_of((rows, width), doc, 0), part_of((1, rows), doc, 1), pl.BlockSpec(memory_space=pltpu.SMEM),
            whole((2, width)), whole((2, width)), whole((1, hidden)),
        ]
        + [ANYWHERE] * 6,
        [
            (*flat, full),
            (*flat, full),
            ((4, width), F32, whole((4, width))),
            ((1, hidden), F32, whole((1, hidden))),
            ((2, width), F32, whole((2, width))),
            ((2, width), F32, whole((2, width))),
            ((2, heads, QUERY_BLOCK), F32, whole((2, heads, QUERY_BLOCK))),
        ]
        + [(left.shape, BF16, ANYWHERE)]
        + [(*what, ANYWHERE) for what in sent[1:]],
        [pltpu.VMEM(*what) for what in sent]
        + [pltpu.VMEM(v.shape, BF16) for v in (weights, up, down)]
        + [pltpu.VMEM(*what) for what in held]
        + [pltpu.SemaphoreType.DMA((11,))],
        16 * rows * width * width + 8 * rows * width * hidden + 12 * band * QUERY_BLOCK * width,
        20 * rows * width + 8 * width * width + 4 * (rows + width) * hidden,
        "layer_two",
        {11: 7, 12: 9, 13: 10},
    )(length, mid, cotangent, coords, rich, gain, shift, bias, weights, up, down, left, normed, active)


def weight_body(count, adds, picks_ref, *refs):
    lefts, rights, outs = refs[:count], refs[count : -2 - adds], refs[-2:]
    step = pl.program_id(0)

    def write(right_refs):
        total = None
        for left_ref, right_ref in zip(lefts, right_refs):
            left, right = (v[...].reshape(v.shape[-2:]) for v in (left_ref, right_ref))
            here = dot_tn(left, right)
            total = here if total is None else total + here
        for at in range(2):

            @pl.when(step == at)
            def _():
                outs[at][...] = low(total + refs[-3][...].astype(F32) if adds and at == 0 else total)

    if len(rights) == count:
        write(rights)
        return
    for which in range(2):

        @pl.when(picks_ref[0] == which)
        def _():
            write(rights[which * count : (which + 1) * count])


def weight_quarters(picks, lefts, rights, rights_one, arrived, name, token=None):
    count = len(lefts)
    specs, operands = [], []
    for array, shape, place in lefts + rights + (rights_one or []):
        operands.append(array)
        specs.append(pl.BlockSpec(shape, lambda j, chosen, place=place: place(chosen[0], chosen[1 + j])))
    width, rows = rights[0][1][-1], lefts[0][1][-2]
    quarter = (width, width)
    if arrived is not None:
        operands.append(arrived)
        specs.append(whole(quarter))
    return kernel_call(
        functools.partial(weight_body, count, int(arrived is not None)),
        (2,),
        specs,
        [(quarter, BF16, whole(quarter))] * 2,
        [],
        4 * width * width * count * rows,
        8 * width * width + 8 * count * rows * width,
        name,
        None,
        token,
    )(picks, *operands)


def place_body(count, places_ref, *refs):
    out_ref, copy_ref = refs[-2:]
    for at, piece in enumerate(refs[:count]):

        @pl.when(pl.program_id(0) == at)
        def _():
            out_ref[...] = piece[...].astype(F32)

    @pl.when(pl.program_id(0) == 0)
    def _():
        copy_ref[...] = refs[0][...]


def placed(places, first, pieces, shape, columns, into, name, token):
    width = pieces[0].shape[0]

    def index(i, where):
        return (0, where[first + i]) if columns else (where[first + i], 0)

    more = [] if into is None else [into]
    quarter = whole((width, width))
    return kernel_call(
        functools.partial(place_body, len(pieces)),
        (len(pieces),),
        [quarter] * len(pieces) + [ANYWHERE] * len(more),
        [(shape, F32, pl.BlockSpec((width, width), index)), ((width, width), BF16, quarter)],
        [],
        0,
        6 * len(pieces) * width * width,
        name,
        {1 + len(pieces): 0} if more else {},
        token,
    )(places, *pieces, *more)


def pack_body(docs, flag_ref, lengths_ref, *refs):
    sides = {1: refs[: 4 * docs], 0: refs[4 * docs : 8 * docs]}
    rich_refs, out_ref = refs[8 * docs : 9 * docs], refs[9 * docs]
    width = out_ref.shape[1]

    def spread(values, base):
        sums = jnp.sum(values, axis=1, keepdims=True)
        shape = (values.shape[0], width)
        lane = lax.broadcasted_iota(jnp.int32, shape, 1)
        row = lax.broadcasted_iota(jnp.int32, shape, 0)
        return jnp.sum(jnp.where(lane == base + row, sums, 0.0), axis=0, keepdims=True)

    for which, side in sides.items():

        @pl.when(flag_ref[0] == which)
        def _():
            bias, gain, shift, stat = (sum(side[4 * d + i][...] for d in range(docs)) for i in range(4))
            for at in range(0, bias.shape[1], width):
                out_ref[at // width : at // width + 1, :] = bias[:, at : at + width]
            base = bias.shape[1] // width
            out_ref[base : base + 2, :] = gain
            out_ref[base + 2 : base + 4, :] = shift
            scalars = spread(stat, 0 if which else stat.shape[0])
            if not which:
                heads = rich_refs[0].shape[1]
                for term in range(2):
                    total = sum(ref[term] for ref in rich_refs)
                    scalars += spread(total, 2 * stat.shape[0] + term * heads)
                count = lengths_ref[0]
                for d in range(1, docs):
                    count += lengths_ref[d]
                lane = lax.broadcasted_iota(jnp.int32, (1, width), 1)
                scalars += jnp.where(lane == 2 * (stat.shape[0] + heads), count.astype(F32), 0.0)
            out_ref[base + 4 : base + 5, :] = scalars
            out_ref[base + 5 :, :] = jnp.zeros((out_ref.shape[0] - base - 5, width), F32)


def packed_row(flag, lengths, one, two, rich, token=None):
    docs = len(one)
    width = one[0][1].shape[1]
    operands = [v for side in (one, two) for parts in side for v in parts] + list(rich)
    rows = -(-(one[0][0].shape[1] // width + 5) // 8) * 8
    return kernel_call(
        functools.partial(pack_body, docs),
        (1,),
        [pl.BlockSpec(memory_space=pltpu.SMEM)] + [whole(v.shape) for v in operands],
        [((rows, width), F32, whole((rows, width)))],
        [],
        0,
        4 * sum(v.size for v in operands),
        "packed_row",
        None,
        token,
    )(flag, lengths, *operands)


def rows_body(docs, flag_ref, *refs):
    out_ref = refs[2 * docs]
    for doc in range(docs):
        for which in range(2):

            @pl.when((flag_ref[0] == which) & (pl.program_id(0) == doc))
            def _():
                out_ref[...] = refs[(1 - which) * docs + doc][...]


def section_rows(flag, one, two):
    docs = len(one)
    rows, width = one[0].shape
    return kernel_call(
        functools.partial(rows_body, docs),
        (docs,),
        [whole((rows, width))] * (2 * docs),
        [((docs * rows, width), one[0].dtype, pl.BlockSpec((rows, width), lambda i, *_: (i, 0)))],
        [],
        0,
        4 * docs * rows * width,
        "section_rows",
    )(flag, *one, *two)


def sum_body(flag_ref, left_ref, right_ref, out_ref):
    out_ref[...] = left_ref[...] + right_ref[...]


def summed(flag, left, right, token):
    return kernel_call(
        sum_body,
        (1,),
        [whole(left.shape)] * 2,
        [(left.shape, left.dtype, whole(left.shape))],
        [],
        0,
        12 * left.size,
        "small_sum",
        None,
        token,
    )(flag, left, right)


STEPS = (
    "d", "d", "D", "back", "pack", "u", "q", "D", "u", "U", "s", "D",
    "s", "S", "U", "D", "U", "D", "S", "rows", "S", "U", "S", "U",
    "S", "q", "ad", "q", "bu", "q", "ns", "fs", "ou", "os",
)


def passed_along(block, axis, distance):
    devices = range(lax.axis_size(axis))
    route = [(i - distance, i) for i in devices if i - distance in devices]
    return lax.ppermute(block, axis, route)


def after(value, token):
    return lax.optimization_barrier((value, token))[0]


def core_swap(block):
    return lax.ppermute(block, "core", [(0, 1), (1, 0)])


class Ordered:
    def __init__(self):
        self.token = None

    def read(self, *values):
        if self.token is None:
            return values if len(values) > 1 else values[0]
        values = lax.optimization_barrier((*values, self.token))[:-1]
        return values if len(values) > 1 else values[0]

    def gave(self, value):
        self.token = value
        return value


def rounded_sum(*blocks):
    return low(sum(block.astype(F32) for block in blocks))


def chips_sum(order, sent, kept):
    across_x = [(0, 1), (1, 0)]
    neighbours = [(0, 1), (1, 0), (2, 3), (3, 2)]
    partners = [(1, 2), (2, 1), (0, 3), (3, 0)]
    z = lax.axis_index("z")
    middle = (z == 1) | (z == 2)
    half = sent.shape[0] // 2
    arrived = lax.ppermute(sent, "x", across_x)
    yield
    parts = (*kept, order.read(arrived))

    def half_of(start):
        return rounded_sum(*(lax.dynamic_slice_in_dim(part, start, half, 0) for part in parts))

    other = half_of(jnp.where(middle, half, 0))
    arrived = lax.ppermute(other, "z", neighbours)
    mine = order.gave(half_of(jnp.where(middle, 0, half)))
    yield
    mine = order.gave(rounded_sum(mine, order.read(arrived)))
    arrived = lax.ppermute(mine, "z", partners)
    yield
    mine = order.gave(rounded_sum(mine, order.read(arrived)))
    arrived = lax.ppermute(mine, "z", neighbours)
    yield
    other = order.read(arrived)
    total = jnp.concatenate([jnp.where(middle, mine, other), jnp.where(middle, other, mine)], axis=0)
    order.gave(total)
    yield total, core_swap(total), lax.ppermute(total, "x", across_x)


def small_sum(flag, block, totals, axes):
    for axis in axes:
        step = 1
        while step < lax.axis_size(axis):
            route = [(i, i ^ step) for i in range(lax.axis_size(axis))]
            arrived = lax.ppermute(block, axis, route)
            yield
            block, totals["token"] = summed(flag, block, arrived, totals["token"])
            step *= 2
    yield block


def local(
    boundary,
    lengths,
    neighbours,
    counts,
    coords,
    square_weights,
    up_weight,
    down_weight,
    up_bias,
    norm_gain,
    norm_bias,
    rich_terms,
):
    first = lax.axis_index("section") == 0
    core, across_x = lax.axis_index("core"), lax.axis_index("x")
    if lax.axis_size("z") != 4 or lax.axis_size("x") != 2:
        across_x = across_x * 0
    use_one = first.astype(jnp.int32)
    keep = jnp.stack([use_one, 2 * core + 1 - across_x, 2 * core + across_x])
    give = jnp.stack([use_one, 2 * (1 - core) + 1 - across_x, 2 * (1 - core) + across_x])
    places = jnp.stack([keep[2], 2 - 4 * core + keep[2], keep[1], 2 - 4 * core + keep[1]])
    documents = lengths.shape[0]
    docs = range(documents)
    rows = boundary.shape[1] // documents
    width = boundary.shape[2]
    hidden = up_weight.shape[2]
    heads = rich_terms.shape[1]
    source = boundary[0]
    squares = square_weights[0]
    up, down, bias = up_weight[0], down_weight[0], up_bias
    gains, shifts = norm_gain[0], norm_bias[0]
    near_t = neighbours.T
    counts_row, coords_row = counts[None], coords[None]
    about = [jnp.stack([lengths[doc], use_one]) for doc in docs]

    kept_one, arrived, stats_one = [], [], []
    sent = None
    for doc in docs:
        here = source if sent is None else after(source, sent)
        sent, stat, links, left, sigma, pull, resid, normed, active, slope = layer_one_forward(
            about[doc], here, doc, rows, near_t, counts_row, gains, shifts, bias, squares, up, down
        )
        kept_one.append((links, resid, slope, sigma, pull, left, normed, active))
        stats_one.append(stat)
        arrived.append(passed_along(sent, "section", 1))

    back, out_two, rich_two, kept, small_two = [], [], [], [], []
    for doc in docs:
        grad_mid, result, stat, bias_grad, gain_grad, shift_grad, rich, left, right, normed, active, pre = layer_two(
            about[doc], arrived[doc], source, doc, coords_row, rich_terms, gains, shifts, bias, squares, up, down,
            *kept_one[doc][5:]
        )
        out_two.append(result)
        kept.append([left, right, normed, active, pre])
        small_two.append((bias_grad, gain_grad, shift_grad, stat))
        rich_two.append(rich)
        back.append(passed_along(grad_mid, "section", -1))
        last_sent = grad_mid

    out_one, small_one = [], []

    def first_back(doc, grad_mid, token=None):
        links, resid, slope, sigma, pull = kept_one[doc][:5]
        grad_x, bias_grad, gain_grad, shift_grad, pre, right, *token = layer_one_backward(
            about[doc], grad_mid, source, doc, gains, counts_row, links, resid, slope, sigma, pull, squares, up, down,
            kept[doc][4], kept[doc][1], token,
        )
        out_one.append(grad_x)
        kept[doc][4], kept[doc][1] = pre, right
        small_one.append((bias_grad, gain_grad, shift_grad, stats_one[doc]))
        return grad_x, *token

    token = last_sent
    for doc in range(documents - 1):
        (token,) = first_back(doc, after(back[doc], token))
    if documents > 1:
        back[-1] = after(back[-1], token)

    quarter, stack = (rows, width), (1, rows, width)
    still, across = lambda one, q: (0, 0), lambda one, q: (0, q)
    own_rows = [functools.partial(lambda d, one, q: (d, 0), d) for d in docs]

    def left_of(one, q):
        return jnp.where(one == 1, (q + 1) // 2, q // 3), 0, 0

    def right_of(one, q):
        return jnp.where(one == 1, jnp.maximum(q - 1, 0), q), 0, 0

    def pairs_of(name):
        if name == "down":
            return (
                [(kept[d][3], quarter, across) for d in docs],
                [(source, quarter, own_rows[d]) for d in docs],
                [(back[d], quarter, still) for d in docs],
            )
        if name == "up":
            return (
                [(kept[d][2], quarter, still) for d in docs],
                [(kept[d][4], quarter, across) for d in docs],
                None,
            )
        return (
            [(kept[d][0], stack, left_of) for d in docs],
            [(kept[d][1], stack, right_of) for d in docs],
            None,
        )

    order = Ordered()
    custom = lax.axis_size("z") == 4 and lax.axis_size("x") == 2
    names = {"d": "down", "u": "up", "s": "square"}
    totals, given, made, pieces = {"token": jnp.zeros((8, 128), F32)}, {}, {}, {}

    def products(letter):
        name, pairs = names[letter], pairs_of(names[letter])
        *quarters, totals["token"] = weight_quarters(give, *pairs, None, name + "_give", totals["token"])
        given[letter] = [core_swap(v) for v in quarters]
        yield
        *made[letter], totals["token"] = weight_quarters(keep, *pairs, given[letter][0], name + "_keep", totals["token"])
        yield

    def flow(letter):
        sent, kept_own = made[letter]
        kept_other = given[letter][1]
        if custom:
            for value in chips_sum(order, sent, (kept_own, kept_other)):
                pieces[letter] = value
                yield
            return
        near, far = lax.psum(rounded_sum(kept_own, kept_other), ("z", "x")), lax.psum(sent, ("z", "x"))
        pieces[letter] = near, core_swap(near), far
        for _ in range(5):
            yield

    def place(letter, which):
        near, near_other, far = pieces[letter]
        first, blocks = {
            "a": (0, lambda: (near, near_other, far, core_swap(far))),
            "b": (0, lambda: (near, near_other, far)),
            "n": (0, lambda: (near, near_other)),
            "f": (2, lambda: (far,)),
            "o": (3, lambda: (core_swap(far),)),
        }[which]
        shape = (width, hidden) if letter == "u" else (hidden, width)
        blocks = [order.read(block) for block in blocks()]
        totals[letter], copy, totals["token"] = placed(
            places, first, blocks, shape, letter == "u", totals.get(letter), names[letter] + "_placed", totals["token"]
        )
        order.gave(copy)
        if which == "f":
            pieces[letter] = (near, near_other, copy)

    running = {letter: products(letter) for letter in names}
    running.update({letter.upper(): flow(letter) for letter in names})
    for step in STEPS:
        if step == "back":
            _, totals["token"] = first_back(documents - 1, back[-1], totals["token"])
        elif step == "pack":
            small, totals["token"] = packed_row(
                use_one[None], lengths, small_one, small_two, rich_two, totals["token"]
            )
            running["q"] = small_sum(use_one[None], small, totals, ("x", "core", "z"))
            next(running["q"])
        elif step == "rows":
            (boundary_out,) = section_rows(order.read(use_one[None]), out_one, out_two)
            order.gave(boundary_out)
        elif step[0] in "abnfo":
            place(step[1], step[0])
        elif step == "q":
            packed = next(running["q"])
        else:
            next(running[step])
    for packed in running["q"]:
        pass
    crossed = lax.ppermute(packed, "section", [(0, 1), (1, 0)])
    down_total, up_total, square_total = (totals[letter] for letter in names)

    at = hidden // width
    size = 9 + 2 * heads
    shared = packed[at + 4, :size] + crossed[at + 4, :size]
    rms = jnp.sqrt(shared[:8].reshape(2, 4) / (shared[8 + 2 * heads] * width))
    rich_total = shared[8 : 8 + 2 * heads].reshape(2, heads)
    return (
        boundary_out[None],
        square_total.reshape(1, 4, width, width),
        up_total.reshape(1, width, hidden),
        down_total[None],
        packed[:at].reshape(1, hidden),
        packed[at : at + 2][None],
        packed[at + 2 : at + 4][None],
        rich_total,
        rms,
    )


def solution(mesh):
    sections, dp = mesh.devices.shape
    split = Mesh(mesh.devices.reshape(sections, dp // 4, 2, 2), ("section", "z", "x", "core"))
    data = ("z", "x", "core")
    in_specs = (
        P("section", data, None),
        P(data),
        P(data, None),
        P(data),
        P(data),
        P("section", None, None, None),
        P("section", None, None),
        P("section", None, None),
        P("section", None),
        P("section", None, None),
        P("section", None, None),
        P(),
    )
    out_specs = (
        P("section", data, None),
        P("section", None, None, None),
        P("section", None, None),
        P("section", None, None),
        P("section", None),
        P("section", None, None),
        P("section", None, None),
        P(),
        P(),
    )
    return jax.shard_map(local, mesh=split, in_specs=in_specs, out_specs=out_specs, check_vma=False)
```
